512 devices in a mesh: gx: 64 (over z, y), gy: 8 (over x, core).
Axes of the slice: x: 4, y: 4, z: 16, core: 2. Of those that a mesh axis runs over, the one named last changes fastest.
Arguments:
- velocity: float32 [3, 256, 64, 256], P(None, 'gx', 'gy'), may hold values from -6 to 6
- cotangent: float32 [3, 256, 64, 256], P(None, 'gx', 'gy'), may hold values from -10.5 to 13.5
- weight_in: float32 [6, 64], replicated, may hold values from -2.5 to 2.5
- bias_in: float32 [64], replicated, may hold values from -3 to 3
- weight_out: float32 [64, 3], replicated, may hold values from -0.75 to 0.75
Outputs:
- new_velocity: float32 [3, 256, 64, 256], P(None, 'gx', 'gy')
- grad_velocity: float32 [3, 256, 64, 256], P(None, 'gx', 'gy')
- grad_weight_in: float32 [6, 64], replicated
- grad_bias_in: float32 [64], replicated
- grad_weight_out: float32 [64, 3], replicated
The draws below stay inside these ranges and needn't reach their ends.
All inputs are finite; a program needn't handle non-finite values.
Results may differ from the reference program's by a relative error of at most 0.0003.
Values sent between devices are 32-bit elements; how exact they have to be, the bound alone decides.
A program may use at most 64 MiB of HBM per device.

```python
import jax
import jax.numpy as jnp
from jax import lax

UNITS = 64
X_CELLS = 256
Y_CELLS = 64
Z_CELLS = 256
ALL_CELLS = 4194304


def draw_cotangent(key, part):
    shape = (3, X_CELLS, Y_CELLS, Z_CELLS)
    base = jnp.clip(jax.random.normal(key, shape, jnp.float32), -4.0, 4.0)
    position = lax_ramp(shape)
    return ((0.5 + base) * position).astype(jnp.float32)


def lax_ramp(shape):
    across = jnp.arange(shape[1], dtype=jnp.float32) / float(max(shape[1] - 1, 1))
    return (1.0 + 2.0 * across)[None, :, None, None]


def level_of(own_key, shape, split, smallest, high):
    level, own = 1.0, jax.random.fold_in(own_key, 6)
    for axis_at, shards_of in split:
        draws = jnp.exp(jax.random.uniform(jax.random.fold_in(own, axis_at), (shards_of,), jnp.float32, smallest / len(split), high / len(split)))
        level = level * jnp.repeat(draws, shape[axis_at] // shards_of).reshape([-1 if axis == axis_at else 1 for axis in range(len(shape))])
    return level


def gaussian(stream_key, shape, width, bound, split=(), kind=jnp.bfloat16):
    values = width * jax.random.normal(stream_key, shape, jnp.float32)
    if split:
        values = values * level_of(stream_key, shape, split, -0.22, 0.18)
    return jnp.clip(values, -bound, bound).astype(kind)


def setup_inputs(seed: int = 0) -> dict:
    arg_keys = jax.random.split(jax.random.key(seed), 6)
    return {
        "velocity": gaussian(arg_keys[0], (3, X_CELLS, Y_CELLS, Z_CELLS), 1.0, 6.0, ((1, 64), (2, 8)), jnp.float32),
        "cotangent": draw_cotangent(jax.random.fold_in(arg_keys[5], 71), 0),
        "weight_in": gaussian(arg_keys[2], (6, UNITS), 6 ** -0.5, 2.5, (), jnp.float32),
        "bias_in": gaussian(arg_keys[3], (UNITS,), 0.5, 3.0, (), jnp.float32),
        "weight_out": gaussian(arg_keys[4], (UNITS, 3), UNITS ** -0.5, 0.75, (), jnp.float32),
    }


FILTER_ALPHA = 0.499
FILTER_GAIN = 0.5 + FILTER_ALPHA
COMPACT_ALPHA = 1.0 / 3.0
STEP_SIZE = 0.5
PRECISE = lax.Precision.HIGHEST

def shifted(values, axis, offset):
    length = values.shape[axis]
    padding = [(0, 0)] * values.ndim
    padding[axis] = (2, 2)
    padded = jnp.pad(values, padding)
    return lax.slice_in_dim(padded, 2 + offset, 2 + offset + length, axis=axis)

def solve_along(right_side, axis, coupling):
    moved = jnp.moveaxis(right_side, axis, 0)
    shape = moved.shape
    flat = moved.reshape(shape[0], -1)
    length = shape[0]
    diagonal = jnp.ones((length,), flat.dtype)
    beside = jnp.full((length,), coupling, flat.dtype)
    below = beside.at[0].set(0.0)
    above = beside.at[length - 1].set(0.0)
    solved = lax.linalg.tridiagonal_solve(below, diagonal, above, flat)
    return jnp.moveaxis(solved.reshape(shape), 0, axis)

def stencil(values, axis):
    return 7.0 / 9.0 * (shifted(values, axis, 1) - shifted(values, axis, -1)) + 1.0 / 36.0 * (shifted(values, axis, 2) - shifted(values, axis, -2))

def derive(values, axis):
    return solve_along(stencil(values, axis), axis, COMPACT_ALPHA)

def derive_adjoint(values, axis):
    return -stencil(solve_along(values, axis, COMPACT_ALPHA), axis)

def smooth(values):
    right_side = FILTER_GAIN * values + 0.5 * FILTER_GAIN * (shifted(values, 1, 1) + shifted(values, 1, -1))
    return solve_along(right_side, 1, FILTER_ALPHA)

def closure_plane(feature_plane, cotangent_plane, weight_in, bias_in, weight_out):
    pre = jnp.dot(weight_in.T, feature_plane, precision=PRECISE) + bias_in[:, None]
    hidden = jnp.tanh(pre)
    forcing = jnp.dot(weight_out.T, hidden, precision=PRECISE)
    grad_out = STEP_SIZE * cotangent_plane
    grad_hidden = jnp.dot(weight_out, grad_out, precision=PRECISE)
    grad_pre = grad_hidden * (1.0 - hidden * hidden)
    grad_feature = jnp.dot(weight_in, grad_pre, precision=PRECISE)
    sum_in = jnp.dot(feature_plane, grad_pre.T, precision=PRECISE)
    sum_bias = jnp.sum(grad_pre, axis=1)
    sum_out = jnp.dot(hidden, grad_out.T, precision=PRECISE)
    return (forcing, grad_feature, sum_in, sum_bias, sum_out)

def reference(velocity, cotangent, weight_in, bias_in, weight_out):
    smoothed = smooth(velocity)
    features = jnp.concatenate([derive(smoothed, 2), derive(smoothed, 3)], axis=0)
    plane_cells = Y_CELLS * Z_CELLS
    feature_planes = jnp.moveaxis(features, 1, 0).reshape(X_CELLS, 6, plane_cells)
    cotangent_planes = jnp.moveaxis(cotangent, 1, 0).reshape(X_CELLS, 3, plane_cells)

    def one_plane(pair):
        return closure_plane(pair[0], pair[1], weight_in, bias_in, weight_out)
    forcing, grad_feature, sum_in, sum_bias, sum_out = lax.map(one_plane, (feature_planes, cotangent_planes))
    forcing = jnp.moveaxis(forcing.reshape(X_CELLS, 3, Y_CELLS, Z_CELLS), 0, 1)
    grad_feature = jnp.moveaxis(grad_feature.reshape(X_CELLS, 6, Y_CELLS, Z_CELLS), 0, 1)
    new_velocity = velocity + STEP_SIZE * forcing
    back = derive_adjoint(grad_feature[0:3], 2) + derive_adjoint(grad_feature[3:6], 3)
    grad_velocity = cotangent + smooth(back)
    cells = float(ALL_CELLS)
    return (new_velocity, grad_velocity, jnp.sum(sum_in, axis=0) / cells, jnp.sum(sum_bias, axis=0) / cells, jnp.sum(sum_out, axis=0) / cells)
```

```python
import functools

import jax
import jax.numpy as jnp
import ml_dtypes
import numpy as np
from jax import lax
from jax.experimental import pallas as pl
from jax.experimental.pallas import tpu as pltpu
from jax.sharding import PartitionSpec as P

FILTER_ALPHA = 0.499
FILTER_GAIN = 0.5 + FILTER_ALPHA
COMPACT_ALPHA = 1.0 / 3.0
STEP_SIZE = 0.5
MESH = pl.DeviceIdType.MESH
F32 = jnp.float32
BF16 = jnp.bfloat16

GROUP = 4
RING = 16
LINE = 8
ROWS = 4
UNITS = 64

UP_W, DOWN_W, UP_C, DOWN_C, RING_L, RING_R, BACK_L, BACK_R, LOCAL, LEFT, RIGHT = (
    0, 4, 8, 12, 16, 32, 48, 68, 88, 104, 108
)


def tridiagonal(length, coupling):
    return np.eye(length) + coupling * (np.eye(length, k=1) + np.eye(length, k=-1))


def smoothing_table():
    devices = GROUP * RING
    length = devices * ROWS
    matrix = tridiagonal(length, FILTER_ALPHA)
    inverse = np.linalg.inv(matrix)
    smoothing = np.linalg.solve(matrix, FILTER_GAIN * tridiagonal(length, 0.5))

    def move(row, pivot):
        return inverse[row, pivot] / inverse[pivot, pivot]

    table = np.zeros((devices, 128))
    block = GROUP * ROWS
    for device in range(devices):
        ring, member = divmod(device, GROUP)
        first = device * ROWS
        last = first + ROWS - 1
        entry = table[device]
        if device < devices - 1:
            entry[UP_W:UP_W + ROWS] = smoothing[last + 1, first:first + ROWS]
        if device > 0:
            entry[DOWN_W:DOWN_W + ROWS] = smoothing[first - 1, first:first + ROWS]
        group_first = ring * block
        group_last = group_first + block - 1
        for other in range(GROUP):
            start = group_first + other * ROWS
            if ring < RING - 1:
                entry[UP_C + other] = move(group_last + 1, start + ROWS)
            if ring > 0:
                entry[DOWN_C + other] = move(group_first - 1, start - 1)
        for other in range(RING):
            if other < ring:
                entry[RING_L + other] = move(group_first, (other + 1) * block)
            if other > ring:
                entry[RING_R + other] = move(group_last, other * block - 1)
        for target in range(GROUP):
            own_first = group_first + target * ROWS
            own_last = own_first + ROWS - 1
            entry[BACK_L + 5 * target] = move(own_first, group_first)
            entry[BACK_R + 5 * target] = move(own_last, group_last)
            for other in range(GROUP):
                start = group_first + other * ROWS
                if other < target:
                    entry[BACK_L + 5 * target + 1 + other] = move(own_first, start + ROWS)
                if other > target:
                    entry[BACK_R + 5 * target + 1 + other] = move(own_last, start - 1)
        entry[LOCAL:LOCAL + ROWS * ROWS] = smoothing[first:last + 1, first:last + 1].reshape(-1)
        for row in range(ROWS):
            entry[LEFT + row] = move(first + row, first)
            entry[RIGHT + row] = move(first + row, last)
    return table.astype(np.float32)


def derivative_matrix(length):
    right = 7.0 / 9.0 * (np.eye(length, k=1) - np.eye(length, k=-1)) + 1.0 / 36.0 * (
        np.eye(length, k=2) - np.eye(length, k=-2)
    )
    return np.linalg.solve(tridiagonal(length, COMPACT_ALPHA), right)


def line_table():
    size = 8
    length = LINE * size
    forward = derivative_matrix(length)
    table = np.zeros((LINE, size, 128))
    for place, matrix in enumerate((forward, forward.T)):
        base = 24 * place
        for device in range(LINE):
            rows = slice(device * size, device * size + size)
            table[device, :, base:base + 8] = matrix[rows, rows]
            if device < LINE - 1:
                table[device, 0, base + 8:base + 16] = matrix[device * size + 8, rows]
                table[device, 1, base + 8:base + 16] = matrix[device * size + 9, rows]
            if device > 0:
                table[device, 2, base + 8:base + 16] = matrix[device * size - 1, rows]
                table[device, 3, base + 8:base + 16] = matrix[device * size - 2, rows]
            for source in range(LINE):
                if source == device:
                    continue
                columns = slice(source * size, source * size + size)
                pivot = source * size + 9 if source < device else source * size - 2
                sent = matrix[pivot, columns]
                factors = matrix[rows, columns] @ sent / (sent @ sent)
                if source == device - 1:
                    factors[0] = 0.0
                if source == device + 1:
                    factors[size - 1] = 0.0
                table[device, :, base + 16 + source] = factors
    table[1:, 0, 48] = 1.0
    table[:-1, size - 1, 49] = 1.0
    return table.astype(np.float32)


def split_table(matrix):
    high = matrix.astype(np.float32).astype(ml_dtypes.bfloat16)
    low = (matrix - high.astype(np.float64)).astype(np.float32).astype(ml_dtypes.bfloat16)
    return [high, low]


def depth_table(length):
    matrix = derivative_matrix(length)
    return np.stack(split_table(matrix.T.copy()) + split_table(matrix))


def split(values):
    high = values.astype(BF16)
    return high, (values - high.astype(F32)).astype(BF16)


def iota(shape, dim):
    return lax.broadcasted_iota(jnp.int32, shape, dim)


def ones_where(condition):
    return jnp.where(condition, 1.0, 0.0).astype(F32)


def matmul(a, b):
    return jnp.dot(a, b, preferred_element_type=F32)


def matmul_nt(a, b, precision=None):
    return lax.dot_general(a, b, (((1,), (1,)), ((), ())), precision=precision, preferred_element_type=F32)


def kernel(
    velocity, cotangent, weight_in, bias_in, weight_out, x_table, y_table, z_table,
    new_velocity, grad_velocity, grad_in, grad_bias, grad_out_t,
    vel, cot, smoothed, feats, gfeats, pulled, nvel, gvel, scalars, columns, tall, ztab,
    left_lhs, back_lhs, force_lhs, rhs, pre_buf, sums,
    x1_send, x1_recv, x2_send, x2_recv, x3_send, x3_recv, y_send, y_recv, y_edge,
    p1, p2, p3,
    local_sem, x1_ss, x1_rs, x2_ss, x2_rs, x3_ss, x3_rs, y_ss, y_rs, ye_ss, ye_rs,
    p1_ss, p1_rs, p2_ss, p2_rs, p3_ss, p3_rs,
):
    gx = lax.axis_index("gx")
    gy = lax.axis_index("gy")
    ring = lax.div(gx, GROUP)
    member = lax.rem(gx, GROUP)

    def in_group(step):
        return lax.rem(member + step, GROUP)

    def in_ring(step):
        return lax.rem(ring + step, RING)

    def in_line(step):
        return lax.rem(gy + step, LINE)

    def group_device(other):
        return (ring * GROUP + other, gy)

    def ring_device(other):
        return (other * GROUP + member, gy)

    def line_device(other):
        return (gx, other)

    barrier = pltpu.get_barrier_semaphore()
    partners = (
        [ring_device(in_ring(step)) for step in range(1, RING)]
        + [group_device(in_group(step)) for step in range(1, GROUP)]
        + [line_device(in_line(step)) for step in range(1, LINE)]
    )
    for partner in partners:
        pl.semaphore_signal(barrier, inc=1, device_id=partner, device_id_type=MESH)

    loads = [
        pltpu.make_async_copy(velocity, vel, local_sem.at[0]),
        pltpu.make_async_copy(x_table.at[gx], scalars, local_sem.at[1]),
        pltpu.make_async_copy(y_table.at[gy], columns, local_sem.at[2]),
        pltpu.make_async_copy(cotangent, cot, local_sem.at[3]),
        pltpu.make_async_copy(z_table, ztab, local_sem.at[4]),
    ]
    for load in loads:
        load.start()

    def remote(src, dst, send_sem, recv_sem, device):
        return pltpu.make_async_remote_copy(
            src_ref=src, dst_ref=dst, send_sem=send_sem, recv_sem=recv_sem, device_id=device, device_id_type=MESH
        )

    sent = []

    def send(*args):
        copy = remote(*args)
        copy.start()
        sent.append(copy)

    def scalar(index):
        return scalars[0, index]

    def build_weights():
        w_high, w_low = split(weight_in[...])
        spread = ones_where(lax.shift_right_logical(iota((512, UNITS), 0), 3) == iota((512, UNITS), 1)).astype(BF16)
        spread_t = ones_where(iota((UNITS, 512), 0) == lax.shift_right_logical(iota((UNITS, 512), 1), 3)).astype(BF16)
        bias = bias_in[...]
        b_high, b_low = split(bias)
        b_rest = bias - b_high.astype(F32) - b_low.astype(F32)
        row = iota((8, 256), 0)
        col = iota((8, 256), 1)
        field = lax.shift_right_logical(col, 3)
        pick_high = ones_where(((field == row) | (field == row + 6)) & (row < 6)).astype(BF16)
        pick_low = ones_where((field == row + 12) & (row < 6)).astype(BF16)
        spread_high = matmul_nt(spread, w_high).astype(BF16)
        spread_low = matmul_nt(spread, w_low).astype(BF16)
        top = matmul(spread_high, pick_high[0:6]) + matmul(spread_low, pick_low[0:6])
        same = lax.bitwise_and(iota((512, 256), 0), 7) == lax.bitwise_and(iota((512, 256), 1), 7)
        top = jnp.where(same, top, 0.0)
        biases = jnp.concatenate([b_high.astype(F32), b_low.astype(F32), b_rest, jnp.zeros((5, UNITS), F32)], axis=0)
        spread_bias = matmul_nt(spread, biases.astype(BF16)).astype(BF16)
        top = top + matmul(spread_bias, ones_where(col == row + 240).astype(BF16))
        left_lhs[0:512, :] = top.astype(BF16)
        o_high, o_low = split(weight_out[...])
        pick_high = ones_where(((field == row + 18) | (field == row + 22)) & (row < 3)).astype(BF16)
        pick_low = ones_where((field == row + 26) & (row < 3)).astype(BF16)
        spread_oh = matmul(spread, o_high).astype(BF16)
        spread_ol = matmul(spread, o_low).astype(BF16)
        bottom = matmul(spread_oh, pick_high[0:3]) + matmul(spread_ol, pick_low[0:3])
        left_lhs[512:1024, :] = jnp.where(same, bottom, 0.0).astype(BF16)

        same_t = lax.bitwise_and(iota((96, 512), 0), 7) == lax.bitwise_and(iota((96, 512), 1), 7)
        row = lax.shift_right_logical(iota((96, 8), 0), 3)
        col = iota((96, 8), 1)
        get_high = ones_where((row == col) & (col < 6)).astype(BF16)
        get_low = ones_where((row == col + 6) & (col < 6)).astype(BF16)
        tall_w = matmul(get_high[:, 0:6], w_high) + matmul(get_low[:, 0:6], w_low)
        back_lhs[...] = jnp.where(same_t, matmul(tall_w.astype(BF16), spread_t), 0.0).astype(BF16)
        get_high = ones_where((row[0:64] == col[0:64]) & (col[0:64] < 3)).astype(BF16)
        get_low = ones_where((row[0:64] == col[0:64] + 4) & (col[0:64] < 3)).astype(BF16)
        tall_o = matmul_nt(get_high[:, 0:3], o_high) + matmul_nt(get_low[:, 0:3], o_low)
        force_lhs[...] = jnp.where(same_t[0:64], matmul(tall_o.astype(BF16), spread_t), 0.0).astype(BF16)

    build_weights()
    loads[0].wait()
    loads[1].wait()
    loads[2].wait()
    line_columns = columns[...]
    for index in range(50):
        tall[index] = jnp.broadcast_to(line_columns[:, index:index + 1], (8, 128))

    def tall_column(index):
        half = tall[index]
        return jnp.concatenate([half, half], axis=1)

    def smooth(src, order, after_barrier, meanwhile, emit):
        for comp in range(3):
            rows = [src[comp, row] for row in range(ROWS)]
            for kind, base in ((0, UP_W), (1, DOWN_W)):
                state = sum(scalar(base + row) * rows[row] for row in range(ROWS))
                for piece in range(GROUP):
                    x1_send[order, piece, kind, comp] = state[2 * piece:2 * piece + 2]
        after_barrier()
        for step in (2, 1, 3):
            other = in_group(step)
            send(
                x1_send.at[order, other], x1_recv.at[order, member],
                x1_ss.at[order, other], x1_rs.at[order, member], group_device(other),
            )
        x1_recv[order, member] = x1_send[order, member]
        meanwhile()
        for step in range(1, GROUP):
            other = in_group(step)
            remote(
                x1_send.at[order, other], x1_recv.at[order, other],
                x1_ss.at[order, other], x1_rs.at[order, other], group_device(other),
            ).wait_recv()
        ups = [x1_recv[order, other, 0] for other in range(GROUP)]
        downs = [x1_recv[order, other, 1] for other in range(GROUP)]
        x2_send[order, 0] = sum(scalar(UP_C + other) * ups[other] for other in range(GROUP))
        x2_send[order, 1] = sum(scalar(DOWN_C + other) * downs[other] for other in range(GROUP))
        for step in (8, 7, 9, 6, 10, 5, 11, 4, 12, 3, 13, 2, 14, 1, 15):
            other = in_ring(step)
            kind = jnp.where(other > ring, 0, 1)
            send(
                x2_send.at[order, kind], x2_recv.at[order, ring],
                x2_ss.at[order, other], x2_rs.at[order, ring], ring_device(other),
            )
        left = jnp.zeros((3, 2, 256), F32)
        right = jnp.zeros((3, 2, 256), F32)
        for step in (1, 15, 2, 14, 3, 13, 4, 12, 5, 11, 6, 10, 7, 9, 8):
            other = in_ring(step)
            remote(
                x2_send.at[order, 0], x2_recv.at[order, other],
                x2_ss.at[order, other], x2_rs.at[order, other], ring_device(other),
            ).wait_recv()
            part = x2_recv[order, other]
            left = left + scalar(RING_L + other) * part
            right = right + scalar(RING_R + other) * part
        for step in (2, 1, 3, 0):
            other = in_group(step)
            target_left = scalar(BACK_L + 5 * other) * left
            target_right = scalar(BACK_R + 5 * other) * right
            for source in range(GROUP):
                target_left = target_left + scalar(BACK_L + 5 * other + 1 + source) * ups[source]
                target_right = target_right + scalar(BACK_R + 5 * other + 1 + source) * downs[source]
            if step == 0:
                x3_recv[order, member, 0] = target_left
                x3_recv[order, member, 1] = target_right
            else:
                x3_send[order, other, 0] = target_left
                x3_send[order, other, 1] = target_right
                send(
                    x3_send.at[order, other], x3_recv.at[order, member],
                    x3_ss.at[order, other], x3_rs.at[order, member], group_device(other),
                )
        for step in range(1, GROUP):
            other = in_group(step)
            remote(
                x3_send.at[order, other], x3_recv.at[order, other],
                x3_ss.at[order, other], x3_rs.at[order, other], group_device(other),
            ).wait_recv()
        for comp in range(3):
            rows = [src[comp, row] for row in range(ROWS)]
            from_left = jnp.concatenate([x3_recv[order, piece, 0, comp] for piece in range(GROUP)], axis=0)
            from_right = jnp.concatenate([x3_recv[order, piece, 1, comp] for piece in range(GROUP)], axis=0)
            for row in range(ROWS):
                total = scalar(LEFT + row) * from_left + scalar(RIGHT + row) * from_right
                for col in range(ROWS):
                    total = total + scalar(LOCAL + ROWS * row + col) * rows[col]
                emit(comp, row, total)

    def line_send(load, order):
        base = 24 * order
        sent_columns = [tall_column(base + 8 + col) for col in range(8)]
        for comp in range(3):
            for row in range(ROWS):
                tile = load(comp, row)
                out = sum(sent_columns[col] * tile[col:col + 1] for col in range(8))
                for kind in range(4):
                    y_send[order, kind, comp, row:row + 1, :] = out[kind:kind + 1]
        for kind, step in ((0, 1), (1, LINE - 1)):
            send(
                y_send.at[order, 2 * kind], y_edge.at[order, kind],
                ye_ss.at[order, kind], ye_rs.at[order, kind], line_device(in_line(step)),
            )
        for step in (4, 5, 3, 2, 6, 1, 7):
            other = in_line(step)
            kind = jnp.where(other > gy, 1, 3)
            send(
                y_send.at[order, kind], y_recv.at[order, gy],
                y_ss.at[order, other], y_rs.at[order, gy], line_device(other),
            )

    def line_local(load, order, store):
        base = 24 * order
        local_columns = [tall_column(base + col) for col in range(8)]
        for comp in range(3):
            for row in range(ROWS):
                tile = load(comp, row)
                store(comp, row, sum(local_columns[col] * tile[col:col + 1] for col in range(8)))

    def line_receive(order, load, store):
        base = 24 * order
        for kind, step in ((0, LINE - 1), (1, 1)):
            remote(
                y_send.at[order, 0], y_edge.at[order, kind],
                ye_ss.at[order, kind], ye_rs.at[order, kind], line_device(in_line(step)),
            ).wait_recv()
        for step in range(1, LINE):
            other = in_line(step)
            remote(
                y_send.at[order, 1], y_recv.at[order, other],
                y_ss.at[order, other], y_rs.at[order, other], line_device(other),
            ).wait_recv()
        y_recv[order, gy] = jnp.zeros((3, ROWS, 256), F32)
        factors = [tall_column(base + 16 + source) for source in range(LINE)]
        first = tall_column(48)
        last = tall_column(49)
        for comp in range(3):
            for row in range(ROWS):
                total = load(comp, row)
                total = total + first * y_edge[order, 0, comp, row:row + 1, :]
                total = total + last * y_edge[order, 1, comp, row:row + 1, :]
                for source in range(LINE):
                    total = total + factors[source] * y_recv[order, source, comp, row:row + 1, :]
                store(comp, row, total)

    def depth_apply(values, order):
        high, low = split(values)
        both = matmul(jnp.concatenate([high, low], axis=0), ztab[2 * order])
        count = values.shape[0]
        return both[0:count] + both[count:2 * count] + matmul(high, ztab[2 * order + 1])

    def wait_barrier():
        pl.semaphore_wait(barrier, len(partners))

    def nothing():
        pass

    def keep_smoothed(comp, row, value):
        smoothed[comp, row] = value

    def load_waits():
        loads[3].wait()
        loads[4].wait()

    smooth(vel, 0, wait_barrier, load_waits, keep_smoothed)

    line_send(lambda comp, row: smoothed[comp, row], 0)
    along_z = depth_apply(smoothed[...].reshape(96, 256), 0)
    for comp in range(3):
        for row in range(ROWS):
            start = (comp * ROWS + row) * 8
            feats[row, 24 + 8 * comp:32 + 8 * comp, :] = along_z[start:start + 8]

    def store_feature(comp, row, value):
        feats[row, 8 * comp:8 * comp + 8, :] = value

    line_local(lambda comp, row: smoothed[comp, row], 0, store_feature)
    line_receive(0, lambda comp, row: feats[row, 8 * comp:8 * comp + 8, :], store_feature)

    def outward(row):
        parts = [STEP_SIZE * cot[comp, row] for comp in range(3)]
        return jnp.concatenate(parts + [jnp.zeros((8, 256), F32)], axis=0)

    def closure(row, carry):
        feature_high, feature_low = split(feats[row])
        rhs[0:48, :] = feature_high
        rhs[48:96, :] = feature_low
        rhs[96:144, :] = feature_high
        out_high, out_low = split(outward(row))
        rhs[144:176, :] = out_high
        rhs[176:208, :] = out_low
        rhs[208:240, :] = out_high
        rhs[240:256, :] = jnp.ones((16, 256), BF16)
        hidden = jnp.tanh(matmul(left_lhs[0:512, :], rhs[...]))
        grad_pre = matmul(left_lhs[512:1024, :], rhs[...]) * (1.0 - hidden * hidden)
        pre_buf[row, 0] = hidden
        pre_buf[row, 1] = grad_pre
        pre_high, pre_low = split(grad_pre)
        both = matmul(back_lhs[...], pre_high)
        gfeats[row] = both[0:48] + both[48:96] + matmul(back_lhs[0:48, :], pre_low)
        return carry

    lax.fori_loop(0, ROWS, closure, 0)

    line_send(lambda comp, row: gfeats[row, 8 * comp:8 * comp + 8, :], 1)
    back_in = jnp.concatenate(
        [gfeats[row, 24 + 8 * comp:32 + 8 * comp, :] for comp in range(3) for row in range(ROWS)], axis=0
    )
    along_z = depth_apply(back_in, 1)

    def add_depth(comp, row, value):
        start = (comp * ROWS + row) * 8
        pulled[comp, row] = value + along_z[start:start + 8]

    line_local(lambda comp, row: gfeats[row, 8 * comp:8 * comp + 8, :], 1, add_depth)

    def forces_and_sums(row, carry):
        hidden = pre_buf[row, 0]
        hidden_high, hidden_low = split(hidden)
        both = matmul(force_lhs[...], hidden_high)
        forcing = both[0:32] + both[32:64] + matmul(force_lhs[0:32, :], hidden_low)
        for comp in range(3):
            nvel[comp, row] = vel[comp, row] + STEP_SIZE * forcing[8 * comp:8 * comp + 8]
        with_ones = jnp.concatenate([feats[row], jnp.ones((8, 256), F32)], axis=0)
        sums[0:56, :] += matmul_nt(with_ones, pre_buf[row, 1], lax.Precision.HIGHEST)
        sums[56:88, :] += matmul_nt(outward(row), hidden, lax.Precision.HIGHEST)
        return carry

    def partial_sums():
        sums[...] = jnp.zeros((88, 512), F32)
        lax.fori_loop(0, ROWS, forces_and_sums, 0)
        same = lax.bitwise_and(iota((88, 512), 0), 7) == lax.bitwise_and(iota((88, 512), 1), 7)
        gather = ones_where(lax.shift_right_logical(iota((512, UNITS), 0), 3) == iota((512, UNITS), 1))
        fold = ones_where(iota((16, 88), 0) == lax.shift_right_logical(iota((16, 88), 1), 3))
        narrow = jnp.dot(
            jnp.where(same, sums[...], 0.0), gather, precision=lax.Precision.HIGHEST, preferred_element_type=F32
        )
        p1[gy] = jnp.dot(fold, narrow, precision=lax.Precision.HIGHEST, preferred_element_type=F32)
        for step in range(1, LINE):
            other = in_line(step)
            send(p1.at[gy], p1.at[gy], p1_ss.at[other], p1_rs.at[gy], line_device(other))

    line_receive(1, lambda comp, row: pulled[comp, row], lambda comp, row, value: pulled.__setitem__((comp, row), value))

    def keep_gradient(comp, row, value):
        gvel[comp, row] = cot[comp, row] + value

    smooth(pulled, 1, nothing, partial_sums, keep_gradient)

    stores = [
        pltpu.make_async_copy(nvel, new_velocity, local_sem.at[0]),
        pltpu.make_async_copy(gvel, grad_velocity, local_sem.at[1]),
    ]
    for store in stores:
        store.start()

    for step in range(1, LINE):
        other = in_line(step)
        remote(p1.at[other], p1.at[other], p1_ss.at[other], p1_rs.at[other], line_device(other)).wait_recv()
    total = p1[0]
    for other in range(1, LINE):
        total = total + p1[other]
    p2[member] = total
    for step in range(1, GROUP):
        other = in_group(step)
        send(p2.at[member], p2.at[member], p2_ss.at[other], p2_rs.at[member], group_device(other))
    for step in range(1, GROUP):
        other = in_group(step)
        remote(p2.at[other], p2.at[other], p2_ss.at[other], p2_rs.at[other], group_device(other)).wait_recv()
    total = p2[0]
    for other in range(1, GROUP):
        total = total + p2[other]
    p3[ring] = total
    for step in range(1, RING):
        other = in_ring(step)
        send(p3.at[ring], p3.at[ring], p3_ss.at[other], p3_rs.at[ring], ring_device(other))
    for step in range(1, RING):
        other = in_ring(step)
        remote(p3.at[other], p3.at[other], p3_ss.at[other], p3_rs.at[other], ring_device(other)).wait_recv()
    total = p3[0]
    for other in range(1, RING):
        total = total + p3[other]
    total = total * (1.0 / float(256 * 64 * 256))
    grad_in[...] = total[0:6]
    grad_bias[...] = total[6:7]
    grad_out_t[...] = total[7:10]

    for copy in sent:
        copy.wait_send()
    for store in stores:
        store.wait()


def local(velocity, cotangent, weight_in, bias_in, weight_out):
    field = velocity.shape
    dma = pltpu.SemaphoreType.DMA
    anywhere = pl.BlockSpec(memory_space=pl.ANY)
    whole = pl.BlockSpec(memory_space=pltpu.VMEM)
    outs = pl.pallas_call(
        kernel,
        out_shape=(
            jax.ShapeDtypeStruct(field, F32),
            jax.ShapeDtypeStruct(field, F32),
            jax.ShapeDtypeStruct((6, UNITS), F32),
            jax.ShapeDtypeStruct((1, UNITS), F32),
            jax.ShapeDtypeStruct((3, UNITS), F32),
        ),
        in_specs=[anywhere, anywhere, whole, whole, whole, anywhere, anywhere, anywhere],
        out_specs=(anywhere, anywhere, whole, whole, whole),
        scratch_shapes=[
            pltpu.VMEM(field, F32),
            pltpu.VMEM(field, F32),
            pltpu.VMEM(field, F32),
            pltpu.VMEM((ROWS, 48, 256), F32),
            pltpu.VMEM((ROWS, 48, 256), F32),
            pltpu.VMEM(field, F32),
            pltpu.VMEM(field, F32),
            pltpu.VMEM(field, F32),
            pltpu.SMEM((1, 128), F32),
            pltpu.VMEM((8, 128), F32),
            pltpu.VMEM((50, 8, 128), F32),
            pltpu.VMEM((4, 256, 256), BF16),
            pltpu.VMEM((1024, 256), BF16),
            pltpu.VMEM((96, 512), BF16),
            pltpu.VMEM((64, 512), BF16),
            pltpu.VMEM((256, 256), BF16),
            pltpu.VMEM((ROWS, 2, 512, 256), F32),
            pltpu.VMEM((88, 512), F32),
            pltpu.VMEM((2, GROUP, 2, 3, 2, 256), F32),
            pltpu.VMEM((2, GROUP, 2, 3, 2, 256), F32),
            pltpu.VMEM((2, 2, 3, 2, 256), F32),
            pltpu.VMEM((2, RING, 3, 2, 256), F32),
            pltpu.VMEM((2, GROUP, 2, 3, 2, 256), F32),
            pltpu.VMEM((2, GROUP, 2, 3, 2, 256), F32),
            pltpu.VMEM((2, 4, 3, ROWS, 256), F32),
            pltpu.VMEM((2, LINE, 3, ROWS, 256), F32),
            pltpu.VMEM((2, 2, 3, ROWS, 256), F32),
            pltpu.VMEM((LINE, 16, UNITS), F32),
            pltpu.VMEM((GROUP, 16, UNITS), F32),
            pltpu.VMEM((RING, 16, UNITS), F32),
            dma((5,)),
            dma((2, GROUP)), dma((2, GROUP)),
            dma((2, RING)), dma((2, RING)),
            dma((2, GROUP)), dma((2, GROUP)),
            dma((2, LINE)), dma((2, LINE)),
            dma((2, 2)), dma((2, 2)),
            dma((LINE,)), dma((LINE,)),
            dma((GROUP,)), dma((GROUP,)),
            dma((RING,)), dma((RING,)),
        ],
        compiler_params=pltpu.CompilerParams(collective_id=0, has_side_effects=True),
        name="closure_step",
    )(
        velocity, cotangent, weight_in, bias_in.reshape(1, UNITS), weight_out,
        jnp.asarray(smoothing_table()).reshape(GROUP * RING, 1, 128), jnp.asarray(line_table()),
        jnp.asarray(depth_table(field[3])),
    )
    return outs[0], outs[1], outs[2], outs[3].reshape(UNITS), outs[4].T


def solution(mesh):
    in_specs = (P(None, "gx", "gy", None), P(None, "gx", "gy", None), P(), P(), P())
    out_specs = (P(None, "gx", "gy", None), P(None, "gx", "gy", None), P(), P(), P())
    return jax.shard_map(local, mesh=mesh, in_specs=in_specs, out_specs=out_specs, check_vma=False)
```

```python
import functools

import jax
import jax.numpy as jnp
import ml_dtypes
import numpy as np
from jax import lax
from jax.experimental import pallas as pl
from jax.experimental.pallas import tpu as pltpu
from jax.sharding import PartitionSpec as P

FILTER_ALPHA = 0.499
FILTER_GAIN = 0.5 + FILTER_ALPHA
COMPACT_ALPHA = 1.0 / 3.0
STEP_SIZE = 0.5
MESH = pl.DeviceIdType.MESH
F32 = jnp.float32
BF16 = jnp.bfloat16

GROUP = 4
RING = 16
LINE = 8
ROWS = 4
UNITS = 64

UP_W, DOWN_W, UP_C, DOWN_C, RING_L, RING_R, BACK_L, BACK_R, LOCAL, LEFT, RIGHT = (
    0, 4, 8, 12, 16, 32, 48, 68, 88, 104, 108
)


def tridiagonal(length, coupling):
    return np.eye(length) + coupling * (np.eye(length, k=1) + np.eye(length, k=-1))


def smoothing_table():
    devices = GROUP * RING
    length = devices * ROWS
    matrix = tridiagonal(length, FILTER_ALPHA)
    inverse = np.linalg.inv(matrix)
    smoothing = np.linalg.solve(matrix, FILTER_GAIN * tridiagonal(length, 0.5))

    def move(row, pivot):
        return inverse[row, pivot] / inverse[pivot, pivot]

    table = np.zeros((devices, 128))
    block = GROUP * ROWS
    for device in range(devices):
        ring, member = divmod(device, GROUP)
        first = device * ROWS
        last = first + ROWS - 1
        entry = table[device]
        if device < devices - 1:
            entry[UP_W:UP_W + ROWS] = smoothing[last + 1, first:first + ROWS]
        if device > 0:
            entry[DOWN_W:DOWN_W + ROWS] = smoothing[first - 1, first:first + ROWS]
        group_first = ring * block
        group_last = group_first + block - 1
        for other in range(GROUP):
            start = group_first + other * ROWS
            if ring < RING - 1:
                entry[UP_C + other] = move(group_last + 1, start + ROWS)
            if ring > 0:
                entry[DOWN_C + other] = move(group_first - 1, start - 1)
        for other in range(RING):
            if other < ring:
                entry[RING_L + other] = move(group_first, (other + 1) * block)
            if other > ring:
                entry[RING_R + other] = move(group_last, other * block - 1)
        for target in range(GROUP):
            own_first = group_first + target * ROWS
            own_last = own_first + ROWS - 1
            entry[BACK_L + 5 * target] = move(own_first, group_first)
            entry[BACK_R + 5 * target] = move(own_last, group_last)
            for other in range(GROUP):
                start = group_first + other * ROWS
                if other < target:
                    entry[BACK_L + 5 * target + 1 + other] = move(own_first, start + ROWS)
                if other > target:
                    entry[BACK_R + 5 * target + 1 + other] = move(own_last, start - 1)
        entry[LOCAL:LOCAL + ROWS * ROWS] = smoothing[first:last + 1, first:last + 1].reshape(-1)
        for row in range(ROWS):
            entry[LEFT + row] = move(first + row, first)
            entry[RIGHT + row] = move(first + row, last)
    return table.astype(np.float32)


def derivative_matrix(length):
    right = 7.0 / 9.0 * (np.eye(length, k=1) - np.eye(length, k=-1)) + 1.0 / 36.0 * (
        np.eye(length, k=2) - np.eye(length, k=-2)
    )
    return np.linalg.solve(tridiagonal(length, COMPACT_ALPHA), right)


def line_table():
    size = 8
    length = LINE * size
    forward = derivative_matrix(length)
    table = np.zeros((LINE, size, 128))
    for place, matrix in enumerate((forward, forward.T)):
        base = 24 * place
        for device in range(LINE):
            rows = slice(device * size, device * size + size)
            table[device, :, base:base + 8] = matrix[rows, rows]
            if device < LINE - 1:
                table[device, 0, base + 8:base + 16] = matrix[device * size + 8, rows]
                table[device, 1, base + 8:base + 16] = matrix[device * size + 9, rows]
            if device > 0:
                table[device, 2, base + 8:base + 16] = matrix[device * size - 1, rows]
                table[device, 3, base + 8:base + 16] = matrix[device * size - 2, rows]
            for source in range(LINE):
                if source == device:
                    continue
                columns = slice(source * size, source * size + size)
                pivot = source * size + 9 if source < device else source * size - 2
                sent = matrix[pivot, columns]
                factors = matrix[rows, columns] @ sent / (sent @ sent)
                if source == device - 1:
                    factors[0] = 0.0
                if source == device + 1:
                    factors[size - 1] = 0.0
                table[device, :, base + 16 + source] = factors
    table[1:, 0, 48] = 1.0
    table[:-1, size - 1, 49] = 1.0
    return table.astype(np.float32)


def split_table(matrix):
    high = matrix.astype(np.float32).astype(ml_dtypes.bfloat16)
    low = (matrix - high.astype(np.float64)).astype(np.float32).astype(ml_dtypes.bfloat16)
    return [high, low]


def depth_table(length):
    matrix = derivative_matrix(length)
    return np.stack(split_table(matrix.T.copy()) + split_table(matrix))


def split(values):
    high = values.astype(BF16)
    return high, (values - high.astype(F32)).astype(BF16)


def iota(shape, dim):
    return lax.broadcasted_iota(jnp.int32, shape, dim)


def ones_where(condition):
    return jnp.where(condition, 1.0, 0.0).astype(F32)


def matmul(a, b):
    return jnp.dot(a, b, preferred_element_type=F32)


def matmul_nt(a, b, precision=None):
    return lax.dot_general(a, b, (((1,), (1,)), ((), ())), precision=precision, preferred_element_type=F32)


def kernel(
    velocity, cotangent, weight_in, bias_in, weight_out, x_table, y_table, z_table,
    new_velocity, grad_velocity, grad_weights,
    w_in, w_bias, w_out, vel, cot, smoothed, feats, gfeats, pulled, nvel, gvel, scalars, columns, tall, ztab,
    left_lhs, back_lhs, force_lhs, rhs, hidden_buf, pre_buf, sums, totals,
    x1_send, x1_recv, x2_send, x2_recv, x3_send, x3_recv, y_send, y_recv, y_edge,
    p1, p2, p3,
    token, local_sem, x1_ss, x1_rs, x2_ss, x2_rs, x3_ss, x3_rs, y_ss, y_rs, ye_ss, ye_rs,
    p1_ss, p1_rs, p2_ss, p2_rs, p3_ss, p3_rs,
):
    gx = lax.axis_index("gx")
    gy = lax.axis_index("gy")
    ring = lax.div(gx, GROUP)
    member = lax.rem(gx, GROUP)

    def in_group(step):
        return lax.rem(member + step, GROUP)

    def in_ring(step):
        return lax.rem(ring + step, RING)

    def in_line(step):
        return lax.rem(gy + step, LINE)

    def group_device(other):
        return (ring * GROUP + other, gy)

    def ring_device(other):
        return (other * GROUP + member, gy)

    def line_device(other):
        return (gx, other)

    barrier = pltpu.get_barrier_semaphore()
    half = RING // 4
    near = list(range(1, half + 1)) + list(range(RING - half, RING))
    partners = (
        [ring_device(in_ring(step)) for step in near]
        + [group_device(in_group(step)) for step in range(1, GROUP)]
        + [line_device(in_line(step)) for step in range(1, LINE)]
    )
    for partner in partners:
        pl.semaphore_signal(barrier, inc=1, device_id=partner, device_id_type=MESH)

    loads = [
        pltpu.make_async_copy(x_table.at[gx], scalars, local_sem.at[0]),
        pltpu.make_async_copy(velocity, vel, local_sem.at[1]),
        pltpu.make_async_copy(y_table.at[gy], columns, local_sem.at[2]),
        pltpu.make_async_copy(weight_in, w_in, local_sem.at[3]),
        pltpu.make_async_copy(bias_in, w_bias, local_sem.at[4]),
        pltpu.make_async_copy(weight_out, w_out, local_sem.at[5]),
        pltpu.make_async_copy(cotangent, cot, local_sem.at[6]),
        pltpu.make_async_copy(z_table, ztab, local_sem.at[7]),
    ]
    for load in loads:
        load.start()

    def remote(src, dst, send_sem, recv_sem, device):
        return pltpu.make_async_remote_copy(
            src_ref=src, dst_ref=dst, send_sem=send_sem, recv_sem=recv_sem, device_id=device, device_id_type=MESH
        )

    sent = []

    def send(*args):
        copy = remote(*args)
        copy.start()
        sent.append(copy)

    def scalar(index):
        return scalars[0, index]

    def build_weights():
        w_high, w_low = split(w_in[...])
        spread = ones_where(lax.shift_right_logical(iota((512, UNITS), 0), 3) == iota((512, UNITS), 1)).astype(BF16)
        spread_t = ones_where(iota((UNITS, 512), 0) == lax.shift_right_logical(iota((UNITS, 512), 1), 3)).astype(BF16)
        bias = w_bias[...]
        b_high, b_low = split(bias)
        b_rest = bias - b_high.astype(F32) - b_low.astype(F32)
        row = iota((8, 256), 0)
        col = iota((8, 256), 1)
        field = lax.shift_right_logical(col, 3)
        pick_high = ones_where(((field == row) | (field == row + 6)) & (row < 6)).astype(BF16)
        pick_low = ones_where((field == row + 12) & (row < 6)).astype(BF16)
        spread_high = matmul_nt(spread, w_high).astype(BF16)
        spread_low = matmul_nt(spread, w_low).astype(BF16)
        top = matmul(spread_high, pick_high[0:6]) + matmul(spread_low, pick_low[0:6])
        same = lax.bitwise_and(iota((512, 256), 0), 7) == lax.bitwise_and(iota((512, 256), 1), 7)
        top = jnp.where(same, top, 0.0)
        biases = jnp.concatenate([b_high.astype(F32), b_low.astype(F32), b_rest, jnp.zeros((5, UNITS), F32)], axis=0)
        spread_bias = matmul_nt(spread, biases.astype(BF16)).astype(BF16)
        top = top + matmul(spread_bias, ones_where(col == row + 240).astype(BF16))
        left_lhs[0:512, :] = top.astype(BF16)
        o_high, o_low = split(w_out[...])
        pick_high = ones_where(((field == row + 18) | (field == row + 22)) & (row < 3)).astype(BF16)
        pick_low = ones_where((field == row + 26) & (row < 3)).astype(BF16)
        spread_oh = matmul_nt(spread, o_high).astype(BF16)
        spread_ol = matmul_nt(spread, o_low).astype(BF16)
        bottom = matmul(spread_oh, pick_high[0:3]) + matmul(spread_ol, pick_low[0:3])
        left_lhs[512:1024, :] = jnp.where(same, bottom, 0.0).astype(BF16)

        same_t = lax.bitwise_and(iota((96, 512), 0), 7) == lax.bitwise_and(iota((96, 512), 1), 7)
        row = lax.shift_right_logical(iota((96, 8), 0), 3)
        col = iota((96, 8), 1)
        get_high = ones_where((row == col) & (col < 6)).astype(BF16)
        get_low = ones_where((row == col + 6) & (col < 6)).astype(BF16)
        tall_w = matmul(get_high[:, 0:6], w_high) + matmul(get_low[:, 0:6], w_low)
        back_lhs[...] = jnp.where(same_t, matmul(tall_w.astype(BF16), spread_t), 0.0).astype(BF16)
        get_high = ones_where((row[0:64] == col[0:64]) & (col[0:64] < 3)).astype(BF16)
        get_low = ones_where((row[0:64] == col[0:64] + 4) & (col[0:64] < 3)).astype(BF16)
        tall_o = matmul(get_high[:, 0:3], o_high) + matmul(get_low[:, 0:3], o_low)
        force_lhs[...] = jnp.where(same_t[0:64], matmul(tall_o.astype(BF16), spread_t), 0.0).astype(BF16)

    def build_columns():
        loads[2].wait()
        line_columns = columns[...]
        for index in range(50):
            tall[index] = jnp.broadcast_to(line_columns[:, index:index + 1], (8, 128))
        for load in loads[3:6]:
            load.wait()
        build_weights()

    def tall_column(index):
        half = tall[index]
        return jnp.concatenate([half, half], axis=1)

    def smooth(src, order, before_send, in_first, before_second, in_second, late_second, emit):
        for comp in range(3):
            rows = [src[comp, row] for row in range(ROWS)]
            for kind, base in ((0, UP_W), (1, DOWN_W)):
                state = sum(scalar(base + row) * rows[row] for row in range(ROWS))
                for piece in range(GROUP):
                    x1_send[order, piece, kind, comp] = state[2 * piece:2 * piece + 2]
        before_send()
        for step in (2, 1, 3):
            other = in_group(step)
            send(
                x1_send.at[order, other], x1_recv.at[order, member],
                x1_ss.at[order, other], x1_rs.at[order, member], group_device(other),
            )
        x1_recv[order, member] = x1_send[order, member]
        in_first()
        for step in range(1, GROUP):
            other = in_group(step)
            remote(
                x1_send.at[order, other], x1_recv.at[order, other],
                x1_ss.at[order, other], x1_rs.at[order, other], group_device(other),
            ).wait_recv()
        ups = [x1_recv[order, other, 0] for other in range(GROUP)]
        downs = [x1_recv[order, other, 1] for other in range(GROUP)]
        x2_send[order, 0] = sum(scalar(UP_C + other) * ups[other] for other in range(GROUP))
        x2_send[order, 1] = sum(scalar(DOWN_C + other) * downs[other] for other in range(GROUP))
        before_second()
        for step in (8, 7, 9, 6, 10, 5, 11, 4, 12, 3, 13, 2, 14, 1, 15):
            other = in_ring(step)
            kind = jnp.where(other > ring, 0, 1)
            send(
                x2_send.at[order, kind], x2_recv.at[order, ring],
                x2_ss.at[order, other], x2_rs.at[order, ring], ring_device(other),
            )
        in_second()
        left = jnp.zeros((3, 2, 256), F32)
        right = jnp.zeros((3, 2, 256), F32)
        for step in (1, 15, 2, 14, 3, 13, 4, 12, 5, 11, 6, 10, 7, 9, 8):
            if step == 5:
                late_second()
            other = in_ring(step)
            remote(
                x2_send.at[order, 0], x2_recv.at[order, other],
                x2_ss.at[order, other], x2_rs.at[order, other], ring_device(other),
            ).wait_recv()
            part = x2_recv[order, other]
            left = left + scalar(RING_L + other) * part
            right = right + scalar(RING_R + other) * part
        for step in (2, 1, 3, 0):
            other = in_group(step)
            target_left = scalar(BACK_L + 5 * other) * left
            target_right = scalar(BACK_R + 5 * other) * right
            for source in range(GROUP):
                target_left = target_left + scalar(BACK_L + 5 * other + 1 + source) * ups[source]
                target_right = target_right + scalar(BACK_R + 5 * other + 1 + source) * downs[source]
            if step == 0:
                x3_recv[order, member, 0] = target_left
                x3_recv[order, member, 1] = target_right
            else:
                x3_send[order, other, 0] = target_left
                x3_send[order, other, 1] = target_right
                send(
                    x3_send.at[order, other], x3_recv.at[order, member],
                    x3_ss.at[order, other], x3_rs.at[order, member], group_device(other),
                )
        for step in range(1, GROUP):
            other = in_group(step)
            remote(
                x3_send.at[order, other], x3_recv.at[order, other],
                x3_ss.at[order, other], x3_rs.at[order, other], group_device(other),
            ).wait_recv()
        for comp in range(3):
            rows = [src[comp, row] for row in range(ROWS)]
            from_left = jnp.concatenate([x3_recv[order, piece, 0, comp] for piece in range(GROUP)], axis=0)
            from_right = jnp.concatenate([x3_recv[order, piece, 1, comp] for piece in range(GROUP)], axis=0)
            for row in range(ROWS):
                total = scalar(LEFT + row) * from_left + scalar(RIGHT + row) * from_right
                for col in range(ROWS):
                    total = total + scalar(LOCAL + ROWS * row + col) * rows[col]
                emit(comp, row, total)

    def line_send(load, order):
        base = 24 * order
        sent_columns = [tall_column(base + 8 + col) for col in range(8)]
        for comp in range(3):
            for row in range(ROWS):
                tile = load(comp, row)
                out = sum(sent_columns[col] * tile[col:col + 1] for col in range(8))
                for kind in range(4):
                    y_send[order, kind, comp, row:row + 1, :] = out[kind:kind + 1]
        for kind, step in ((0, 1), (1, LINE - 1)):
            send(
                y_send.at[order, 2 * kind], y_edge.at[order, kind],
                ye_ss.at[order, kind], ye_rs.at[order, kind], line_device(in_line(step)),
            )
        for step in (4, 5, 3, 2, 6, 1, 7):
            other = in_line(step)
            kind = jnp.where(other > gy, 1, 3)
            send(
                y_send.at[order, kind], y_recv.at[order, gy],
                y_ss.at[order, other], y_rs.at[order, gy], line_device(other),
            )

    def line_local(load, order, store):
        base = 24 * order
        local_columns = [tall_column(base + col) for col in range(8)]
        for comp in range(3):
            for row in range(ROWS):
                tile = load(comp, row)
                store(comp, row, sum(local_columns[col] * tile[col:col + 1] for col in range(8)))

    def line_receive(order, load, store):
        base = 24 * order
        for kind, step in ((0, LINE - 1), (1, 1)):
            remote(
                y_send.at[order, 0], y_edge.at[order, kind],
                ye_ss.at[order, kind], ye_rs.at[order, kind], line_device(in_line(step)),
            ).wait_recv()
        for step in range(1, LINE):
            other = in_line(step)
            remote(
                y_send.at[order, 1], y_recv.at[order, other],
                y_ss.at[order, other], y_rs.at[order, other], line_device(other),
            ).wait_recv()
        y_recv[order, gy] = jnp.zeros((3, ROWS, 256), F32)
        factors = [tall_column(base + 16 + source) for source in range(LINE)]
        first = tall_column(48)
        last = tall_column(49)
        for comp in range(3):
            for row in range(ROWS):
                total = load(comp, row)
                total = total + first * y_edge[order, 0, comp, row:row + 1, :]
                total = total + last * y_edge[order, 1, comp, row:row + 1, :]
                for source in range(LINE):
                    total = total + factors[source] * y_recv[order, source, comp, row:row + 1, :]
                store(comp, row, total)

    def depth_apply(values, order):
        high, low = split(values)
        both = matmul(jnp.concatenate([high, low], axis=0), ztab[2 * order])
        count = values.shape[0]
        return both[0:count] + both[count:2 * count] + matmul(high, ztab[2 * order + 1])

    def pass_tokens():
        pl.semaphore_wait(barrier, len(partners))
        for kind, step in ((0, half), (1, RING - half)):
            pl.semaphore_signal(
                token.at[kind], inc=1, device_id=ring_device(in_ring(step)), device_id_type=MESH
            )

    def wait_tokens():
        for kind in range(2):
            pl.semaphore_wait(token.at[kind], 1)

    def nothing():
        pass

    def keep_smoothed(comp, row, value):
        smoothed[comp, row] = value

    def load_rest():
        for load in loads[6:]:
            load.wait()

    loads[0].wait()
    loads[1].wait()
    build_columns()
    smooth(vel, 0, pass_tokens, load_rest, wait_tokens, nothing, nothing, keep_smoothed)

    line_send(lambda comp, row: smoothed[comp, row], 0)
    along_z = depth_apply(smoothed[...].reshape(96, 256), 0)
    for comp in range(3):
        for row in range(ROWS):
            start = (comp * ROWS + row) * 8
            feats[row, 24 + 8 * comp:32 + 8 * comp, :] = along_z[start:start + 8]

    def store_feature(comp, row, value):
        feats[row, 8 * comp:8 * comp + 8, :] = value

    line_local(lambda comp, row: smoothed[comp, row], 0, store_feature)
    line_receive(0, lambda comp, row: feats[row, 8 * comp:8 * comp + 8, :], store_feature)

    def outward(row):
        parts = [STEP_SIZE * cot[comp, row] for comp in range(3)]
        return jnp.concatenate(parts + [jnp.zeros((8, 256), F32)], axis=0)

    def closure(row, carry):
        feature_high, feature_low = split(feats[row])
        rhs[0:48, :] = feature_high
        rhs[48:96, :] = feature_low
        rhs[96:144, :] = feature_high
        out_high, out_low = split(outward(row))
        rhs[144:176, :] = out_high
        rhs[176:208, :] = out_low
        rhs[208:240, :] = out_high
        rhs[240:256, :] = jnp.ones((16, 256), BF16)
        hidden = jnp.tanh(matmul(left_lhs[0:512, :], rhs[...]))
        grad_pre = matmul(left_lhs[512:1024, :], rhs[...]) * (1.0 - hidden * hidden)
        pre_high, pre_low = split(grad_pre)
        hidden_buf[row] = hidden
        pre_buf[row, 0] = pre_high
        pre_buf[row, 1] = pre_low
        both = matmul(back_lhs[...], pre_high)
        gfeats[row] = both[0:48] + both[48:96] + matmul(back_lhs[0:48, :], pre_low)
        return carry

    lax.fori_loop(0, ROWS, closure, 0)

    line_send(lambda comp, row: gfeats[row, 8 * comp:8 * comp + 8, :], 1)
    back_in = jnp.concatenate(
        [gfeats[row, 24 + 8 * comp:32 + 8 * comp, :] for comp in range(3) for row in range(ROWS)], axis=0
    )
    along_z = depth_apply(back_in, 1)

    def add_depth(comp, row, value):
        start = (comp * ROWS + row) * 8
        pulled[comp, row] = value + along_z[start:start + 8]

    line_local(lambda comp, row: gfeats[row, 8 * comp:8 * comp + 8, :], 1, add_depth)

    def forces_and_sums(row, carry):
        hidden_high, hidden_low = split(hidden_buf[row])
        both = matmul(force_lhs[...], hidden_high)
        forcing = both[0:32] + both[32:64] + matmul(force_lhs[0:32, :], hidden_low)
        for comp in range(3):
            nvel[comp, row] = vel[comp, row] + STEP_SIZE * forcing[8 * comp:8 * comp + 8]
        feature_high, feature_low = split(feats[row])
        ones = jnp.ones((16, 256), BF16)
        both = matmul_nt(jnp.concatenate([feature_high, ones, feature_low], axis=0), pre_buf[row, 0])
        rest = matmul_nt(jnp.concatenate([feature_high, ones], axis=0), pre_buf[row, 1])
        sums[0:48, :] += both[0:48] + both[64:112] + rest[0:48]
        sums[48:56, :] += both[48:56] + rest[48:56]
        out_high, out_low = split(outward(row))
        both = matmul_nt(jnp.concatenate([out_high, out_low], axis=0), hidden_high)
        rest = matmul_nt(out_high, hidden_low)
        sums[56:88, :] += both[0:32] + both[32:64] + rest
        return carry

    def first_sums():
        sums[...] = jnp.zeros((88, 512), F32)
        lax.fori_loop(0, ROWS // 2, forces_and_sums, 0)

    def last_sums():
        lax.fori_loop(ROWS // 2, ROWS, forces_and_sums, 0)
        same = lax.bitwise_and(iota((88, 512), 0), 7) == lax.bitwise_and(iota((88, 512), 1), 7)
        gather = ones_where(lax.shift_right_logical(iota((512, UNITS), 0), 3) == iota((512, UNITS), 1)).astype(BF16)
        high, low = split(jnp.where(same, sums[...], 0.0))
        narrow = matmul(high, gather) + matmul(low, gather)
        folded = [jnp.sum(narrow[8 * part:8 * part + 8], axis=0, keepdims=True) for part in range(11)]
        front = jnp.concatenate(folded[0:8], axis=0)
        back = jnp.concatenate(folded[8:11] + [jnp.zeros((5, UNITS), F32)], axis=0)
        p1[gy] = jnp.concatenate([front, back], axis=1)
        for step in range(1, LINE):
            other = in_line(step)
            send(p1.at[gy], p1.at[gy], p1_ss.at[other], p1_rs.at[gy], line_device(other))

    def sum_line():
        for step in range(1, LINE):
            other = in_line(step)
            remote(p1.at[other], p1.at[other], p1_ss.at[other], p1_rs.at[other], line_device(other)).wait_recv()
        total = p1[0]
        for other in range(1, LINE):
            total = total + p1[other]
        p2[member] = total
        for step in range(1, GROUP):
            other = in_group(step)
            send(p2.at[member], p2.at[member], p2_ss.at[other], p2_rs.at[member], group_device(other))

    def sum_group():
        for step in range(1, GROUP):
            other = in_group(step)
            remote(p2.at[other], p2.at[other], p2_ss.at[other], p2_rs.at[other], group_device(other)).wait_recv()
        total = p2[0]
        for other in range(1, GROUP):
            total = total + p2[other]
        p3[ring] = total
        for step in (8, 7, 9, 6, 10, 5, 11, 4, 12, 3, 13, 2, 14, 1, 15):
            other = in_ring(step)
            send(p3.at[ring], p3.at[ring], p3_ss.at[other], p3_rs.at[ring], ring_device(other))

    def sum_ring():
        for step in range(1, RING):
            other = in_ring(step)
            remote(p3.at[other], p3.at[other], p3_ss.at[other], p3_rs.at[other], ring_device(other)).wait_recv()
        total = p3[0]
        for other in range(1, RING):
            total = total + p3[other]
        totals[...] = total * (1.0 / float(256 * 64 * 256))

    first_sums()

    def keep_pulled(comp, row, value):
        pulled[comp, row] = value

    line_receive(1, lambda comp, row: pulled[comp, row], keep_pulled)

    def keep_gradient(comp, row, value):
        gvel[comp, row] = cot[comp, row] + value

    stores = [
        pltpu.make_async_copy(nvel, new_velocity, local_sem.at[0]),
        pltpu.make_async_copy(gvel, grad_velocity, local_sem.at[1]),
        pltpu.make_async_copy(totals, grad_weights, local_sem.at[2]),
    ]

    def store_velocity():
        stores[0].start()
        sum_line()

    smooth(pulled, 1, nothing, last_sums, nothing, store_velocity, sum_group, keep_gradient)
    stores[1].start()
    sum_ring()
    stores[2].start()
    for copy in sent:
        copy.wait_send()
    for store in stores:
        store.wait()


def finish(new_velocity_in, grad_velocity_in, grads, new_velocity, grad_velocity, grad_in, grad_bias, grad_out_t):
    new_velocity[...] = new_velocity_in[...]
    grad_velocity[...] = grad_velocity_in[...]
    front = grads[:, 0:UNITS]
    grad_in[...] = front[0:6]
    grad_bias[...] = front[6:7]
    grad_out_t[0:1] = front[7:8]
    grad_out_t[1:3] = grads[0:2, UNITS:2 * UNITS]


def local(velocity, cotangent, weight_in, bias_in, weight_out):
    field = velocity.shape
    dma = pltpu.SemaphoreType.DMA
    anywhere = pl.BlockSpec(memory_space=pl.ANY)
    whole = pl.BlockSpec(memory_space=pltpu.VMEM)
    mid = pl.pallas_call(
        kernel,
        out_shape=(
            jax.ShapeDtypeStruct(field, F32),
            jax.ShapeDtypeStruct(field, F32),
            jax.ShapeDtypeStruct((8, 128), F32),
        ),
        in_specs=[anywhere] * 8,
        out_specs=(anywhere, anywhere, anywhere),
        scratch_shapes=[
            pltpu.VMEM((6, UNITS), F32),
            pltpu.VMEM((1, UNITS), F32),
            pltpu.VMEM((3, UNITS), F32),
            pltpu.VMEM(field, F32),
            pltpu.VMEM(field, F32),
            pltpu.VMEM(field, F32),
            pltpu.VMEM((ROWS, 48, 256), F32),
            pltpu.VMEM((ROWS, 48, 256), F32),
            pltpu.VMEM(field, F32),
            pltpu.VMEM(field, F32),
            pltpu.VMEM(field, F32),
            pltpu.SMEM((1, 128), F32),
            pltpu.VMEM((8, 128), F32),
            pltpu.VMEM((50, 8, 128), F32),
            pltpu.VMEM((4, 256, 256), BF16),
            pltpu.VMEM((1024, 256), BF16),
            pltpu.VMEM((96, 512), BF16),
            pltpu.VMEM((64, 512), BF16),
            pltpu.VMEM((256, 256), BF16),
            pltpu.VMEM((ROWS, 512, 256), F32),
            pltpu.VMEM((ROWS, 2, 512, 256), BF16),
            pltpu.VMEM((88, 512), F32),
            pltpu.VMEM((8, 128), F32),
            pltpu.VMEM((2, GROUP, 2, 3, 2, 256), F32),
            pltpu.VMEM((2, GROUP, 2, 3, 2, 256), F32),
            pltpu.VMEM((2, 2, 3, 2, 256), F32),
            pltpu.VMEM((2, RING, 3, 2, 256), F32),
            pltpu.VMEM((2, GROUP, 2, 3, 2, 256), F32),
            pltpu.VMEM((2, GROUP, 2, 3, 2, 256), F32),
            pltpu.VMEM((2, 4, 3, ROWS, 256), F32),
            pltpu.VMEM((2, LINE, 3, ROWS, 256), F32),
            pltpu.VMEM((2, 2, 3, ROWS, 256), F32),
            pltpu.VMEM((LINE, 8, 128), F32),
            pltpu.VMEM((GROUP, 8, 128), F32),
            pltpu.VMEM((RING, 8, 128), F32),
            pltpu.SemaphoreType.REGULAR((2,)),
            dma((8,)),
            dma((2, GROUP)), dma((2, GROUP)),
            dma((2, RING)), dma((2, RING)),
            dma((2, GROUP)), dma((2, GROUP)),
            dma((2, LINE)), dma((2, LINE)),
            dma((2, 2)), dma((2, 2)),
            dma((LINE,)), dma((LINE,)),
            dma((GROUP,)), dma((GROUP,)),
            dma((RING,)), dma((RING,)),
        ],
        compiler_params=pltpu.CompilerParams(collective_id=0, has_side_effects=True),
        name="closure_step",
    )(
        velocity, cotangent, weight_in, bias_in.reshape(1, UNITS), weight_out.T,
        jnp.asarray(smoothing_table()).reshape(GROUP * RING, 1, 128), jnp.asarray(line_table()),
        jnp.asarray(depth_table(field[3])),
    )
    outs = pl.pallas_call(
        finish,
        out_shape=(
            jax.ShapeDtypeStruct(field, F32),
            jax.ShapeDtypeStruct(field, F32),
            jax.ShapeDtypeStruct((6, UNITS), F32),
            jax.ShapeDtypeStruct((1, UNITS), F32),
            jax.ShapeDtypeStruct((3, UNITS), F32),
        ),
        in_specs=[whole] * 3,
        out_specs=(whole,) * 5,
        name="finish",
    )(*mid)
    return outs[0], outs[1], outs[2], outs[3].reshape(UNITS), outs[4].T


def solution(mesh):
    in_specs = (P(None, "gx", "gy", None), P(None, "gx", "gy", None), P(), P(), P())
    out_specs = (P(None, "gx", "gy", None), P(None, "gx", "gy", None), P(), P(), P())
    return jax.shard_map(local, mesh=mesh, in_specs=in_specs, out_specs=out_specs, check_vma=False)
```

```python
import functools

import jax
import jax.numpy as jnp
import ml_dtypes
import numpy as np
from jax import lax
from jax.experimental import pallas as pl
from jax.experimental.pallas import tpu as pltpu
from jax.sharding import PartitionSpec as P

FILTER_ALPHA = 0.499
FILTER_GAIN = 0.5 + FILTER_ALPHA
COMPACT_ALPHA = 1.0 / 3.0
STEP_SIZE = 0.5
MESH = pl.DeviceIdType.MESH
F32 = jnp.float32
BF16 = jnp.bfloat16

GROUP = 4
RING = 16
LINE = 8
ROWS = 4
UNITS = 64

UP_W, DOWN_W, UP_C, DOWN_C, RING_L, RING_R, BACK_L, BACK_R, LOCAL, LEFT, RIGHT = (
    0, 4, 8, 12, 16, 32, 48, 68, 88, 104, 108
)


def tridiagonal(length, coupling):
    return np.eye(length) + coupling * (np.eye(length, k=1) + np.eye(length, k=-1))


def smoothing_table():
    devices = GROUP * RING
    length = devices * ROWS
    matrix = tridiagonal(length, FILTER_ALPHA)
    inverse = np.linalg.inv(matrix)
    smoothing = np.linalg.solve(matrix, FILTER_GAIN * tridiagonal(length, 0.5))

    def move(row, pivot):
        return inverse[row, pivot] / inverse[pivot, pivot]

    table = np.zeros((devices, 128))
    block = GROUP * ROWS
    for device in range(devices):
        ring, member = divmod(device, GROUP)
        first = device * ROWS
        last = first + ROWS - 1
        entry = table[device]
        if device < devices - 1:
            entry[UP_W:UP_W + ROWS] = smoothing[last + 1, first:first + ROWS]
        if device > 0:
            entry[DOWN_W:DOWN_W + ROWS] = smoothing[first - 1, first:first + ROWS]
        group_first = ring * block
        group_last = group_first + block - 1
        for other in range(GROUP):
            start = group_first + other * ROWS
            if ring < RING - 1:
                entry[UP_C + other] = move(group_last + 1, start + ROWS)
            if ring > 0:
                entry[DOWN_C + other] = move(group_first - 1, start - 1)
        for other in range(RING):
            if other < ring:
                entry[RING_L + other] = move(group_first, (other + 1) * block)
            if other > ring:
                entry[RING_R + other] = move(group_last, other * block - 1)
        for target in range(GROUP):
            own_first = group_first + target * ROWS
            own_last = own_first + ROWS - 1
            entry[BACK_L + 5 * target] = move(own_first, group_first)
            entry[BACK_R + 5 * target] = move(own_last, group_last)
            for other in range(GROUP):
                start = group_first + other * ROWS
                if other < target:
                    entry[BACK_L + 5 * target + 1 + other] = move(own_first, start + ROWS)
                if other > target:
                    entry[BACK_R + 5 * target + 1 + other] = move(own_last, start - 1)
        entry[LOCAL:LOCAL + ROWS * ROWS] = smoothing[first:last + 1, first:last + 1].reshape(-1)
        for row in range(ROWS):
            entry[LEFT + row] = move(first + row, first)
            entry[RIGHT + row] = move(first + row, last)
    return table.astype(np.float32)


def derivative_matrix(length):
    right = 7.0 / 9.0 * (np.eye(length, k=1) - np.eye(length, k=-1)) + 1.0 / 36.0 * (
        np.eye(length, k=2) - np.eye(length, k=-2)
    )
    return np.linalg.solve(tridiagonal(length, COMPACT_ALPHA), right)


def line_table():
    size = 8
    length = LINE * size
    forward = derivative_matrix(length)
    table = np.zeros((LINE, size, 128))
    for place, matrix in enumerate((forward, forward.T)):
        base = 24 * place
        for device in range(LINE):
            rows = slice(device * size, device * size + size)
            table[device, :, base:base + 8] = matrix[rows, rows]
            if device < LINE - 1:
                table[device, 0, base + 8:base + 16] = matrix[device * size + 8, rows]
                table[device, 1, base + 8:base + 16] = matrix[device * size + 9, rows]
            if device > 0:
                table[device, 2, base + 8:base + 16] = matrix[device * size - 1, rows]
                table[device, 3, base + 8:base + 16] = matrix[device * size - 2, rows]
            for step in range(1, LINE):
                source = (device - step) % LINE
                columns = slice(source * size, source * size + size)
                pivot = source * size + 9 if source < device else source * size - 2
                sent = matrix[pivot, columns]
                factors = matrix[rows, columns] @ sent / (sent @ sent)
                if source == device - 1:
                    factors[0] = 0.0
                if source == device + 1:
                    factors[size - 1] = 0.0
                table[device, :, base + 16 + step] = factors
    table[1:, 0, 48] = 1.0
    table[:-1, size - 1, 49] = 1.0
    return table.astype(np.float32)


def split_table(matrix):
    high = matrix.astype(np.float32).astype(ml_dtypes.bfloat16)
    low = (matrix - high.astype(np.float64)).astype(np.float32).astype(ml_dtypes.bfloat16)
    return [high, low]


def depth_table(length):
    matrix = derivative_matrix(length)
    return np.stack(split_table(matrix.T.copy()) + split_table(matrix))


def split(values):
    high = values.astype(BF16)
    return high, (values - high.astype(F32)).astype(BF16)


def iota(shape, dim):
    return lax.broadcasted_iota(jnp.int32, shape, dim)


def ones_where(condition):
    return jnp.where(condition, 1.0, 0.0).astype(F32)


def matmul(a, b):
    return jnp.dot(a, b, preferred_element_type=F32)


def matmul_nt(a, b, precision=None):
    return lax.dot_general(a, b, (((1,), (1,)), ((), ())), precision=precision, preferred_element_type=F32)


def kernel(
    velocity, cotangent, weight_in, bias_in, weight_out, x_table, y_table, z_table,
    new_velocity, grad_velocity, grad_weights,
    w_in, w_bias, w_out, vel, cot, along_y, smoothed, feats, gfeats, pulled, nvel, gvel,
    scalars, columns, tall, ztab,
    left_lhs, back_lhs, force_lhs, rhs, hidden_buf, pre_buf, sums, totals,
    x1_send, x1_recv, state, x2_send, x2_recv, x3_send, x3_recv, plane_send, plane_recv, plane_edge,
    y_send, y_recv, y_edge,
    p1, p2, p3,
    token, local_sem, x1_ss, x1_rs, x2_ss, x2_rs, x3_ss, x3_rs, plane_ss, plane_rs, edge_ss, edge_rs,
    y_ss, y_rs, ye_ss, ye_rs,
    p1_ss, p1_rs, p2_ss, p2_rs, p3_ss, p3_rs,
):
    gx = lax.axis_index("gx")
    gy = lax.axis_index("gy")
    ring = lax.div(gx, GROUP)
    member = lax.rem(gx, GROUP)

    def in_group(step):
        return lax.rem(member + step, GROUP)

    def in_ring(step):
        return lax.rem(ring + step, RING)

    def in_line(step):
        return lax.rem(gy + step, LINE)

    def group_device(other):
        return (ring * GROUP + other, gy)

    def ring_device(other):
        return (other * GROUP + member, gy)

    def line_device(other):
        return (gx, other)

    def plane_device(other, place):
        return (ring * GROUP + other, place)

    barrier = pltpu.get_barrier_semaphore()
    half = RING // 4
    near = list(range(1, half + 1)) + list(range(RING - half, RING))
    partners = (
        [ring_device(in_ring(step)) for step in near]
        + [
            plane_device(in_group(step), in_line(along))
            for step in range(GROUP) for along in range(LINE) if step or along
        ]
    )
    for partner in partners:
        pl.semaphore_signal(barrier, inc=1, device_id=partner, device_id_type=MESH)

    loads = [
        pltpu.make_async_copy(x_table.at[gx], scalars, local_sem.at[0]),
        pltpu.make_async_copy(velocity, vel, local_sem.at[1]),
        pltpu.make_async_copy(y_table.at[gy], columns, local_sem.at[2]),
        pltpu.make_async_copy(weight_in, w_in, local_sem.at[3]),
        pltpu.make_async_copy(bias_in, w_bias, local_sem.at[4]),
        pltpu.make_async_copy(weight_out, w_out, local_sem.at[5]),
        pltpu.make_async_copy(cotangent, cot, local_sem.at[6]),
        pltpu.make_async_copy(z_table, ztab, local_sem.at[7]),
    ]
    for load in loads:
        load.start()

    def remote(src, dst, send_sem, recv_sem, device):
        return pltpu.make_async_remote_copy(
            src_ref=src, dst_ref=dst, send_sem=send_sem, recv_sem=recv_sem, device_id=device, device_id_type=MESH
        )

    sent = []

    def send(*args, drain=True):
        copy = remote(*args)
        copy.start()
        if drain:
            sent.append(copy)

    def scalar(index):
        return scalars[0, index]

    def build_weights():
        for load in loads[3:6]:
            load.wait()
        w_high, w_low = split(w_in[...])
        spread = ones_where(lax.shift_right_logical(iota((512, UNITS), 0), 3) == iota((512, UNITS), 1)).astype(BF16)
        spread_t = ones_where(iota((UNITS, 512), 0) == lax.shift_right_logical(iota((UNITS, 512), 1), 3)).astype(BF16)
        bias = w_bias[...]
        b_high, b_low = split(bias)
        b_rest = bias - b_high.astype(F32) - b_low.astype(F32)
        row = iota((8, 256), 0)
        col = iota((8, 256), 1)
        field = lax.shift_right_logical(col, 3)
        pick_high = ones_where(((field == row) | (field == row + 6)) & (row < 6)).astype(BF16)
        pick_low = ones_where((field == row + 12) & (row < 6)).astype(BF16)
        spread_high = matmul_nt(spread, w_high).astype(BF16)
        spread_low = matmul_nt(spread, w_low).astype(BF16)
        top = matmul(spread_high, pick_high[0:6]) + matmul(spread_low, pick_low[0:6])
        same = lax.bitwise_and(iota((512, 256), 0), 7) == lax.bitwise_and(iota((512, 256), 1), 7)
        top = jnp.where(same, top, 0.0)
        biases = jnp.concatenate([b_high.astype(F32), b_low.astype(F32), b_rest, jnp.zeros((5, UNITS), F32)], axis=0)
        spread_bias = matmul_nt(spread, biases.astype(BF16)).astype(BF16)
        top = top + matmul(spread_bias, ones_where(col == row + 240).astype(BF16))
        left_lhs[0:512, :] = top.astype(BF16)
        o_high, o_low = split(w_out[...])
        pick_high = ones_where(((field == row + 18) | (field == row + 22)) & (row < 3)).astype(BF16)
        pick_low = ones_where((field == row + 26) & (row < 3)).astype(BF16)
        spread_oh = matmul_nt(spread, o_high).astype(BF16)
        spread_ol = matmul_nt(spread, o_low).astype(BF16)
        bottom = matmul(spread_oh, pick_high[0:3]) + matmul(spread_ol, pick_low[0:3])
        left_lhs[512:1024, :] = jnp.where(same, bottom, 0.0).astype(BF16)

        same_t = lax.bitwise_and(iota((96, 512), 0), 7) == lax.bitwise_and(iota((96, 512), 1), 7)
        row = lax.shift_right_logical(iota((96, 8), 0), 3)
        col = iota((96, 8), 1)
        get_high = ones_where((row == col) & (col < 6)).astype(BF16)
        get_low = ones_where((row == col + 6) & (col < 6)).astype(BF16)
        tall_w = matmul(get_high[:, 0:6], w_high) + matmul(get_low[:, 0:6], w_low)
        back_lhs[...] = jnp.where(same_t, matmul(tall_w.astype(BF16), spread_t), 0.0).astype(BF16)
        get_high = ones_where((row[0:64] == col[0:64]) & (col[0:64] < 3)).astype(BF16)
        get_low = ones_where((row[0:64] == col[0:64] + 4) & (col[0:64] < 3)).astype(BF16)
        tall_o = matmul(get_high[:, 0:3], o_high) + matmul(get_low[:, 0:3], o_low)
        force_lhs[...] = jnp.where(same_t[0:64], matmul(tall_o.astype(BF16), spread_t), 0.0).astype(BF16)

    def build_columns():
        loads[2].wait()
        line_columns = columns[...]
        for index in range(50):
            tall[index] = jnp.broadcast_to(line_columns[:, index:index + 1], (8, 128))

    def tall_column(index):
        half = tall[index]
        return jnp.concatenate([half, half], axis=1)

    lower = iota((8, 128), 1) < 64

    def turn(tile):
        return pltpu.roll(tile, 64, 1)

    def pack(left, right, piece):
        lanes = slice(128 * (piece // 2), 128 * (piece // 2) + 128)
        if piece % 2 == 0:
            return jnp.where(lower, left[:, lanes], turn(right[:, lanes]))
        return jnp.where(lower, turn(left[:, lanes]), right[:, lanes])

    def unpack(pieces):
        left = [jnp.where(lower, pieces[2 * t], turn(pieces[2 * t + 1])) for t in range(2)]
        right = [jnp.where(lower, turn(pieces[2 * t]), pieces[2 * t + 1]) for t in range(2)]
        return jnp.concatenate(left, axis=1), jnp.concatenate(right, axis=1)

    def two_scalars(left_index, right_index):
        return jnp.where(lower, scalar(left_index), scalar(right_index))

    def states(rows):
        return [sum(scalar(base + row) * rows[row] for row in range(ROWS)) for base in (UP_W, DOWN_W)]

    def local_rows(rows):
        return [
            sum(scalar(LOCAL + ROWS * row + col) * rows[col] for col in range(ROWS)) for row in range(ROWS)
        ]

    def pieces_send(source, target, send_sems, recv_sems, order):
        for step in (2, 1, 3):
            other = in_group(step)
            send(
                source.at[order, other], target.at[order, member],
                send_sems.at[order, other], recv_sems.at[order, member], group_device(other),
            )

    def pieces_wait(source, target, send_sems, recv_sems, order):
        for step in range(1, GROUP):
            other = in_group(step)
            remote(
                source.at[order, other], target.at[order, other],
                send_sems.at[order, other], recv_sems.at[order, other], group_device(other),
            ).wait_recv()

    def ring_send(order, load):
        gathered = []
        for comp in range(3):
            gathered.append(sum(
                two_scalars(UP_C + other, DOWN_C + other) * load(other, comp) for other in range(GROUP)
            ))
        first, second, third = gathered
        turned = turn(third)
        front = jnp.where(lower, first, turn(second))
        x2_send[order, 0, 0] = front[0:4]
        x2_send[order, 0, 1] = front[4:8]
        x2_send[order, 0, 2] = jnp.where(lower[0:4], third[0:4], turned[4:8])
        front = jnp.where(lower, turn(first), second)
        x2_send[order, 1, 0] = front[0:4]
        x2_send[order, 1, 1] = front[4:8]
        x2_send[order, 1, 2] = jnp.where(lower[0:4], turned[0:4], third[4:8])
        for step in (8, 7, 9, 6, 10, 5, 11, 4, 12, 3, 13, 2, 14, 1, 15):
            other = in_ring(step)
            kind = jnp.where(other > ring, 0, 1)
            send(
                x2_send.at[order, kind], x2_recv.at[order, ring],
                x2_ss.at[order, other], x2_rs.at[order, ring], ring_device(other),
            )

    def ring_receive(order, midway):
        left = jnp.zeros((3, 4, 128), F32)
        right = jnp.zeros((3, 4, 128), F32)
        for step in (1, 15, 2, 14, 3, 13, 4, 12, 5, 11, 6, 10, 7, 9, 8):
            if step == 5:
                midway()
            other = in_ring(step)
            remote(
                x2_send.at[order, 0], x2_recv.at[order, other],
                x2_ss.at[order, other], x2_rs.at[order, other], ring_device(other),
            ).wait_recv()
            part = x2_recv[order, other]
            left = left + scalar(RING_L + other) * part
            right = right + scalar(RING_R + other) * part
        front_left = jnp.concatenate([left[0], left[1]], axis=0)
        front_right = jnp.concatenate([right[0], right[1]], axis=0)
        back_left = jnp.concatenate([left[2], pltpu.roll(left[2], 64, 1)], axis=0)
        back_right = jnp.concatenate([pltpu.roll(right[2], 64, 1), right[2]], axis=0)
        return [
            jnp.where(lower, front_left, turn(front_right)),
            jnp.where(lower, turn(front_left), front_right),
            jnp.where(lower, back_left, back_right),
        ]

    def back_piece(ring_state, load, other, comp):
        total = two_scalars(BACK_L + 5 * other, BACK_R + 5 * other) * ring_state[comp]
        for source in range(GROUP):
            index = 5 * other + 1 + source
            total = total + two_scalars(BACK_L + index, BACK_R + index) * load(source, comp)
        return total

    def project(order, other, comp, tile):
        out = sum(tall[24 * order + 8 + col] * tile[col:col + 1] for col in range(8))
        for kind in range(4):
            plane_send[order, other, kind, comp:comp + 1, :] = out[kind:kind + 1]

    def plane_rows_send(order):
        for step in (2, 1, 3, 0):
            other = in_group(step)
            for along in (4, 5, 3, 6, 2, 7, 1):
                place = in_line(along)
                kind = jnp.where(place > gy, 1, 3)
                send(
                    plane_send.at[order, other, kind], plane_recv.at[order, member, along - 1],
                    plane_ss.at[order], plane_rs.at[order], plane_device(other, place), drain=False,
                )
            for kind, along in ((0, 1), (1, LINE - 1)):
                send(
                    plane_send.at[order, other, 2 * kind], plane_edge.at[order, member, kind],
                    edge_ss.at[order], edge_rs.at[order], plane_device(other, in_line(along)), drain=False,
                )

    def plane_rows_all(order):
        device = plane_device(in_group(1), in_line(1))
        return (
            remote(plane_recv.at[order], plane_recv.at[order], plane_ss.at[order], plane_rs.at[order], device),
            remote(plane_edge.at[order], plane_edge.at[order], edge_ss.at[order], edge_rs.at[order], device),
        )

    def plane_rows_wait(order):
        for copy in plane_rows_all(order):
            copy.wait_recv()

    def plane_rows_drain(order):
        for copy in plane_rows_all(order):
            copy.wait_send()

    def from_plane(order, source, comp):
        total = tall[48] * plane_edge[order, source, 0, comp:comp + 1, :]
        total = total + tall[49] * plane_edge[order, source, 1, comp:comp + 1, :]
        for along in range(1, LINE):
            total = total + tall[24 * order + 16 + along] * plane_recv[order, source, along - 1, comp:comp + 1, :]
        return total

    def own_block(order, tile):
        return sum(tall[24 * order + col] * tile[col:col + 1] for col in range(8))

    def line_send(load, order):
        base = 24 * order
        sent_columns = [tall_column(base + 8 + col) for col in range(8)]
        for comp in range(3):
            for row in range(ROWS):
                tile = load(comp, row)
                out = sum(sent_columns[col] * tile[col:col + 1] for col in range(8))
                for kind in range(4):
                    y_send[order, kind, comp, row:row + 1, :] = out[kind:kind + 1]
        for kind, step in ((0, 1), (1, LINE - 1)):
            send(
                y_send.at[order, 2 * kind], y_edge.at[order, kind],
                ye_ss.at[order, kind], ye_rs.at[order, kind], line_device(in_line(step)),
            )
        for step in (4, 5, 3, 2, 6, 1, 7):
            other = in_line(step)
            kind = jnp.where(other > gy, 1, 3)
            send(
                y_send.at[order, kind], y_recv.at[order, step - 1],
                y_ss.at[order, step - 1], y_rs.at[order, step - 1], line_device(other),
            )

    def line_local(load, order, store):
        base = 24 * order
        local_columns = [tall_column(base + col) for col in range(8)]
        for comp in range(3):
            for row in range(ROWS):
                tile = load(comp, row)
                store(comp, row, sum(local_columns[col] * tile[col:col + 1] for col in range(8)))

    def line_receive(order, load, store):
        base = 24 * order
        for kind, step in ((0, LINE - 1), (1, 1)):
            remote(
                y_send.at[order, 0], y_edge.at[order, kind],
                ye_ss.at[order, kind], ye_rs.at[order, kind], line_device(in_line(step)),
            ).wait_recv()
        for step in range(1, LINE):
            remote(
                y_send.at[order, 1], y_recv.at[order, step - 1],
                y_ss.at[order, step - 1], y_rs.at[order, step - 1], line_device(in_line(step)),
            ).wait_recv()
        factors = [tall_column(base + 16 + step) for step in range(1, LINE)]
        first = tall_column(48)
        last = tall_column(49)
        for comp in range(3):
            for row in range(ROWS):
                total = load(comp, row)
                total = total + first * y_edge[order, 0, comp, row:row + 1, :]
                total = total + last * y_edge[order, 1, comp, row:row + 1, :]
                for step in range(1, LINE):
                    total = total + factors[step - 1] * y_recv[order, step - 1, comp, row:row + 1, :]
                store(comp, row, total)

    def depth_apply(values, order):
        high, low = split(values)
        both = matmul(jnp.concatenate([high, low], axis=0), ztab[2 * order])
        count = values.shape[0]
        return both[0:count] + both[count:2 * count] + matmul(high, ztab[2 * order + 1])

    def pass_tokens():
        pl.semaphore_wait(barrier, len(partners))
        for kind, step in ((0, half), (1, RING - half)):
            pl.semaphore_signal(
                token.at[kind], inc=1, device_id=ring_device(in_ring(step)), device_id_type=MESH
            )

    def wait_tokens():
        for kind in range(2):
            pl.semaphore_wait(token.at[kind], 1)

    def nothing():
        pass

    loads[0].wait()
    loads[1].wait()
    for comp in range(3):
        left, right = states([vel[comp, row] for row in range(ROWS)])
        for piece in range(GROUP):
            x1_send[0, piece, comp] = pack(left, right, piece)
    build_columns()
    pass_tokens()
    pieces_send(x1_send, x1_recv, x1_ss, x1_rs, 0)
    line_send(lambda comp, row: vel[comp, row], 0)
    x1_recv[0, member] = x1_send[0, member]
    build_weights()
    for load in loads[6:]:
        load.wait()

    def keep_along(comp, row, value):
        along_y[comp, row] = value

    line_local(lambda comp, row: vel[comp, row], 0, keep_along)
    pieces_wait(x1_send, x1_recv, x1_ss, x1_rs, 0)
    wait_tokens()

    def first_piece(source, comp):
        return x1_recv[0, source, comp]

    ring_send(0, first_piece)
    line_receive(0, lambda comp, row: along_y[comp, row], keep_along)
    for comp in range(3):
        for row, value in enumerate(local_rows([vel[comp, row] for row in range(ROWS)])):
            smoothed[comp, row] = value
        for row, value in enumerate(local_rows([along_y[comp, row] for row in range(ROWS)])):
            feats[row, 8 * comp:8 * comp + 8, :] = value
    ring_state = ring_receive(0, nothing)
    for step in (2, 1, 3, 0):
        other = in_group(step)
        for comp in range(3):
            tile = back_piece(ring_state, first_piece, other, comp)
            x3_send[0, other, comp] = tile
            project(0, other, comp, tile)
    pieces_send(x3_send, x3_recv, x3_ss, x3_rs, 0)
    plane_rows_send(0)
    x3_recv[0, member] = x3_send[0, member]
    pieces_wait(x3_send, x3_recv, x3_ss, x3_rs, 0)
    for comp in range(3):
        left, right = unpack([x3_recv[0, piece, comp] for piece in range(GROUP)])
        for row in range(ROWS):
            smoothed[comp, row] += scalar(LEFT + row) * left + scalar(RIGHT + row) * right
    along_z = depth_apply(smoothed[...].reshape(96, 256), 0)
    for comp in range(3):
        for row in range(ROWS):
            start = (comp * ROWS + row) * 8
            feats[row, 24 + 8 * comp:32 + 8 * comp, :] = along_z[start:start + 8]
    plane_rows_wait(0)
    for comp in range(3):
        left, right = unpack([
            own_block(0, x3_recv[0, piece, comp]) + from_plane(0, piece, comp) for piece in range(GROUP)
        ])
        for row in range(ROWS):
            feats[row, 8 * comp:8 * comp + 8, :] += scalar(LEFT + row) * left + scalar(RIGHT + row) * right

    def outward(row):
        parts = [STEP_SIZE * cot[comp, row] for comp in range(3)]
        return jnp.concatenate(parts + [jnp.zeros((8, 256), F32)], axis=0)

    def closure(row, carry):
        feature_high, feature_low = split(feats[row])
        rhs[0:48, :] = feature_high
        rhs[48:96, :] = feature_low
        rhs[96:144, :] = feature_high
        out_high, out_low = split(outward(row))
        rhs[144:176, :] = out_high
        rhs[176:208, :] = out_low
        rhs[208:240, :] = out_high
        rhs[240:256, :] = jnp.ones((16, 256), BF16)
        hidden = jnp.tanh(matmul(left_lhs[0:512, :], rhs[...]))
        grad_pre = matmul(left_lhs[512:1024, :], rhs[...]) * (1.0 - hidden * hidden)
        pre_high, pre_low = split(grad_pre)
        hidden_buf[row] = hidden
        pre_buf[row, 0] = pre_high
        pre_buf[row, 1] = pre_low
        both = matmul(back_lhs[...], pre_high)
        gfeats[row] = both[0:48] + both[48:96] + matmul(back_lhs[0:48, :], pre_low)
        return carry

    lax.fori_loop(0, ROWS, closure, 0)

    def grad_along_y(comp, row):
        return gfeats[row, 8 * comp:8 * comp + 8, :]

    back_in = jnp.concatenate(
        [gfeats[row, 24 + 8 * comp:32 + 8 * comp, :] for comp in range(3) for row in range(ROWS)], axis=0
    )
    along_z = depth_apply(back_in, 1)
    for comp in range(3):
        left_y, right_y = states([grad_along_y(comp, row) for row in range(ROWS)])
        starts = [(comp * ROWS + row) * 8 for row in range(ROWS)]
        left_z, right_z = states([along_z[start:start + 8] for start in starts])
        for piece in range(GROUP):
            tile = pack(left_y, right_y, piece)
            x1_send[1, piece, comp] = own_block(1, tile) + pack(left_z, right_z, piece)
            project(1, piece, comp, tile)
        for row in range(ROWS):
            pulled[comp, row] = along_z[starts[row]:starts[row] + 8]
    pieces_send(x1_send, x1_recv, x1_ss, x1_rs, 1)
    plane_rows_send(1)
    line_send(grad_along_y, 1)
    x1_recv[1, member] = x1_send[1, member]

    def keep_pulled(comp, row, value):
        pulled[comp, row] = value

    line_local(grad_along_y, 1, lambda comp, row, value: keep_pulled(comp, row, pulled[comp, row] + value))

    def forces_and_sums(row, carry):
        hidden_high, hidden_low = split(hidden_buf[row])
        both = matmul(force_lhs[...], hidden_high)
        forcing = both[0:32] + both[32:64] + matmul(force_lhs[0:32, :], hidden_low)
        for comp in range(3):
            nvel[comp, row] = vel[comp, row] + STEP_SIZE * forcing[8 * comp:8 * comp + 8]
        feature_high, feature_low = split(feats[row])
        ones = jnp.ones((16, 256), BF16)
        both = matmul_nt(jnp.concatenate([feature_high, ones, feature_low], axis=0), pre_buf[row, 0])
        rest = matmul_nt(jnp.concatenate([feature_high, ones], axis=0), pre_buf[row, 1])
        sums[0:48, :] += both[0:48] + both[64:112] + rest[0:48]
        sums[48:56, :] += both[48:56] + rest[48:56]
        out_high, out_low = split(outward(row))
        both = matmul_nt(jnp.concatenate([out_high, out_low], axis=0), hidden_high)
        rest = matmul_nt(out_high, hidden_low)
        sums[56:88, :] += both[0:32] + both[32:64] + rest
        return carry

    def partial_sums():
        sums[...] = jnp.zeros((88, 512), F32)
        lax.fori_loop(0, ROWS, forces_and_sums, 0)
        same = lax.bitwise_and(iota((88, 512), 0), 7) == lax.bitwise_and(iota((88, 512), 1), 7)
        gather = ones_where(lax.shift_right_logical(iota((512, UNITS), 0), 3) == iota((512, UNITS), 1)).astype(BF16)
        high, low = split(jnp.where(same, sums[...], 0.0))
        narrow = matmul(high, gather) + matmul(low, gather)
        folded = [jnp.sum(narrow[8 * part:8 * part + 8], axis=0, keepdims=True) for part in range(11)]
        front = jnp.concatenate(folded[0:8], axis=0)
        back = jnp.concatenate(folded[8:11] + [jnp.zeros((5, UNITS), F32)], axis=0)
        p1[gy] = jnp.concatenate([front, back], axis=1)
        for step in range(1, LINE):
            other = in_line(step)
            send(p1.at[gy], p1.at[gy], p1_ss.at[other], p1_rs.at[gy], line_device(other))

    def sum_line():
        for step in range(1, LINE):
            other = in_line(step)
            remote(p1.at[other], p1.at[other], p1_ss.at[other], p1_rs.at[other], line_device(other)).wait_recv()
        total = p1[0]
        for other in range(1, LINE):
            total = total + p1[other]
        p2[member] = total
        for step in range(1, GROUP):
            other = in_group(step)
            send(p2.at[member], p2.at[member], p2_ss.at[other], p2_rs.at[member], group_device(other))

    def sum_group():
        for step in range(1, GROUP):
            other = in_group(step)
            remote(p2.at[other], p2.at[other], p2_ss.at[other], p2_rs.at[other], group_device(other)).wait_recv()
        total = p2[0]
        for other in range(1, GROUP):
            total = total + p2[other]
        p3[ring] = total
        for step in (8, 7, 9, 6, 10, 5, 11, 4, 12, 3, 13, 2, 14, 1, 15):
            other = in_ring(step)
            send(p3.at[ring], p3.at[ring], p3_ss.at[other], p3_rs.at[ring], ring_device(other))

    def sum_ring():
        for step in range(1, RING):
            other = in_ring(step)
            remote(p3.at[other], p3.at[other], p3_ss.at[other], p3_rs.at[other], ring_device(other)).wait_recv()
        total = p3[0]
        for other in range(1, RING):
            total = total + p3[other]
        totals[...] = total * (1.0 / float(256 * 64 * 256))

    stores = [
        pltpu.make_async_copy(nvel, new_velocity, local_sem.at[0]),
        pltpu.make_async_copy(gvel, grad_velocity, local_sem.at[1]),
        pltpu.make_async_copy(totals, grad_weights, local_sem.at[2]),
    ]
    partial_sums()
    stores[0].start()
    pieces_wait(x1_send, x1_recv, x1_ss, x1_rs, 1)
    plane_rows_wait(1)
    for source in range(GROUP):
        for comp in range(3):
            state[source, comp] = x1_recv[1, source, comp] + from_plane(1, source, comp)

    def second_piece(source, comp):
        return state[source, comp]

    ring_send(1, second_piece)
    line_receive(1, lambda comp, row: pulled[comp, row], keep_pulled)
    for comp in range(3):
        for row, value in enumerate(local_rows([pulled[comp, row] for row in range(ROWS)])):
            gvel[comp, row] = cot[comp, row] + value
    sum_line()
    ring_state = ring_receive(1, sum_group)
    for step in (2, 1, 3, 0):
        other = in_group(step)
        for comp in range(3):
            x3_send[1, other, comp] = back_piece(ring_state, second_piece, other, comp)
    pieces_send(x3_send, x3_recv, x3_ss, x3_rs, 1)
    x3_recv[1, member] = x3_send[1, member]
    pieces_wait(x3_send, x3_recv, x3_ss, x3_rs, 1)
    for comp in range(3):
        left, right = unpack([x3_recv[1, piece, comp] for piece in range(GROUP)])
        for row in range(ROWS):
            gvel[comp, row] += scalar(LEFT + row) * left + scalar(RIGHT + row) * right
    stores[1].start()
    sum_ring()
    stores[2].start()
    plane_rows_drain(0)
    plane_rows_drain(1)
    for copy in sent:
        copy.wait_send()
    for store in stores:
        store.wait()


def finish(new_velocity_in, grad_velocity_in, grads, new_velocity, grad_velocity, grad_in, grad_bias, grad_out_t):
    new_velocity[...] = new_velocity_in[...]
    grad_velocity[...] = grad_velocity_in[...]
    front = grads[:, 0:UNITS]
    grad_in[...] = front[0:6]
    grad_bias[...] = front[6:7]
    grad_out_t[0:1] = front[7:8]
    grad_out_t[1:3] = grads[0:2, UNITS:2 * UNITS]


def local(velocity, cotangent, weight_in, bias_in, weight_out):
    field = velocity.shape
    dma = pltpu.SemaphoreType.DMA
    anywhere = pl.BlockSpec(memory_space=pl.ANY)
    whole = pl.BlockSpec(memory_space=pltpu.VMEM)
    mid = pl.pallas_call(
        kernel,
        out_shape=(
            jax.ShapeDtypeStruct(field, F32),
            jax.ShapeDtypeStruct(field, F32),
            jax.ShapeDtypeStruct((8, 128), F32),
        ),
        in_specs=[anywhere] * 8,
        out_specs=(anywhere, anywhere, anywhere),
        scratch_shapes=[
            pltpu.VMEM((6, UNITS), F32),
            pltpu.VMEM((1, UNITS), F32),
            pltpu.VMEM((3, UNITS), F32),
            pltpu.VMEM(field, F32),
            pltpu.VMEM(field, F32),
            pltpu.VMEM(field, F32),
            pltpu.VMEM(field, F32),
            pltpu.VMEM((ROWS, 48, 256), F32),
            pltpu.VMEM((ROWS, 48, 256), F32),
            pltpu.VMEM(field, F32),
            pltpu.VMEM(field, F32),
            pltpu.VMEM(field, F32),
            pltpu.SMEM((1, 128), F32),
            pltpu.VMEM((8, 128), F32),
            pltpu.VMEM((50, 8, 128), F32),
            pltpu.VMEM((4, 256, 256), BF16),
            pltpu.VMEM((1024, 256), BF16),
            pltpu.VMEM((96, 512), BF16),
            pltpu.VMEM((64, 512), BF16),
            pltpu.VMEM((256, 256), BF16),
            pltpu.VMEM((ROWS, 512, 256), F32),
            pltpu.VMEM((ROWS, 2, 512, 256), BF16),
            pltpu.VMEM((88, 512), F32),
            pltpu.VMEM((8, 128), F32),
            pltpu.VMEM((2, GROUP, 3, 8, 128), F32),
            pltpu.VMEM((2, GROUP, 3, 8, 128), F32),
            pltpu.VMEM((GROUP, 3, 8, 128), F32),
            pltpu.VMEM((2, 2, 3, 4, 128), F32),
            pltpu.VMEM((2, RING, 3, 4, 128), F32),
            pltpu.VMEM((2, GROUP, 3, 8, 128), F32),
            pltpu.VMEM((2, GROUP, 3, 8, 128), F32),
            pltpu.VMEM((2, GROUP, 4, 3, 128), F32),
            pltpu.VMEM((2, GROUP, LINE - 1, 3, 128), F32),
            pltpu.VMEM((2, GROUP, 2, 3, 128), F32),
            pltpu.VMEM((2, 4, 3, ROWS, 256), F32),
            pltpu.VMEM((2, LINE - 1, 3, ROWS, 256), F32),
            pltpu.VMEM((2, 2, 3, ROWS, 256), F32),
            pltpu.VMEM((LINE, 8, 128), F32),
            pltpu.VMEM((GROUP, 8, 128), F32),
            pltpu.VMEM((RING, 8, 128), F32),
            pltpu.SemaphoreType.REGULAR((2,)),
            dma((8,)),
            dma((2, GROUP)), dma((2, GROUP)),
            dma((2, RING)), dma((2, RING)),
            dma((2, GROUP)), dma((2, GROUP)),
            dma((2,)), dma((2,)), dma((2,)), dma((2,)),
            dma((2, LINE - 1)), dma((2, LINE - 1)),
            dma((2, 2)), dma((2, 2)),
            dma((LINE,)), dma((LINE,)),
            dma((GROUP,)), dma((GROUP,)),
            dma((RING,)), dma((RING,)),
        ],
        compiler_params=pltpu.CompilerParams(collective_id=0, has_side_effects=True),
        name="closure_step",
    )(
        velocity, cotangent, weight_in, bias_in.reshape(1, UNITS), weight_out.T,
        jnp.asarray(smoothing_table()).reshape(GROUP * RING, 1, 128), jnp.asarray(line_table()),
        jnp.asarray(depth_table(field[3])),
    )
    outs = pl.pallas_call(
        finish,
        out_shape=(
            jax.ShapeDtypeStruct(field, F32),
            jax.ShapeDtypeStruct(field, F32),
            jax.ShapeDtypeStruct((6, UNITS), F32),
            jax.ShapeDtypeStruct((1, UNITS), F32),
            jax.ShapeDtypeStruct((3, UNITS), F32),
        ),
        in_specs=[whole] * 3,
        out_specs=(whole,) * 5,
        name="finish",
    )(*mid)
    return outs[0], outs[1], outs[2], outs[3].reshape(UNITS), outs[4].T


def solution(mesh):
    in_specs = (P(None, "gx", "gy", None), P(None, "gx", "gy", None), P(), P(), P())
    out_specs = (P(None, "gx", "gy", None), P(None, "gx", "gy", None), P(), P(), P())
    return jax.shard_map(local, mesh=mesh, in_specs=in_specs, out_specs=out_specs, check_vma=False)
```

```python
import functools

import jax
import jax.numpy as jnp
import ml_dtypes
import numpy as np
from jax import lax
from jax.experimental import pallas as pl
from jax.experimental.pallas import tpu as pltpu
from jax.sharding import PartitionSpec as P

FILTER_ALPHA = 0.499
FILTER_GAIN = 0.5 + FILTER_ALPHA
COMPACT_ALPHA = 1.0 / 3.0
STEP_SIZE = 0.5
MESH = pl.DeviceIdType.MESH
F32 = jnp.float32
BF16 = jnp.bfloat16

GROUP = 4
RING = 16
LINE = 8
ROWS = 4
UNITS = 64
RESERVED = 66300000

UP_W, DOWN_W, UP_C, DOWN_C, RING_L, RING_R, BACK_L, BACK_R, LOCAL, LEFT, RIGHT = (
    0, 4, 8, 12, 16, 32, 48, 68, 88, 104, 108
)


def tridiagonal(length, coupling):
    return np.eye(length) + coupling * (np.eye(length, k=1) + np.eye(length, k=-1))


def smoothing_table():
    devices = GROUP * RING
    length = devices * ROWS
    matrix = tridiagonal(length, FILTER_ALPHA)
    inverse = np.linalg.inv(matrix)
    smoothing = np.linalg.solve(matrix, FILTER_GAIN * tridiagonal(length, 0.5))

    def move(row, pivot):
        return inverse[row, pivot] / inverse[pivot, pivot]

    table = np.zeros((devices, 128))
    block = GROUP * ROWS
    for device in range(devices):
        ring, member = divmod(device, GROUP)
        first = device * ROWS
        last = first + ROWS - 1
        entry = table[device]
        if device < devices - 1:
            entry[UP_W:UP_W + ROWS] = smoothing[last + 1, first:first + ROWS]
        if device > 0:
            entry[DOWN_W:DOWN_W + ROWS] = smoothing[first - 1, first:first + ROWS]
        group_first = ring * block
        group_last = group_first + block - 1
        for other in range(GROUP):
            start = group_first + other * ROWS
            if ring < RING - 1:
                entry[UP_C + other] = move(group_last + 1, start + ROWS)
            if ring > 0:
                entry[DOWN_C + other] = move(group_first - 1, start - 1)
        for other in range(RING):
            if other < ring:
                entry[RING_L + other] = move(group_first, (other + 1) * block)
            if other > ring:
                entry[RING_R + other] = move(group_last, other * block - 1)
        for target in range(GROUP):
            own_first = group_first + target * ROWS
            own_last = own_first + ROWS - 1
            entry[BACK_L + 5 * target] = move(own_first, group_first)
            entry[BACK_R + 5 * target] = move(own_last, group_last)
            for other in range(GROUP):
                start = group_first + other * ROWS
                if other < target:
                    entry[BACK_L + 5 * target + 1 + other] = move(own_first, start + ROWS)
                if other > target:
                    entry[BACK_R + 5 * target + 1 + other] = move(own_last, start - 1)
        entry[LOCAL:LOCAL + ROWS * ROWS] = smoothing[first:last + 1, first:last + 1].reshape(-1)
        for row in range(ROWS):
            entry[LEFT + row] = move(first + row, first)
            entry[RIGHT + row] = move(first + row, last)
    return table.astype(np.float32)


def derivative_matrix(length):
    right = 7.0 / 9.0 * (np.eye(length, k=1) - np.eye(length, k=-1)) + 1.0 / 36.0 * (
        np.eye(length, k=2) - np.eye(length, k=-2)
    )
    return np.linalg.solve(tridiagonal(length, COMPACT_ALPHA), right)


def line_table():
    size = 8
    length = LINE * size
    forward = derivative_matrix(length)
    table = np.zeros((LINE, size, 128))
    for place, matrix in enumerate((forward, forward.T)):
        base = 24 * place
        for device in range(LINE):
            rows = slice(device * size, device * size + size)
            table[device, :, base:base + 8] = matrix[rows, rows]
            if device < LINE - 1:
                table[device, 0, base + 8:base + 16] = matrix[device * size + 8, rows]
                table[device, 1, base + 8:base + 16] = matrix[device * size + 9, rows]
            if device > 0:
                table[device, 2, base + 8:base + 16] = matrix[device * size - 1, rows]
                table[device, 3, base + 8:base + 16] = matrix[device * size - 2, rows]
            for step in range(1, LINE):
                source = (device - step) % LINE
                columns = slice(source * size, source * size + size)
                pivot = source * size + 9 if source < device else source * size - 2
                sent = matrix[pivot, columns]
                factors = matrix[rows, columns] @ sent / (sent @ sent)
                if source == device - 1:
                    factors[0] = 0.0
                if source == device + 1:
                    factors[size - 1] = 0.0
                table[device, :, base + 16 + step] = factors
    table[1:, 0, 48] = 1.0
    table[:-1, size - 1, 49] = 1.0
    return table.astype(np.float32)


def split_table(matrix):
    high = matrix.astype(np.float32).astype(ml_dtypes.bfloat16)
    low = (matrix - high.astype(np.float64)).astype(np.float32).astype(ml_dtypes.bfloat16)
    return [high, low]


def depth_table(length):
    matrix = derivative_matrix(length)
    return np.stack(split_table(matrix.T.copy()) + split_table(matrix))


def split(values):
    high = values.astype(BF16)
    return high, (values - high.astype(F32)).astype(BF16)


def iota(shape, dim):
    return lax.broadcasted_iota(jnp.int32, shape, dim)


def ones_where(condition):
    return jnp.where(condition, 1.0, 0.0).astype(F32)


def matmul(a, b):
    return jnp.dot(a, b, preferred_element_type=F32)


def matmul_nt(a, b, precision=None):
    return lax.dot_general(a, b, (((1,), (1,)), ((), ())), precision=precision, preferred_element_type=F32)


def kernel(
    velocity, cotangent, weight_in, bias_in, weight_out, x_table, y_table, z_table,
    new_velocity, grad_velocity, grad_weights,
    w_in, w_bias, w_out, vel, cot, along_y, smoothed, feats, gfeats, pulled,
    scalars, columns, tall, ztab,
    left_lhs, back_lhs, force_lhs, rhs, hidden_buf, pre_buf, sums,
    x1_send, x1_recv, state, x2_send, x2_recv, x3_send, x3_recv, plane_send, plane_recv, plane_edge,
    y_send, y_recv, y_edge,
    p1, p2, p3,
    token, local_sem, x1_ss, x1_rs, x2_ss, x2_rs, x3_ss, x3_rs, plane_ss, plane_rs, edge_ss, edge_rs,
    y_ss, y_rs, ye_ss, ye_rs,
    p1_ss, p1_rs, p2_ss, p2_rs, p3_ss, p3_rs,
):
    gx = lax.axis_index("gx")
    gy = lax.axis_index("gy")
    ring = lax.div(gx, GROUP)
    member = lax.rem(gx, GROUP)

    def in_group(step):
        return lax.rem(member + step, GROUP)

    def in_ring(step):
        return lax.rem(ring + step, RING)

    def in_line(step):
        return lax.rem(gy + step, LINE)

    def group_device(other):
        return (ring * GROUP + other, gy)

    def ring_device(other):
        return (other * GROUP + member, gy)

    def line_device(other):
        return (gx, other)

    def plane_device(other, place):
        return (ring * GROUP + other, place)

    barrier = pltpu.get_barrier_semaphore()
    half = RING // 4
    near = list(range(1, half + 1)) + list(range(RING - half, RING))
    partners = (
        [ring_device(in_ring(step)) for step in near]
        + [
            plane_device(in_group(step), in_line(along))
            for step in range(GROUP) for along in range(LINE) if step or along
        ]
    )
    for partner in partners:
        pl.semaphore_signal(barrier, inc=1, device_id=partner, device_id_type=MESH)

    loads = [
        pltpu.make_async_copy(x_table.at[gx], scalars, local_sem.at[0]),
        pltpu.make_async_copy(velocity, vel, local_sem.at[1]),
        pltpu.make_async_copy(y_table.at[gy], columns, local_sem.at[2]),
        pltpu.make_async_copy(weight_in, w_in, local_sem.at[3]),
        pltpu.make_async_copy(bias_in, w_bias, local_sem.at[4]),
        pltpu.make_async_copy(weight_out, w_out, local_sem.at[5]),
        pltpu.make_async_copy(cotangent, cot, local_sem.at[6]),
        pltpu.make_async_copy(z_table, ztab, local_sem.at[7]),
    ]
    for load in loads:
        load.start()

    def remote(src, dst, send_sem, recv_sem, device):
        return pltpu.make_async_remote_copy(
            src_ref=src, dst_ref=dst, send_sem=send_sem, recv_sem=recv_sem, device_id=device, device_id_type=MESH
        )

    sent = []

    def send(*args, drain=True):
        copy = remote(*args)
        copy.start()
        if drain:
            sent.append(copy)

    def scalar(index):
        return scalars[0, index]

    def build_weights():
        for load in loads[3:6]:
            load.wait()
        w_high, w_low = split(w_in[...])
        spread = ones_where(lax.shift_right_logical(iota((512, UNITS), 0), 3) == iota((512, UNITS), 1)).astype(BF16)
        spread_t = ones_where(iota((UNITS, 512), 0) == lax.shift_right_logical(iota((UNITS, 512), 1), 3)).astype(BF16)
        bias = w_bias[...]
        b_high, b_low = split(bias)
        b_rest = bias - b_high.astype(F32) - b_low.astype(F32)
        row = iota((8, 256), 0)
        col = iota((8, 256), 1)
        field = lax.shift_right_logical(col, 3)
        pick_high = ones_where(((field == row) | (field == row + 6)) & (row < 6)).astype(BF16)
        pick_low = ones_where((field == row + 12) & (row < 6)).astype(BF16)
        spread_high = matmul_nt(spread, w_high).astype(BF16)
        spread_low = matmul_nt(spread, w_low).astype(BF16)
        top = matmul(spread_high, pick_high[0:6]) + matmul(spread_low, pick_low[0:6])
        same = lax.bitwise_and(iota((512, 256), 0), 7) == lax.bitwise_and(iota((512, 256), 1), 7)
        top = jnp.where(same, top, 0.0)
        biases = jnp.concatenate([b_high.astype(F32), b_low.astype(F32), b_rest, jnp.zeros((5, UNITS), F32)], axis=0)
        spread_bias = matmul_nt(spread, biases.astype(BF16)).astype(BF16)
        top = top + matmul(spread_bias, ones_where(col == row + 240).astype(BF16))
        left_lhs[0:512, :] = top.astype(BF16)
        o_high, o_low = split(w_out[...])
        pick_high = ones_where(((field == row + 18) | (field == row + 22)) & (row < 3)).astype(BF16)
        pick_low = ones_where((field == row + 26) & (row < 3)).astype(BF16)
        spread_oh = matmul_nt(spread, o_high).astype(BF16)
        spread_ol = matmul_nt(spread, o_low).astype(BF16)
        bottom = matmul(spread_oh, pick_high[0:3]) + matmul(spread_ol, pick_low[0:3])
        left_lhs[512:1024, :] = jnp.where(same, bottom, 0.0).astype(BF16)

        same_t = lax.bitwise_and(iota((96, 512), 0), 7) == lax.bitwise_and(iota((96, 512), 1), 7)
        row = lax.shift_right_logical(iota((96, 8), 0), 3)
        col = iota((96, 8), 1)
        get_high = ones_where((row == col) & (col < 6)).astype(BF16)
        get_low = ones_where((row == col + 6) & (col < 6)).astype(BF16)
        tall_w = matmul(get_high[:, 0:6], w_high) + matmul(get_low[:, 0:6], w_low)
        back_lhs[...] = jnp.where(same_t, matmul(tall_w.astype(BF16), spread_t), 0.0).astype(BF16)
        get_high = ones_where((row[0:64] == col[0:64]) & (col[0:64] < 3)).astype(BF16)
        get_low = ones_where((row[0:64] == col[0:64] + 4) & (col[0:64] < 3)).astype(BF16)
        tall_o = matmul(get_high[:, 0:3], o_high) + matmul(get_low[:, 0:3], o_low)
        force_lhs[...] = jnp.where(same_t[0:64], matmul(tall_o.astype(BF16), spread_t), 0.0).astype(BF16)

    def build_columns():
        loads[2].wait()
        line_columns = columns[...]
        for index in range(50):
            tall[index] = jnp.broadcast_to(line_columns[:, index:index + 1], (8, 128))

    def tall_column(index):
        half = tall[index]
        return jnp.concatenate([half, half], axis=1)

    lower = iota((8, 128), 1) < 64

    def turn(tile):
        return pltpu.roll(tile, 64, 1)

    def pack(left, right, piece):
        lanes = slice(128 * (piece // 2), 128 * (piece // 2) + 128)
        if piece % 2 == 0:
            return jnp.where(lower, left[:, lanes], turn(right[:, lanes]))
        return jnp.where(lower, turn(left[:, lanes]), right[:, lanes])

    def unpack(pieces):
        left = [jnp.where(lower, pieces[2 * t], turn(pieces[2 * t + 1])) for t in range(2)]
        right = [jnp.where(lower, turn(pieces[2 * t]), pieces[2 * t + 1]) for t in range(2)]
        return jnp.concatenate(left, axis=1), jnp.concatenate(right, axis=1)

    def two_scalars(left_index, right_index):
        return jnp.where(lower, scalar(left_index), scalar(right_index))

    def states(rows):
        return [sum(scalar(base + row) * rows[row] for row in range(ROWS)) for base in (UP_W, DOWN_W)]

    def local_rows(rows):
        return [
            sum(scalar(LOCAL + ROWS * row + col) * rows[col] for col in range(ROWS)) for row in range(ROWS)
        ]

    def pieces_send(source, target, send_sems, recv_sems, order):
        for step in (2, 1, 3):
            other = in_group(step)
            send(
                source.at[order, other], target.at[order, member],
                send_sems.at[order, other], recv_sems.at[order, member], group_device(other),
            )

    def pieces_wait(source, target, send_sems, recv_sems, order):
        for step in range(1, GROUP):
            other = in_group(step)
            remote(
                source.at[order, other], target.at[order, other],
                send_sems.at[order, other], recv_sems.at[order, other], group_device(other),
            ).wait_recv()

    def ring_send(order, load):
        gathered = []
        for comp in range(3):
            gathered.append(sum(
                two_scalars(UP_C + other, DOWN_C + other) * load(other, comp) for other in range(GROUP)
            ))
        first, second, third = gathered
        turned = turn(third)
        front = jnp.where(lower, first, turn(second))
        x2_send[order, 0, 0] = front[0:4]
        x2_send[order, 0, 1] = front[4:8]
        x2_send[order, 0, 2] = jnp.where(lower[0:4], third[0:4], turned[4:8])
        front = jnp.where(lower, turn(first), second)
        x2_send[order, 1, 0] = front[0:4]
        x2_send[order, 1, 1] = front[4:8]
        x2_send[order, 1, 2] = jnp.where(lower[0:4], turned[0:4], third[4:8])
        for step in (8, 7, 9, 6, 10, 5, 11, 4, 12, 3, 13, 2, 14, 1, 15):
            other = in_ring(step)
            kind = jnp.where(other > ring, 0, 1)
            send(
                x2_send.at[order, kind], x2_recv.at[order, ring],
                x2_ss.at[order, other], x2_rs.at[order, ring], ring_device(other),
            )

    def ring_receive(order):
        left = jnp.zeros((3, 4, 128), F32)
        right = jnp.zeros((3, 4, 128), F32)
        for step in (1, 15, 2, 14, 3, 13, 4, 12, 5, 11, 6, 10, 7, 9, 8):
            other = in_ring(step)
            remote(
                x2_send.at[order, 0], x2_recv.at[order, other],
                x2_ss.at[order, other], x2_rs.at[order, other], ring_device(other),
            ).wait_recv()
            part = x2_recv[order, other]
            left = left + scalar(RING_L + other) * part
            right = right + scalar(RING_R + other) * part
        front_left = jnp.concatenate([left[0], left[1]], axis=0)
        front_right = jnp.concatenate([right[0], right[1]], axis=0)
        back_left = jnp.concatenate([left[2], pltpu.roll(left[2], 64, 1)], axis=0)
        back_right = jnp.concatenate([pltpu.roll(right[2], 64, 1), right[2]], axis=0)
        return [
            jnp.where(lower, front_left, turn(front_right)),
            jnp.where(lower, turn(front_left), front_right),
            jnp.where(lower, back_left, back_right),
        ]

    def back_piece(ring_state, load, other, comp):
        total = two_scalars(BACK_L + 5 * other, BACK_R + 5 * other) * ring_state[comp]
        for source in range(GROUP):
            index = 5 * other + 1 + source
            total = total + two_scalars(BACK_L + index, BACK_R + index) * load(source, comp)
        return total

    def project(order, other, comp, tile):
        out = sum(tall[24 * order + 8 + col] * tile[col:col + 1] for col in range(8))
        for kind in range(4):
            plane_send[order, other, kind, comp:comp + 1, :] = out[kind:kind + 1]

    def plane_rows_send(order):
        for step in (2, 1, 3, 0):
            other = in_group(step)
            for along in (4, 5, 3, 6, 2, 7, 1):
                place = in_line(along)
                kind = jnp.where(place > gy, 1, 3)
                send(
                    plane_send.at[order, other, kind], plane_recv.at[order, member, along - 1],
                    plane_ss.at[order], plane_rs.at[order], plane_device(other, place), drain=False,
                )
            for kind, along in ((0, 1), (1, LINE - 1)):
                send(
                    plane_send.at[order, other, 2 * kind], plane_edge.at[order, member, kind],
                    edge_ss.at[order], edge_rs.at[order], plane_device(other, in_line(along)), drain=False,
                )

    def plane_rows_all(order):
        device = plane_device(in_group(1), in_line(1))
        return (
            remote(plane_recv.at[order], plane_recv.at[order], plane_ss.at[order], plane_rs.at[order], device),
            remote(plane_edge.at[order], plane_edge.at[order], edge_ss.at[order], edge_rs.at[order], device),
        )

    def plane_rows_wait(order):
        for copy in plane_rows_all(order):
            copy.wait_recv()

    def plane_rows_drain(order):
        for copy in plane_rows_all(order):
            copy.wait_send()

    def from_plane(order, source, comp):
        total = tall[48] * plane_edge[order, source, 0, comp:comp + 1, :]
        total = total + tall[49] * plane_edge[order, source, 1, comp:comp + 1, :]
        for along in range(1, LINE):
            total = total + tall[24 * order + 16 + along] * plane_recv[order, source, along - 1, comp:comp + 1, :]
        return total

    def own_block(order, tile):
        return sum(tall[24 * order + col] * tile[col:col + 1] for col in range(8))

    def line_send(load, order):
        base = 24 * order
        sent_columns = [tall_column(base + 8 + col) for col in range(8)]
        for comp in range(3):
            for row in range(ROWS):
                tile = load(comp, row)
                out = sum(sent_columns[col] * tile[col:col + 1] for col in range(8))
                for kind in range(4):
                    y_send[order, kind, comp, row:row + 1, :] = out[kind:kind + 1]
        for kind, step in ((0, 1), (1, LINE - 1)):
            send(
                y_send.at[order, 2 * kind], y_edge.at[order, kind],
                ye_ss.at[order, kind], ye_rs.at[order, kind], line_device(in_line(step)),
            )
        for step in (4, 5, 3, 2, 6, 1, 7):
            other = in_line(step)
            kind = jnp.where(other > gy, 1, 3)
            send(
                y_send.at[order, kind], y_recv.at[order, step - 1],
                y_ss.at[order, step - 1], y_rs.at[order, step - 1], line_device(other),
            )

    def line_local(load, order, store):
        base = 24 * order
        local_columns = [tall_column(base + col) for col in range(8)]
        for comp in range(3):
            for row in range(ROWS):
                tile = load(comp, row)
                store(comp, row, sum(local_columns[col] * tile[col:col + 1] for col in range(8)))

    def line_receive(order, load, store):
        base = 24 * order
        for kind, step in ((0, LINE - 1), (1, 1)):
            remote(
                y_send.at[order, 0], y_edge.at[order, kind],
                ye_ss.at[order, kind], ye_rs.at[order, kind], line_device(in_line(step)),
            ).wait_recv()
        for step in range(1, LINE):
            remote(
                y_send.at[order, 1], y_recv.at[order, step - 1],
                y_ss.at[order, step - 1], y_rs.at[order, step - 1], line_device(in_line(step)),
            ).wait_recv()
        factors = [tall_column(base + 16 + step) for step in range(1, LINE)]
        first = tall_column(48)
        last = tall_column(49)
        for comp in range(3):
            for row in range(ROWS):
                total = load(comp, row)
                total = total + first * y_edge[order, 0, comp, row:row + 1, :]
                total = total + last * y_edge[order, 1, comp, row:row + 1, :]
                for step in range(1, LINE):
                    total = total + factors[step - 1] * y_recv[order, step - 1, comp, row:row + 1, :]
                store(comp, row, total)

    def depth_apply(values, order):
        high, low = split(values)
        both = matmul(jnp.concatenate([high, low], axis=0), ztab[2 * order])
        count = values.shape[0]
        return both[0:count] + both[count:2 * count] + matmul(high, ztab[2 * order + 1])

    def pass_tokens():
        pl.semaphore_wait(barrier, len(partners))
        for kind, step in ((0, half), (1, RING - half)):
            pl.semaphore_signal(
                token.at[kind], inc=1, device_id=ring_device(in_ring(step)), device_id_type=MESH
            )

    def wait_tokens():
        for kind in range(2):
            pl.semaphore_wait(token.at[kind], 1)

    loads[0].wait()
    loads[1].wait()
    for comp in range(3):
        left, right = states([vel[comp, row] for row in range(ROWS)])
        for piece in range(GROUP):
            x1_send[0, piece, comp] = pack(left, right, piece)
    build_columns()
    pass_tokens()
    pieces_send(x1_send, x1_recv, x1_ss, x1_rs, 0)
    line_send(lambda comp, row: vel[comp, row], 0)
    x1_recv[0, member] = x1_send[0, member]
    build_weights()
    for load in loads[6:]:
        load.wait()

    def keep_along(comp, row, value):
        along_y[comp, row] = value

    line_local(lambda comp, row: vel[comp, row], 0, keep_along)
    pieces_wait(x1_send, x1_recv, x1_ss, x1_rs, 0)
    wait_tokens()

    def first_piece(source, comp):
        return x1_recv[0, source, comp]

    ring_send(0, first_piece)
    line_receive(0, lambda comp, row: along_y[comp, row], keep_along)
    for comp in range(3):
        for row, value in enumerate(local_rows([vel[comp, row] for row in range(ROWS)])):
            smoothed[comp, row] = value
        for row, value in enumerate(local_rows([along_y[comp, row] for row in range(ROWS)])):
            feats[row, 8 * comp:8 * comp + 8, :] = value
    ring_state = ring_receive(0)
    for step in (2, 1, 3, 0):
        other = in_group(step)
        for comp in range(3):
            tile = back_piece(ring_state, first_piece, other, comp)
            x3_send[0, other, comp] = tile
            project(0, other, comp, tile)
    pieces_send(x3_send, x3_recv, x3_ss, x3_rs, 0)
    plane_rows_send(0)
    x3_recv[0, member] = x3_send[0, member]
    pieces_wait(x3_send, x3_recv, x3_ss, x3_rs, 0)
    for comp in range(3):
        left, right = unpack([x3_recv[0, piece, comp] for piece in range(GROUP)])
        for row in range(ROWS):
            smoothed[comp, row] += scalar(LEFT + row) * left + scalar(RIGHT + row) * right
    along_z = depth_apply(smoothed[...].reshape(96, 256), 0)
    for comp in range(3):
        for row in range(ROWS):
            start = (comp * ROWS + row) * 8
            feats[row, 24 + 8 * comp:32 + 8 * comp, :] = along_z[start:start + 8]
    plane_rows_wait(0)
    for comp in range(3):
        left, right = unpack([
            own_block(0, x3_recv[0, piece, comp]) + from_plane(0, piece, comp) for piece in range(GROUP)
        ])
        for row in range(ROWS):
            feats[row, 8 * comp:8 * comp + 8, :] += scalar(LEFT + row) * left + scalar(RIGHT + row) * right

    def outward(row):
        parts = [STEP_SIZE * cot[comp, row] for comp in range(3)]
        return jnp.concatenate(parts + [jnp.zeros((8, 256), F32)], axis=0)

    def closure(row, carry):
        feature_high, feature_low = split(feats[row])
        rhs[0:48, :] = feature_high
        rhs[48:96, :] = feature_low
        rhs[96:144, :] = feature_high
        out_high, out_low = split(outward(row))
        rhs[144:176, :] = out_high
        rhs[176:208, :] = out_low
        rhs[208:240, :] = out_high
        rhs[240:256, :] = jnp.ones((16, 256), BF16)
        hidden = jnp.tanh(matmul(left_lhs[0:512, :], rhs[...]))
        grad_pre = matmul(left_lhs[512:1024, :], rhs[...]) * (1.0 - hidden * hidden)
        pre_high, pre_low = split(grad_pre)
        hidden_buf[row] = hidden
        pre_buf[row, 0] = pre_high
        pre_buf[row, 1] = pre_low
        both = matmul(back_lhs[...], pre_high)
        gfeats[row] = both[0:48] + both[48:96] + matmul(back_lhs[0:48, :], pre_low)
        return carry

    lax.fori_loop(0, ROWS, closure, 0)

    def grad_along_y(comp, row):
        return gfeats[row, 8 * comp:8 * comp + 8, :]

    back_in = jnp.concatenate(
        [gfeats[row, 24 + 8 * comp:32 + 8 * comp, :] for comp in range(3) for row in range(ROWS)], axis=0
    )
    along_z = depth_apply(back_in, 1)
    for comp in range(3):
        left_y, right_y = states([grad_along_y(comp, row) for row in range(ROWS)])
        starts = [(comp * ROWS + row) * 8 for row in range(ROWS)]
        left_z, right_z = states([along_z[start:start + 8] for start in starts])
        for piece in range(GROUP):
            tile = pack(left_y, right_y, piece)
            x1_send[1, piece, comp] = own_block(1, tile) + pack(left_z, right_z, piece)
            project(1, piece, comp, tile)
        for row in range(ROWS):
            pulled[comp, row] = along_z[starts[row]:starts[row] + 8]
    pieces_send(x1_send, x1_recv, x1_ss, x1_rs, 1)
    plane_rows_send(1)
    x1_recv[1, member] = x1_send[1, member]

    def keep_pulled(comp, row, value):
        pulled[comp, row] = value

    def line_part():
        line_send(grad_along_y, 1)
        line_local(grad_along_y, 1, lambda comp, row, value: keep_pulled(comp, row, pulled[comp, row] + value))

    def forces(row, carry):
        hidden_high, hidden_low = split(hidden_buf[row])
        both = matmul(force_lhs[...], hidden_high)
        forcing = both[0:32] + both[32:64] + matmul(force_lhs[0:32, :], hidden_low)
        for comp in range(3):
            new_velocity[comp, row] = vel[comp, row] + STEP_SIZE * forcing[8 * comp:8 * comp + 8]
        return carry

    def row_sums(row, carry):
        hidden_high, hidden_low = split(hidden_buf[row])
        feature_high, feature_low = split(feats[row])
        ones = jnp.ones((16, 256), BF16)
        both = matmul_nt(jnp.concatenate([feature_high, ones, feature_low], axis=0), pre_buf[row, 0])
        rest = matmul_nt(jnp.concatenate([feature_high, ones], axis=0), pre_buf[row, 1])
        sums[0:48, :] += both[0:48] + both[64:112] + rest[0:48]
        sums[48:56, :] += both[48:56] + rest[48:56]
        out_high, out_low = split(outward(row))
        both = matmul_nt(jnp.concatenate([out_high, out_low], axis=0), hidden_high)
        rest = matmul_nt(out_high, hidden_low)
        sums[56:88, :] += both[0:32] + both[32:64] + rest
        return carry

    def partial_sums():
        sums[...] = jnp.zeros((88, 512), F32)
        lax.fori_loop(0, ROWS, row_sums, 0)
        same = lax.bitwise_and(iota((88, 512), 0), 7) == lax.bitwise_and(iota((88, 512), 1), 7)
        gather = ones_where(lax.shift_right_logical(iota((512, UNITS), 0), 3) == iota((512, UNITS), 1)).astype(BF16)
        high, low = split(jnp.where(same, sums[...], 0.0))
        narrow = matmul(high, gather) + matmul(low, gather)
        folded = [jnp.sum(narrow[8 * part:8 * part + 8], axis=0, keepdims=True) for part in range(11)]
        front = jnp.concatenate(folded[0:8], axis=0)
        back = jnp.concatenate(folded[8:11] + [jnp.zeros((5, UNITS), F32)], axis=0)
        p1[gy] = jnp.concatenate([front, back], axis=1)
        for step in range(1, LINE):
            other = in_line(step)
            send(p1.at[gy], p1.at[gy], p1_ss.at[other], p1_rs.at[gy], line_device(other))

    def sum_line():
        for step in range(1, LINE):
            other = in_line(step)
            remote(p1.at[other], p1.at[other], p1_ss.at[other], p1_rs.at[other], line_device(other)).wait_recv()
        total = p1[0]
        for other in range(1, LINE):
            total = total + p1[other]
        p2[member] = total
        for step in range(1, GROUP):
            other = in_group(step)
            send(p2.at[member], p2.at[member], p2_ss.at[other], p2_rs.at[member], group_device(other))

    def sum_group():
        for step in range(1, GROUP):
            other = in_group(step)
            remote(p2.at[other], p2.at[other], p2_ss.at[other], p2_rs.at[other], group_device(other)).wait_recv()
        total = p2[0]
        for other in range(1, GROUP):
            total = total + p2[other]
        p3[ring] = total
        for step in (8, 7, 9, 6, 10, 5, 11, 4, 12, 3, 13, 2, 14, 1, 15):
            other = in_ring(step)
            send(p3.at[ring], p3.at[ring], p3_ss.at[other], p3_rs.at[ring], ring_device(other))

    def sum_ring():
        for step in range(1, RING):
            other = in_ring(step)
            remote(p3.at[other], p3.at[other], p3_ss.at[other], p3_rs.at[other], ring_device(other)).wait_recv()
        total = p3[0]
        for other in range(1, RING):
            total = total + p3[other]
        grad_weights[...] = total * (1.0 / float(256 * 64 * 256))

    partial_sums()
    line_part()
    pieces_wait(x1_send, x1_recv, x1_ss, x1_rs, 1)
    plane_rows_wait(1)
    for source in range(GROUP):
        for comp in range(3):
            state[source, comp] = x1_recv[1, source, comp] + from_plane(1, source, comp)

    def second_piece(source, comp):
        return state[source, comp]

    ring_send(1, second_piece)
    sum_line()
    lax.fori_loop(0, ROWS, forces, 0)
    line_receive(1, lambda comp, row: pulled[comp, row], keep_pulled)
    for comp in range(3):
        for row, value in enumerate(local_rows([pulled[comp, row] for row in range(ROWS)])):
            grad_velocity[comp, row] = cot[comp, row] + value
    sum_group()
    ring_state = ring_receive(1)
    for step in (2, 1, 3, 0):
        other = in_group(step)
        for comp in range(3):
            x3_send[1, other, comp] = back_piece(ring_state, second_piece, other, comp)
    pieces_send(x3_send, x3_recv, x3_ss, x3_rs, 1)
    x3_recv[1, member] = x3_send[1, member]
    pieces_wait(x3_send, x3_recv, x3_ss, x3_rs, 1)
    for comp in range(3):
        left, right = unpack([x3_recv[1, piece, comp] for piece in range(GROUP)])
        for row in range(ROWS):
            grad_velocity[comp, row] += scalar(LEFT + row) * left + scalar(RIGHT + row) * right
    sum_ring()
    plane_rows_drain(0)
    plane_rows_drain(1)
    for copy in sent:
        copy.wait_send()


def finish(new_velocity_in, grad_velocity_in, grads, new_velocity, grad_velocity, grad_in, grad_bias, grad_out_t, sems):
    copies = [
        pltpu.make_async_copy(new_velocity_in, new_velocity, sems.at[0]),
        pltpu.make_async_copy(grad_velocity_in, grad_velocity, sems.at[1]),
    ]
    for copy in copies:
        copy.start()
    front = grads[:, 0:UNITS]
    grad_in[...] = front[0:6]
    grad_bias[...] = front[6:7]
    grad_out_t[0:1] = front[7:8]
    grad_out_t[1:3] = grads[0:2, UNITS:2 * UNITS]
    for copy in copies:
        copy.wait()


def local(velocity, cotangent, weight_in, bias_in, weight_out):
    field = velocity.shape
    dma = pltpu.SemaphoreType.DMA
    anywhere = pl.BlockSpec(memory_space=pl.ANY)
    whole = pl.BlockSpec(memory_space=pltpu.VMEM)
    mid = pl.pallas_call(
        kernel,
        out_shape=(
            pltpu.VMEM(field, F32),
            pltpu.VMEM(field, F32),
            pltpu.VMEM((8, 128), F32),
        ),
        in_specs=[anywhere] * 8,
        out_specs=(whole, whole, whole),
        scratch_shapes=[
            pltpu.VMEM((6, UNITS), F32),
            pltpu.VMEM((1, UNITS), F32),
            pltpu.VMEM((3, UNITS), F32),
            pltpu.VMEM(field, F32),
            pltpu.VMEM(field, F32),
            pltpu.VMEM(field, F32),
            pltpu.VMEM(field, F32),
            pltpu.VMEM((ROWS, 48, 256), F32),
            pltpu.VMEM((ROWS, 48, 256), F32),
            pltpu.VMEM(field, F32),
            pltpu.SMEM((1, 128), F32),
            pltpu.VMEM((8, 128), F32),
            pltpu.VMEM((50, 8, 128), F32),
            pltpu.VMEM((4, 256, 256), BF16),
            pltpu.VMEM((1024, 256), BF16),
            pltpu.VMEM((96, 512), BF16),
            pltpu.VMEM((64, 512), BF16),
            pltpu.VMEM((256, 256), BF16),
            pltpu.VMEM((ROWS, 512, 256), F32),
            pltpu.VMEM((ROWS, 2, 512, 256), BF16),
            pltpu.VMEM((88, 512), F32),
            pltpu.VMEM((2, GROUP, 3, 8, 128), F32),
            pltpu.VMEM((2, GROUP, 3, 8, 128), F32),
            pltpu.VMEM((GROUP, 3, 8, 128), F32),
            pltpu.VMEM((2, 2, 3, 4, 128), F32),
            pltpu.VMEM((2, RING, 3, 4, 128), F32),
            pltpu.VMEM((2, GROUP, 3, 8, 128), F32),
            pltpu.VMEM((2, GROUP, 3, 8, 128), F32),
            pltpu.VMEM((2, GROUP, 4, 3, 128), F32),
            pltpu.VMEM((2, GROUP, LINE - 1, 3, 128), F32),
            pltpu.VMEM((2, GROUP, 2, 3, 128), F32),
            pltpu.VMEM((2, 4, 3, ROWS, 256), F32),
            pltpu.VMEM((2, LINE - 1, 3, ROWS, 256), F32),
            pltpu.VMEM((2, 2, 3, ROWS, 256), F32),
            pltpu.VMEM((LINE, 8, 128), F32),
            pltpu.VMEM((GROUP, 8, 128), F32),
            pltpu.VMEM((RING, 8, 128), F32),
            pltpu.SemaphoreType.REGULAR((2,)),
            dma((8,)),
            dma((2, GROUP)), dma((2, GROUP)),
            dma((2, RING)), dma((2, RING)),
            dma((2, GROUP)), dma((2, GROUP)),
            dma((2,)), dma((2,)), dma((2,)), dma((2,)),
            dma((2, LINE - 1)), dma((2, LINE - 1)),
            dma((2, 2)), dma((2, 2)),
            dma((LINE,)), dma((LINE,)),
            dma((GROUP,)), dma((GROUP,)),
            dma((RING,)), dma((RING,)),
        ],
        compiler_params=pltpu.CompilerParams(collective_id=0, has_side_effects=True, vmem_limit_bytes=RESERVED),
        name="closure_step",
    )(
        velocity, cotangent, weight_in, bias_in.reshape(1, UNITS), weight_out.T,
        jnp.asarray(smoothing_table()).reshape(GROUP * RING, 1, 128), jnp.asarray(line_table()),
        jnp.asarray(depth_table(field[3])),
    )
    outs = pl.pallas_call(
        finish,
        out_shape=(
            jax.ShapeDtypeStruct(field, F32),
            jax.ShapeDtypeStruct(field, F32),
            jax.ShapeDtypeStruct((6, UNITS), F32),
            jax.ShapeDtypeStruct((1, UNITS), F32),
            jax.ShapeDtypeStruct((3, UNITS), F32),
        ),
        in_specs=[whole] * 3,
        out_specs=(anywhere, anywhere, whole, whole, whole),
        scratch_shapes=[dma((2,))],
        compiler_params=pltpu.CompilerParams(vmem_limit_bytes=1 << 20),
        name="finish",
    )(*mid)
    return outs[0], outs[1], outs[2], outs[3].reshape(UNITS), outs[4].T


def solution(mesh):
    in_specs = (P(None, "gx", "gy", None), P(None, "gx", "gy", None), P(), P(), P())
    out_specs = (P(None, "gx", "gy", None), P(None, "gx", "gy", None), P(), P(), P())
    return jax.shard_map(local, mesh=mesh, in_specs=in_specs, out_specs=out_specs, check_vma=False)
```

```python
import functools

import jax
import jax.numpy as jnp
import ml_dtypes
import numpy as np
from jax import lax
from jax.experimental import pallas as pl
from jax.experimental.pallas import tpu as pltpu
from jax.sharding import PartitionSpec as P

FILTER_ALPHA = 0.499
FILTER_GAIN = 0.5 + FILTER_ALPHA
COMPACT_ALPHA = 1.0 / 3.0
STEP_SIZE = 0.5
MESH = pl.DeviceIdType.MESH
F32 = jnp.float32
BF16 = jnp.bfloat16

GROUP = 4
RING = 16
LINE = 8
ROWS = 4
UNITS = 64
RESERVED = 66300000

UP_W, DOWN_W, UP_C, DOWN_C, RING_L, RING_R, BACK_L, BACK_R, LOCAL, LEFT, RIGHT = (
    0, 4, 8, 12, 16, 32, 48, 68, 88, 104, 108
)


def tridiagonal(length, coupling):
    return np.eye(length) + coupling * (np.eye(length, k=1) + np.eye(length, k=-1))


def smoothing_table():
    devices = GROUP * RING
    length = devices * ROWS
    matrix = tridiagonal(length, FILTER_ALPHA)
    inverse = np.linalg.inv(matrix)
    smoothing = np.linalg.solve(matrix, FILTER_GAIN * tridiagonal(length, 0.5))

    def move(row, pivot):
        return inverse[row, pivot] / inverse[pivot, pivot]

    table = np.zeros((devices, 128))
    block = GROUP * ROWS
    for device in range(devices):
        ring, member = divmod(device, GROUP)
        first = device * ROWS
        last = first + ROWS - 1
        entry = table[device]
        if device < devices - 1:
            entry[UP_W:UP_W + ROWS] = smoothing[last + 1, first:first + ROWS]
        if device > 0:
            entry[DOWN_W:DOWN_W + ROWS] = smoothing[first - 1, first:first + ROWS]
        group_first = ring * block
        group_last = group_first + block - 1
        for other in range(GROUP):
            start = group_first + other * ROWS
            if ring < RING - 1:
                entry[UP_C + other] = move(group_last + 1, start + ROWS)
            if ring > 0:
                entry[DOWN_C + other] = move(group_first - 1, start - 1)
        for other in range(RING):
            if other < ring:
                entry[RING_L + other] = move(group_first, (other + 1) * block)
            if other > ring:
                entry[RING_R + other] = move(group_last, other * block - 1)
        for target in range(GROUP):
            own_first = group_first + target * ROWS
            own_last = own_first + ROWS - 1
            entry[BACK_L + 5 * target] = move(own_first, group_first)
            entry[BACK_R + 5 * target] = move(own_last, group_last)
            for other in range(GROUP):
                start = group_first + other * ROWS
                if other < target:
                    entry[BACK_L + 5 * target + 1 + other] = move(own_first, start + ROWS)
                if other > target:
                    entry[BACK_R + 5 * target + 1 + other] = move(own_last, start - 1)
        entry[LOCAL:LOCAL + ROWS * ROWS] = smoothing[first:last + 1, first:last + 1].reshape(-1)
        for row in range(ROWS):
            entry[LEFT + row] = move(first + row, first)
            entry[RIGHT + row] = move(first + row, last)
    return table.astype(np.float32)


def derivative_matrix(length):
    right = 7.0 / 9.0 * (np.eye(length, k=1) - np.eye(length, k=-1)) + 1.0 / 36.0 * (
        np.eye(length, k=2) - np.eye(length, k=-2)
    )
    return np.linalg.solve(tridiagonal(length, COMPACT_ALPHA), right)


def line_table():
    size = 8
    length = LINE * size
    forward = derivative_matrix(length)
    table = np.zeros((LINE, size, 128))
    for place, matrix in enumerate((forward, forward.T)):
        base = 24 * place
        for device in range(LINE):
            rows = slice(device * size, device * size + size)
            table[device, :, base:base + 8] = matrix[rows, rows]
            if device < LINE - 1:
                table[device, 0, base + 8:base + 16] = matrix[device * size + 8, rows]
                table[device, 1, base + 8:base + 16] = matrix[device * size + 9, rows]
            if device > 0:
                table[device, 2, base + 8:base + 16] = matrix[device * size - 1, rows]
                table[device, 3, base + 8:base + 16] = matrix[device * size - 2, rows]
            for step in range(1, LINE):
                source = (device - step) % LINE
                columns = slice(source * size, source * size + size)
                pivot = source * size + 9 if source < device else source * size - 2
                sent = matrix[pivot, columns]
                factors = matrix[rows, columns] @ sent / (sent @ sent)
                if source == device - 1:
                    factors[0] = 0.0
                if source == device + 1:
                    factors[size - 1] = 0.0
                table[device, :, base + 16 + step] = factors
    table[1:, 0, 48] = 1.0
    table[:-1, size - 1, 49] = 1.0
    return table.astype(np.float32)


def split_table(matrix):
    high = matrix.astype(np.float32).astype(ml_dtypes.bfloat16)
    low = (matrix - high.astype(np.float64)).astype(np.float32).astype(ml_dtypes.bfloat16)
    return [high, low]


def depth_table(length):
    matrix = derivative_matrix(length)
    return np.stack(split_table(matrix.T.copy()) + split_table(matrix))


def split(values):
    high = values.astype(BF16)
    return high, (values - high.astype(F32)).astype(BF16)


def iota(shape, dim):
    return lax.broadcasted_iota(jnp.int32, shape, dim)


def ones_where(condition):
    return jnp.where(condition, 1.0, 0.0).astype(F32)


def matmul(a, b):
    return jnp.dot(a, b, preferred_element_type=F32)


def matmul_nt(a, b, precision=None):
    return lax.dot_general(a, b, (((1,), (1,)), ((), ())), precision=precision, preferred_element_type=F32)


def kernel(
    velocity, cotangent, weight_in, bias_in, weight_out, x_table, y_table, z_table,
    new_velocity, grad_velocity, grad_weights,
    w_in, w_bias, w_out, vel, cot, along_y, smoothed, feats, gfeats, pulled,
    scalars, columns, tall, ztab,
    left_lhs, out_lhs, back_lhs, force_lhs, rhs, pulled_out, hidden_buf, pre_buf, sums,
    x1_send, x1_recv, state, x2_send, x2_recv, x3_send, x3_recv, plane_send, plane_recv, plane_edge,
    y_send, y_recv, y_edge,
    p1, p2, p3,
    token, local_sem, x1_ss, x1_rs, x2_ss, x2_rs, x3_ss, x3_rs, plane_ss, plane_rs, edge_ss, edge_rs,
    y_ss, y_rs, ye_ss, ye_rs,
    p1_ss, p1_rs, p2_ss, p2_rs, p3_ss, p3_rs,
):
    gx = lax.axis_index("gx")
    gy = lax.axis_index("gy")
    ring = lax.div(gx, GROUP)
    member = lax.rem(gx, GROUP)

    def in_group(step):
        return lax.rem(member + step, GROUP)

    def in_ring(step):
        return lax.rem(ring + step, RING)

    def in_line(step):
        return lax.rem(gy + step, LINE)

    def group_device(other):
        return (ring * GROUP + other, gy)

    def ring_device(other):
        return (other * GROUP + member, gy)

    def line_device(other):
        return (gx, other)

    def plane_device(other, place):
        return (ring * GROUP + other, place)

    barrier = pltpu.get_barrier_semaphore()
    half = RING // 4
    partners = (
        [ring_device(in_ring(step)) for step in (4, 12, 3, 13, 2, 14, 1, 15)]
        + [line_device(in_line(step)) for step in range(1, LINE)]
        + [group_device(in_group(step)) for step in range(1, GROUP)]
    )
    for partner in partners:
        pl.semaphore_signal(barrier, inc=1, device_id=partner, device_id_type=MESH)

    loads = [
        pltpu.make_async_copy(x_table.at[gx], scalars, local_sem.at[0]),
        pltpu.make_async_copy(velocity, vel, local_sem.at[1]),
        pltpu.make_async_copy(y_table.at[gy], columns, local_sem.at[2]),
        pltpu.make_async_copy(weight_in, w_in, local_sem.at[3]),
        pltpu.make_async_copy(bias_in, w_bias, local_sem.at[4]),
        pltpu.make_async_copy(weight_out, w_out, local_sem.at[5]),
        pltpu.make_async_copy(cotangent, cot, local_sem.at[6]),
        pltpu.make_async_copy(z_table, ztab, local_sem.at[7]),
    ]
    for load in loads:
        load.start()

    def remote(src, dst, send_sem, recv_sem, device):
        return pltpu.make_async_remote_copy(
            src_ref=src, dst_ref=dst, send_sem=send_sem, recv_sem=recv_sem, device_id=device, device_id_type=MESH
        )

    sent = []

    def send(*args, drain=True):
        copy = remote(*args)
        copy.start()
        if drain:
            sent.append(copy)

    def drain(count):
        for copy in sent[:count]:
            copy.wait_send()
        del sent[:count]

    def scalar(index):
        return scalars[0, index]

    def build_weights():
        for load in loads[3:6]:
            load.wait()
        w_high, w_low = split(w_in[...])
        spread = ones_where(lax.shift_right_logical(iota((512, UNITS), 0), 3) == iota((512, UNITS), 1)).astype(BF16)
        spread_t = ones_where(iota((UNITS, 512), 0) == lax.shift_right_logical(iota((UNITS, 512), 1), 3)).astype(BF16)
        bias = w_bias[...]
        b_high, b_low = split(bias)
        b_rest = bias - b_high.astype(F32) - b_low.astype(F32)
        row = iota((8, 160), 0)
        col = iota((8, 160), 1)
        field = lax.shift_right_logical(col, 3)
        pick_high = ones_where(((field == row) | (field == row + 6)) & (row < 6)).astype(BF16)
        pick_low = ones_where((field == row + 12) & (row < 6)).astype(BF16)
        spread_high = matmul_nt(spread, w_high).astype(BF16)
        spread_low = matmul_nt(spread, w_low).astype(BF16)
        top = matmul(spread_high, pick_high[0:6]) + matmul(spread_low, pick_low[0:6])
        same = lax.bitwise_and(iota((512, 160), 0), 7) == lax.bitwise_and(iota((512, 160), 1), 7)
        top = jnp.where(same, top, 0.0)
        biases = jnp.concatenate([b_high.astype(F32), b_low.astype(F32), b_rest, jnp.zeros((5, UNITS), F32)], axis=0)
        spread_bias = matmul_nt(spread, biases.astype(BF16)).astype(BF16)
        top = top + matmul(spread_bias, ones_where(col == row + 144).astype(BF16))
        left_lhs[...] = top.astype(BF16)
        o_high, o_low = split(w_out[...])
        row, field, same = row[:, 0:96], field[:, 0:96], same[:, 0:96]
        pick_high = ones_where(((field == row) | (field == row + 4)) & (row < 3)).astype(BF16)
        pick_low = ones_where((field == row + 8) & (row < 3)).astype(BF16)
        spread_oh = matmul_nt(spread, o_high).astype(BF16)
        spread_ol = matmul_nt(spread, o_low).astype(BF16)
        bottom = matmul(spread_oh, pick_high[0:3]) + matmul(spread_ol, pick_low[0:3])
        out_lhs[...] = jnp.where(same, bottom, 0.0).astype(BF16)

        same_t = lax.bitwise_and(iota((96, 512), 0), 7) == lax.bitwise_and(iota((96, 512), 1), 7)
        row = lax.shift_right_logical(iota((96, 8), 0), 3)
        col = iota((96, 8), 1)
        get_high = ones_where((row == col) & (col < 6)).astype(BF16)
        get_low = ones_where((row == col + 6) & (col < 6)).astype(BF16)
        tall_w = matmul(get_high[:, 0:6], w_high) + matmul(get_low[:, 0:6], w_low)
        back_lhs[...] = jnp.where(same_t, matmul(tall_w.astype(BF16), spread_t), 0.0).astype(BF16)
        get_high = ones_where((row[0:64] == col[0:64]) & (col[0:64] < 3)).astype(BF16)
        get_low = ones_where((row[0:64] == col[0:64] + 4) & (col[0:64] < 3)).astype(BF16)
        tall_o = matmul(get_high[:, 0:3], o_high) + matmul(get_low[:, 0:3], o_low)
        force_lhs[...] = jnp.where(same_t[0:64], matmul(tall_o.astype(BF16), spread_t), 0.0).astype(BF16)

    def build_columns():
        loads[2].wait()
        line_columns = columns[...]
        for index in range(50):
            tall[index] = jnp.broadcast_to(line_columns[:, index:index + 1], (8, 128))

    def tall_column(index):
        half = tall[index]
        return jnp.concatenate([half, half], axis=1)

    lower = iota((8, 128), 1) < 64

    def turn(tile):
        return pltpu.roll(tile, 64, 1)

    def pack(left, right, piece):
        lanes = slice(128 * (piece // 2), 128 * (piece // 2) + 128)
        if piece % 2 == 0:
            return jnp.where(lower, left[:, lanes], turn(right[:, lanes]))
        return jnp.where(lower, turn(left[:, lanes]), right[:, lanes])

    def unpack(pieces):
        left = [jnp.where(lower, pieces[2 * t], turn(pieces[2 * t + 1])) for t in range(2)]
        right = [jnp.where(lower, turn(pieces[2 * t]), pieces[2 * t + 1]) for t in range(2)]
        return jnp.concatenate(left, axis=1), jnp.concatenate(right, axis=1)

    def two_scalars(left_index, right_index):
        return jnp.where(lower, scalar(left_index), scalar(right_index))

    def states(rows):
        return [sum(scalar(base + row) * rows[row] for row in range(ROWS)) for base in (UP_W, DOWN_W)]

    def local_rows(rows):
        return [
            sum(scalar(LOCAL + ROWS * row + col) * rows[col] for col in range(ROWS)) for row in range(ROWS)
        ]

    def pieces_send(source, target, send_sems, recv_sems, order):
        for step in (2, 1, 3):
            other = in_group(step)
            send(
                source.at[order, other], target.at[order, member],
                send_sems.at[order, other], recv_sems.at[order, member], group_device(other),
            )

    def pieces_wait(source, target, send_sems, recv_sems, order):
        for step in range(1, GROUP):
            other = in_group(step)
            remote(
                source.at[order, other], target.at[order, other],
                send_sems.at[order, other], recv_sems.at[order, other], group_device(other),
            ).wait_recv()

    def ring_send(order, load):
        gathered = []
        for comp in range(3):
            gathered.append(sum(
                two_scalars(UP_C + other, DOWN_C + other) * load(other, comp) for other in range(GROUP)
            ))
        first, second, third = gathered
        turned = turn(third)
        front = jnp.where(lower, first, turn(second))
        x2_send[order, 0, 0] = front[0:4]
        x2_send[order, 0, 1] = front[4:8]
        x2_send[order, 0, 2] = jnp.where(lower[0:4], third[0:4], turned[4:8])
        front = jnp.where(lower, turn(first), second)
        x2_send[order, 1, 0] = front[0:4]
        x2_send[order, 1, 1] = front[4:8]
        x2_send[order, 1, 2] = jnp.where(lower[0:4], turned[0:4], third[4:8])
        for step in (8, 7, 9, 6, 10, 5, 11, 4, 12, 3, 13, 2, 14, 1, 15):
            other = in_ring(step)
            kind = jnp.where(other > ring, 0, 1)
            send(
                x2_send.at[order, kind], x2_recv.at[order, ring],
                x2_ss.at[order, other], x2_rs.at[order, ring], ring_device(other),
            )

    def ring_receive(order):
        left = jnp.zeros((3, 4, 128), F32)
        right = jnp.zeros((3, 4, 128), F32)
        for step in (1, 15, 2, 14, 3, 13, 4, 12, 5, 11, 6, 10, 7, 9, 8):
            other = in_ring(step)
            remote(
                x2_send.at[order, 0], x2_recv.at[order, other],
                x2_ss.at[order, other], x2_rs.at[order, other], ring_device(other),
            ).wait_recv()
            part = x2_recv[order, other]
            left = left + scalar(RING_L + other) * part
            right = right + scalar(RING_R + other) * part
        front_left = jnp.concatenate([left[0], left[1]], axis=0)
        front_right = jnp.concatenate([right[0], right[1]], axis=0)
        back_left = jnp.concatenate([left[2], pltpu.roll(left[2], 64, 1)], axis=0)
        back_right = jnp.concatenate([pltpu.roll(right[2], 64, 1), right[2]], axis=0)
        return [
            jnp.where(lower, front_left, turn(front_right)),
            jnp.where(lower, turn(front_left), front_right),
            jnp.where(lower, back_left, back_right),
        ]

    def back_piece(ring_state, load, other, comp):
        total = two_scalars(BACK_L + 5 * other, BACK_R + 5 * other) * ring_state[comp]
        for source in range(GROUP):
            index = 5 * other + 1 + source
            total = total + two_scalars(BACK_L + index, BACK_R + index) * load(source, comp)
        return total

    def project(order, other, comp, tile):
        out = sum(tall[24 * order + 8 + col] * tile[col:col + 1] for col in range(8))
        for kind in range(4):
            plane_send[order, other, kind // 2, kind % 2, comp:comp + 1, :] = out[kind:kind + 1]

    def plane_rows_send(order):
        for step in (2, 1, 3, 0):
            other = in_group(step)
            for along in (4, 5, 3, 6, 2, 7, 1):
                place = in_line(along)
                side = jnp.where(place > gy, 0, 1)
                if along in (1, LINE - 1):
                    send(
                        plane_send.at[order, other, side], plane_edge.at[order, member, 0 if along == 1 else 1],
                        edge_ss.at[order], edge_rs.at[order], plane_device(other, place), drain=False,
                    )
                else:
                    send(
                        plane_send.at[order, other, side, 1], plane_recv.at[order, member, along - 2],
                        plane_ss.at[order], plane_rs.at[order], plane_device(other, place), drain=False,
                    )

    def plane_rows_all(order):
        device = plane_device(in_group(1), in_line(1))
        return (
            remote(plane_recv.at[order], plane_recv.at[order], plane_ss.at[order], plane_rs.at[order], device),
            remote(plane_edge.at[order], plane_edge.at[order], edge_ss.at[order], edge_rs.at[order], device),
        )

    def plane_rows_wait(order):
        for copy in plane_rows_all(order):
            copy.wait_recv()

    def plane_rows_drain(order):
        for copy in plane_rows_all(order):
            copy.wait_send()

    def from_plane(order, source, comp):
        def row(ref, *index):
            return ref[(order, source) + index + (slice(comp, comp + 1),)]

        factor = 24 * order + 16
        total = tall[48] * row(plane_edge, 0, 0) + tall[factor + 1] * row(plane_edge, 0, 1)
        total = total + tall[49] * row(plane_edge, 1, 0) + tall[factor + LINE - 1] * row(plane_edge, 1, 1)
        for along in range(2, LINE - 1):
            total = total + tall[factor + along] * row(plane_recv, along - 2)
        return total

    def own_block(order, tile):
        return sum(tall[24 * order + col] * tile[col:col + 1] for col in range(8))

    def line_send(load, order):
        base = 24 * order
        sent_columns = [tall_column(base + 8 + col) for col in range(8)]
        for comp in range(3):
            for row in range(ROWS):
                tile = load(comp, row)
                out = sum(sent_columns[col] * tile[col:col + 1] for col in range(8))
                for kind in range(4):
                    y_send[order, kind, comp, row:row + 1, :] = out[kind:kind + 1]
        for kind, step in ((0, 1), (1, LINE - 1)):
            send(
                y_send.at[order, 2 * kind], y_edge.at[order, kind],
                ye_ss.at[order, kind], ye_rs.at[order, kind], line_device(in_line(step)),
            )
        for step in (4, 5, 3, 2, 6, 1, 7):
            other = in_line(step)
            kind = jnp.where(other > gy, 1, 3)
            send(
                y_send.at[order, kind], y_recv.at[order, step - 1],
                y_ss.at[order, step - 1], y_rs.at[order, step - 1], line_device(other),
            )

    def line_local(load, order, store):
        base = 24 * order
        local_columns = [tall_column(base + col) for col in range(8)]
        for comp in range(3):
            for row in range(ROWS):
                tile = load(comp, row)
                store(comp, row, sum(local_columns[col] * tile[col:col + 1] for col in range(8)))

    def line_receive(order, load, store):
        base = 24 * order
        for kind, step in ((0, LINE - 1), (1, 1)):
            remote(
                y_send.at[order, 0], y_edge.at[order, kind],
                ye_ss.at[order, kind], ye_rs.at[order, kind], line_device(in_line(step)),
            ).wait_recv()
        for step in range(1, LINE):
            remote(
                y_send.at[order, 1], y_recv.at[order, step - 1],
                y_ss.at[order, step - 1], y_rs.at[order, step - 1], line_device(in_line(step)),
            ).wait_recv()
        factors = [tall_column(base + 16 + step) for step in range(1, LINE)]
        first = tall_column(48)
        last = tall_column(49)
        for comp in range(3):
            for row in range(ROWS):
                total = load(comp, row)
                total = total + first * y_edge[order, 0, comp, row:row + 1, :]
                total = total + last * y_edge[order, 1, comp, row:row + 1, :]
                for step in range(1, LINE):
                    total = total + factors[step - 1] * y_recv[order, step - 1, comp, row:row + 1, :]
                store(comp, row, total)

    def depth_apply(values, order):
        high, low = split(values)
        both = matmul(jnp.concatenate([high, low], axis=0), ztab[2 * order])
        count = values.shape[0]
        return both[0:count] + both[count:2 * count] + matmul(high, ztab[2 * order + 1])

    def pass_tokens():
        pl.semaphore_wait(barrier, len(partners))
        for kind, step in ((0, half), (1, RING - half)):
            pl.semaphore_signal(
                token.at[kind], inc=1, device_id=ring_device(in_ring(step)), device_id_type=MESH
            )

        for step in range(1, GROUP):
            pl.semaphore_signal(
                token.at[1 + step], inc=1, device_id=group_device(in_group(step)), device_id_type=MESH
            )

    def wait_tokens(first, last):
        for kind in range(first, last):
            pl.semaphore_wait(token.at[kind], 1)

    loads[0].wait()
    loads[1].wait()
    for comp in range(3):
        left, right = states([vel[comp, row] for row in range(ROWS)])
        for piece in range(GROUP):
            x1_send[0, piece, comp] = pack(left, right, piece)
    build_columns()
    pass_tokens()
    pieces_send(x1_send, x1_recv, x1_ss, x1_rs, 0)
    line_send(lambda comp, row: vel[comp, row], 0)
    x1_recv[0, member] = x1_send[0, member]
    build_weights()
    for load in loads[6:]:
        load.wait()

    def keep_along(comp, row, value):
        along_y[comp, row] = value

    line_local(lambda comp, row: vel[comp, row], 0, keep_along)
    pieces_wait(x1_send, x1_recv, x1_ss, x1_rs, 0)
    wait_tokens(0, 2)

    def first_piece(source, comp):
        return x1_recv[0, source, comp]

    ring_send(0, first_piece)
    line_receive(0, lambda comp, row: along_y[comp, row], keep_along)
    for comp in range(3):
        for row, value in enumerate(local_rows([vel[comp, row] for row in range(ROWS)])):
            smoothed[comp, row] = value
        for row, value in enumerate(local_rows([along_y[comp, row] for row in range(ROWS)])):
            feats[row, 8 * comp:8 * comp + 8, :] = value
    def outward(row):
        parts = [STEP_SIZE * cot[comp, row] for comp in range(3)]
        return jnp.concatenate(parts + [jnp.zeros((8, 256), F32)], axis=0)

    def grad_of_hidden(row, carry):
        out_high, out_low = split(outward(row))
        pulled_out[row] = matmul(out_lhs[...], jnp.concatenate([out_high, out_low, out_high], axis=0))
        rhs[row, 144:160, :] = jnp.ones((16, 256), BF16)
        return carry

    lax.fori_loop(0, ROWS, grad_of_hidden, 0)
    wait_tokens(2, 1 + GROUP)
    ring_state = ring_receive(0)
    for step in (2, 1, 3, 0):
        other = in_group(step)
        for comp in range(3):
            tile = back_piece(ring_state, first_piece, other, comp)
            x3_send[0, other, comp] = tile
            project(0, other, comp, tile)
    plane_rows_send(0)
    pieces_send(x3_send, x3_recv, x3_ss, x3_rs, 0)
    x3_recv[0, member] = x3_send[0, member]
    pieces_wait(x3_send, x3_recv, x3_ss, x3_rs, 0)
    for comp in range(3):
        left, right = unpack([x3_recv[0, piece, comp] for piece in range(GROUP)])
        for row in range(ROWS):
            smoothed[comp, row] += scalar(LEFT + row) * left + scalar(RIGHT + row) * right
    along_z = depth_apply(smoothed[...].reshape(96, 256), 0)
    for comp in range(3):
        for row in range(ROWS):
            start = (comp * ROWS + row) * 8
            feats[row, 24 + 8 * comp:32 + 8 * comp, :] = along_z[start:start + 8]
    plane_rows_wait(0)
    for comp in range(3):
        left, right = unpack([
            own_block(0, x3_recv[0, piece, comp]) + from_plane(0, piece, comp) for piece in range(GROUP)
        ])
        for row in range(ROWS):
            feats[row, 8 * comp:8 * comp + 8, :] += scalar(LEFT + row) * left + scalar(RIGHT + row) * right

    def closure(row):
        feature_high, feature_low = split(feats[row])
        rhs[row, 0:48, :] = feature_high
        rhs[row, 48:96, :] = feature_low
        rhs[row, 96:144, :] = feature_high
        hidden = jnp.tanh(matmul(left_lhs[...], rhs[row]))
        grad_pre = pulled_out[row] * (1.0 - hidden * hidden)
        pre_high, pre_low = split(grad_pre)
        hidden_buf[row] = hidden
        pre_buf[row, 0] = pre_high
        pre_buf[row, 1] = pre_low
        both = matmul(back_lhs[...], pre_high)
        gfeats[row] = both[0:48] + both[48:96] + matmul(back_lhs[0:48, :], pre_low)

    for row in range(ROWS):
        closure(row)

    def grad_along_y(comp, row):
        return gfeats[row, 8 * comp:8 * comp + 8, :]

    packed = {}
    for comp in range(3):
        left, right = states([grad_along_y(comp, row) for row in range(ROWS)])
        for piece in range(GROUP):
            packed[piece, comp] = pack(left, right, piece)
            project(1, piece, comp, packed[piece, comp])
    plane_rows_send(1)
    back_in = jnp.concatenate(
        [gfeats[row, 24 + 8 * comp:32 + 8 * comp, :] for comp in range(3) for row in range(ROWS)], axis=0
    )
    along_z = depth_apply(back_in, 1)
    for comp in range(3):
        starts = [(comp * ROWS + row) * 8 for row in range(ROWS)]
        left, right = states([along_z[start:start + 8] for start in starts])
        for piece in range(GROUP):
            x1_send[1, piece, comp] = own_block(1, packed[piece, comp]) + pack(left, right, piece)
        for row in range(ROWS):
            pulled[comp, row] = along_z[starts[row]:starts[row] + 8]
    pieces_send(x1_send, x1_recv, x1_ss, x1_rs, 1)
    x1_recv[1, member] = x1_send[1, member]

    def keep_pulled(comp, row, value):
        pulled[comp, row] = value

    def line_part():
        line_send(grad_along_y, 1)
        line_local(grad_along_y, 1, lambda comp, row, value: keep_pulled(comp, row, pulled[comp, row] + value))

    def forces(row, carry):
        hidden_high, hidden_low = split(hidden_buf[row])
        both = matmul(force_lhs[...], hidden_high)
        forcing = both[0:32] + both[32:64] + matmul(force_lhs[0:32, :], hidden_low)
        for comp in range(3):
            new_velocity[comp, row] = vel[comp, row] + STEP_SIZE * forcing[8 * comp:8 * comp + 8]
        return carry

    def row_sums(row, carry):
        hidden_high, hidden_low = split(hidden_buf[row])
        feature_high, feature_low = split(feats[row])
        ones = jnp.ones((16, 256), BF16)
        both = matmul_nt(jnp.concatenate([feature_high, ones, feature_low], axis=0), pre_buf[row, 0])
        rest = matmul_nt(jnp.concatenate([feature_high, ones], axis=0), pre_buf[row, 1])
        sums[0:48, :] += both[0:48] + both[64:112] + rest[0:48]
        sums[48:56, :] += both[48:56] + rest[48:56]
        out_high, out_low = split(outward(row))
        both = matmul_nt(jnp.concatenate([out_high, out_low], axis=0), hidden_high)
        rest = matmul_nt(out_high, hidden_low)
        sums[56:88, :] += both[0:32] + both[32:64] + rest
        return carry

    def partial_sums():
        sums[...] = jnp.zeros((88, 512), F32)
        lax.fori_loop(0, ROWS, row_sums, 0)
        same = lax.bitwise_and(iota((88, 512), 0), 7) == lax.bitwise_and(iota((88, 512), 1), 7)
        gather = ones_where(lax.shift_right_logical(iota((512, UNITS), 0), 3) == iota((512, UNITS), 1)).astype(BF16)
        high, low = split(jnp.where(same, sums[...], 0.0))
        narrow = matmul(high, gather) + matmul(low, gather)
        folded = [jnp.sum(narrow[8 * part:8 * part + 8], axis=0, keepdims=True) for part in range(11)]
        front = jnp.concatenate(folded[0:8], axis=0)
        back = jnp.concatenate(folded[8:11] + [jnp.zeros((5, UNITS), F32)], axis=0)
        p1[gy] = jnp.concatenate([front, back], axis=1)
        for step in range(1, LINE):
            other = in_line(step)
            send(p1.at[gy], p1.at[gy], p1_ss.at[other], p1_rs.at[gy], line_device(other))

    def sum_line():
        for step in range(1, LINE):
            other = in_line(step)
            remote(p1.at[other], p1.at[other], p1_ss.at[other], p1_rs.at[other], line_device(other)).wait_recv()
        total = p1[0]
        for other in range(1, LINE):
            total = total + p1[other]
        p2[member] = total
        for step in range(1, GROUP):
            other = in_group(step)
            send(p2.at[member], p2.at[member], p2_ss.at[other], p2_rs.at[member], group_device(other))

    def sum_group():
        for step in range(1, GROUP):
            other = in_group(step)
            remote(p2.at[other], p2.at[other], p2_ss.at[other], p2_rs.at[other], group_device(other)).wait_recv()
        total = p2[0]
        for other in range(1, GROUP):
            total = total + p2[other]
        p3[ring] = total
        for step in (8, 7, 9, 6, 10, 5, 11, 4, 12, 3, 13, 2, 14, 1, 15):
            other = in_ring(step)
            send(p3.at[ring], p3.at[ring], p3_ss.at[other], p3_rs.at[ring], ring_device(other))

    def sum_ring():
        for step in range(1, RING):
            other = in_ring(step)
            remote(p3.at[other], p3.at[other], p3_ss.at[other], p3_rs.at[other], ring_device(other)).wait_recv()
        total = p3[0]
        for other in range(1, RING):
            total = total + p3[other]
        grad_weights[...] = total * (1.0 / float(256 * 64 * 256))

    partial_sums()
    line_part()
    pieces_wait(x1_send, x1_recv, x1_ss, x1_rs, 1)
    plane_rows_wait(1)
    for source in range(GROUP):
        for comp in range(3):
            state[source, comp] = x1_recv[1, source, comp] + from_plane(1, source, comp)

    def second_piece(source, comp):
        return state[source, comp]

    early = len(sent)
    ring_send(1, second_piece)
    sum_line()
    lax.fori_loop(0, ROWS, forces, 0)
    line_receive(1, lambda comp, row: pulled[comp, row], keep_pulled)
    for comp in range(3):
        for row, value in enumerate(local_rows([pulled[comp, row] for row in range(ROWS)])):
            grad_velocity[comp, row] = cot[comp, row] + value
    sum_group()
    drain(early)
    plane_rows_drain(0)
    plane_rows_drain(1)
    ring_state = ring_receive(1)
    for step in (2, 1, 3, 0):
        other = in_group(step)
        for comp in range(3):
            x3_send[1, other, comp] = back_piece(ring_state, second_piece, other, comp)
    pieces_send(x3_send, x3_recv, x3_ss, x3_rs, 1)
    x3_recv[1, member] = x3_send[1, member]
    pieces_wait(x3_send, x3_recv, x3_ss, x3_rs, 1)
    for comp in range(3):
        left, right = unpack([x3_recv[1, piece, comp] for piece in range(GROUP)])
        for row in range(ROWS):
            grad_velocity[comp, row] += scalar(LEFT + row) * left + scalar(RIGHT + row) * right
    sum_ring()
    drain(len(sent))


def finish(new_velocity_in, grad_velocity_in, grads, new_velocity, grad_velocity, grad_in, grad_bias, grad_out_t, sems):
    copies = [
        pltpu.make_async_copy(new_velocity_in, new_velocity, sems.at[0]),
        pltpu.make_async_copy(grad_velocity_in, grad_velocity, sems.at[1]),
    ]
    for copy in copies:
        copy.start()
    front = grads[:, 0:UNITS]
    grad_in[...] = front[0:6]
    grad_bias[...] = front[6:7]
    grad_out_t[0:1] = front[7:8]
    grad_out_t[1:3] = grads[0:2, UNITS:2 * UNITS]
    for copy in copies:
        copy.wait()


def local(velocity, cotangent, weight_in, bias_in, weight_out):
    field = velocity.shape
    dma = pltpu.SemaphoreType.DMA
    anywhere = pl.BlockSpec(memory_space=pl.ANY)
    whole = pl.BlockSpec(memory_space=pltpu.VMEM)
    mid = pl.pallas_call(
        kernel,
        out_shape=(
            pltpu.VMEM(field, F32),
            pltpu.VMEM(field, F32),
            pltpu.VMEM((8, 128), F32),
        ),
        in_specs=[anywhere] * 8,
        out_specs=(whole, whole, whole),
        scratch_shapes=[
            pltpu.VMEM((6, UNITS), F32),
            pltpu.VMEM((1, UNITS), F32),
            pltpu.VMEM((3, UNITS), F32),
            pltpu.VMEM(field, F32),
            pltpu.VMEM(field, F32),
            pltpu.VMEM(field, F32),
            pltpu.VMEM(field, F32),
            pltpu.VMEM((ROWS, 48, 256), F32),
            pltpu.VMEM((ROWS, 48, 256), F32),
            pltpu.VMEM(field, F32),
            pltpu.SMEM((1, 128), F32),
            pltpu.VMEM((8, 128), F32),
            pltpu.VMEM((50, 8, 128), F32),
            pltpu.VMEM((4, 256, 256), BF16),
            pltpu.VMEM((512, 160), BF16),
            pltpu.VMEM((512, 96), BF16),
            pltpu.VMEM((96, 512), BF16),
            pltpu.VMEM((64, 512), BF16),
            pltpu.VMEM((ROWS, 160, 256), BF16),
            pltpu.VMEM((ROWS, 512, 256), F32),
            pltpu.VMEM((ROWS, 512, 256), F32),
            pltpu.VMEM((ROWS, 2, 512, 256), BF16),
            pltpu.VMEM((88, 512), F32),
            pltpu.VMEM((2, GROUP, 3, 8, 128), F32),
            pltpu.VMEM((2, GROUP, 3, 8, 128), F32),
            pltpu.VMEM((GROUP, 3, 8, 128), F32),
            pltpu.VMEM((2, 2, 3, 4, 128), F32),
            pltpu.VMEM((2, RING, 3, 4, 128), F32),
            pltpu.VMEM((2, GROUP, 3, 8, 128), F32),
            pltpu.VMEM((2, GROUP, 3, 8, 128), F32),
            pltpu.VMEM((2, GROUP, 2, 2, 3, 128), F32),
            pltpu.VMEM((2, GROUP, LINE - 3, 3, 128), F32),
            pltpu.VMEM((2, GROUP, 2, 2, 3, 128), F32),
            pltpu.VMEM((2, 4, 3, ROWS, 256), F32),
            pltpu.VMEM((2, LINE - 1, 3, ROWS, 256), F32),
            pltpu.VMEM((2, 2, 3, ROWS, 256), F32),
            pltpu.VMEM((LINE, 8, 128), F32),
            pltpu.VMEM((GROUP, 8, 128), F32),
            pltpu.VMEM((RING, 8, 128), F32),
            pltpu.SemaphoreType.REGULAR((1 + GROUP,)),
            dma((8,)),
            dma((2, GROUP)), dma((2, GROUP)),
            dma((2, RING)), dma((2, RING)),
            dma((2, GROUP)), dma((2, GROUP)),
            dma((2,)), dma((2,)), dma((2,)), dma((2,)),
            dma((2, LINE - 1)), dma((2, LINE - 1)),
            dma((2, 2)), dma((2, 2)),
            dma((LINE,)), dma((LINE,)),
            dma((GROUP,)), dma((GROUP,)),
            dma((RING,)), dma((RING,)),
        ],
        compiler_params=pltpu.CompilerParams(collective_id=0, has_side_effects=True, vmem_limit_bytes=RESERVED),
        name="closure_step",
    )(
        velocity, cotangent, weight_in, bias_in.reshape(1, UNITS), weight_out.T,
        jnp.asarray(smoothing_table()).reshape(GROUP * RING, 1, 128), jnp.asarray(line_table()),
        jnp.asarray(depth_table(field[3])),
    )
    outs = pl.pallas_call(
        finish,
        out_shape=(
            jax.ShapeDtypeStruct(field, F32),
            jax.ShapeDtypeStruct(field, F32),
            jax.ShapeDtypeStruct((6, UNITS), F32),
            jax.ShapeDtypeStruct((1, UNITS), F32),
            jax.ShapeDtypeStruct((3, UNITS), F32),
        ),
        in_specs=[whole] * 3,
        out_specs=(anywhere, anywhere, whole, whole, whole),
        scratch_shapes=[dma((2,))],
        compiler_params=pltpu.CompilerParams(vmem_limit_bytes=1 << 20),
        name="finish",
    )(*mid)
    return outs[0], outs[1], outs[2], outs[3].reshape(UNITS), outs[4].T


def solution(mesh):
    in_specs = (P(None, "gx", "gy", None), P(None, "gx", "gy", None), P(), P(), P())
    out_specs = (P(None, "gx", "gy", None), P(None, "gx", "gy", None), P(), P(), P())
    return jax.shard_map(local, mesh=mesh, in_specs=in_specs, out_specs=out_specs, check_vma=False)
```

```python
import functools

import jax
import jax.numpy as jnp
import ml_dtypes
import numpy as np
from jax import lax
from jax.experimental import pallas as pl
from jax.experimental.pallas import tpu as pltpu
from jax.sharding import PartitionSpec as P

FILTER_ALPHA = 0.499
FILTER_GAIN = 0.5 + FILTER_ALPHA
COMPACT_ALPHA = 1.0 / 3.0
STEP_SIZE = 0.5
MESH = pl.DeviceIdType.MESH
F32 = jnp.float32
BF16 = jnp.bfloat16

GROUP = 4
RING = 16
LINE = 8
ROWS = 4
UNITS = 64
RESERVED = 66300000

UP_W, DOWN_W, UP_C, DOWN_C, RING_L, RING_R, BACK_L, BACK_R, LOCAL, LEFT, RIGHT = (
    0, 4, 8, 12, 16, 32, 48, 68, 88, 104, 108
)


def tridiagonal(length, coupling):
    return np.eye(length) + coupling * (np.eye(length, k=1) + np.eye(length, k=-1))


def smoothing_table():
    devices = GROUP * RING
    length = devices * ROWS
    matrix = tridiagonal(length, FILTER_ALPHA)
    inverse = np.linalg.inv(matrix)
    smoothing = np.linalg.solve(matrix, FILTER_GAIN * tridiagonal(length, 0.5))

    def move(row, pivot):
        return inverse[row, pivot] / inverse[pivot, pivot]

    table = np.zeros((devices, 128))
    block = GROUP * ROWS
    for device in range(devices):
        ring, member = divmod(device, GROUP)
        first = device * ROWS
        last = first + ROWS - 1
        entry = table[device]
        if device < devices - 1:
            entry[UP_W:UP_W + ROWS] = smoothing[last + 1, first:first + ROWS]
        if device > 0:
            entry[DOWN_W:DOWN_W + ROWS] = smoothing[first - 1, first:first + ROWS]
        group_first = ring * block
        group_last = group_first + block - 1
        for other in range(GROUP):
            start = group_first + other * ROWS
            if ring < RING - 1:
                entry[UP_C + other] = move(group_last + 1, start + ROWS)
            if ring > 0:
                entry[DOWN_C + other] = move(group_first - 1, start - 1)
        for other in range(RING):
            if other < ring:
                entry[RING_L + other] = move(group_first, (other + 1) * block)
            if other > ring:
                entry[RING_R + other] = move(group_last, other * block - 1)
        for target in range(GROUP):
            own_first = group_first + target * ROWS
            own_last = own_first + ROWS - 1
            entry[BACK_L + 5 * target] = move(own_first, group_first)
            entry[BACK_R + 5 * target] = move(own_last, group_last)
            for other in range(GROUP):
                start = group_first + other * ROWS
                if other < target:
                    entry[BACK_L + 5 * target + 1 + other] = move(own_first, start + ROWS)
                if other > target:
                    entry[BACK_R + 5 * target + 1 + other] = move(own_last, start - 1)
        entry[LOCAL:LOCAL + ROWS * ROWS] = smoothing[first:last + 1, first:last + 1].reshape(-1)
        for row in range(ROWS):
            entry[LEFT + row] = move(first + row, first)
            entry[RIGHT + row] = move(first + row, last)
    return table.astype(np.float32)


def derivative_matrix(length):
    right = 7.0 / 9.0 * (np.eye(length, k=1) - np.eye(length, k=-1)) + 1.0 / 36.0 * (
        np.eye(length, k=2) - np.eye(length, k=-2)
    )
    return np.linalg.solve(tridiagonal(length, COMPACT_ALPHA), right)


def line_table():
    size = 8
    length = LINE * size
    forward = derivative_matrix(length)
    table = np.zeros((LINE, size, 128))
    for place, matrix in enumerate((forward, forward.T)):
        base = 24 * place
        for device in range(LINE):
            rows = slice(device * size, device * size + size)
            table[device, :, base:base + 8] = matrix[rows, rows]
            if device < LINE - 1:
                table[device, 0, base + 8:base + 16] = matrix[device * size + 8, rows]
                table[device, 1, base + 8:base + 16] = matrix[device * size + 9, rows]
            if device > 0:
                table[device, 2, base + 8:base + 16] = matrix[device * size - 1, rows]
                table[device, 3, base + 8:base + 16] = matrix[device * size - 2, rows]
            for step in range(1, LINE):
                source = (device - step) % LINE
                columns = slice(source * size, source * size + size)
                pivot = source * size + 9 if source < device else source * size - 2
                sent = matrix[pivot, columns]
                factors = matrix[rows, columns] @ sent / (sent @ sent)
                if source == device - 1:
                    factors[0] = 0.0
                if source == device + 1:
                    factors[size - 1] = 0.0
                table[device, :, base + 16 + step] = factors
    table[1:, 0, 48] = 1.0
    table[:-1, size - 1, 49] = 1.0
    return table.astype(np.float32)


def split_table(matrix):
    high = matrix.astype(np.float32).astype(ml_dtypes.bfloat16)
    low = (matrix - high.astype(np.float64)).astype(np.float32).astype(ml_dtypes.bfloat16)
    return [high, low]


def depth_table(length):
    matrix = derivative_matrix(length)
    return np.stack(split_table(matrix.T.copy()) + split_table(matrix))


def split(values):
    high = values.astype(BF16)
    return high, (values - high.astype(F32)).astype(BF16)


def iota(shape, dim):
    return lax.broadcasted_iota(jnp.int32, shape, dim)


def ones_where(condition):
    return jnp.where(condition, 1.0, 0.0).astype(F32)


def matmul(a, b):
    return jnp.dot(a, b, preferred_element_type=F32)


def matmul_nt(a, b, precision=None):
    return lax.dot_general(a, b, (((1,), (1,)), ((), ())), precision=precision, preferred_element_type=F32)


def kernel(
    velocity, cotangent, weight_in, bias_in, weight_out, x_table, y_table, z_table,
    new_velocity, grad_velocity, grad_weights,
    w_in, w_bias, w_out, vel, cot, along_y, smoothed, feats, gfeats, pulled,
    scalars, columns, tall, ztab,
    left_lhs, out_lhs, back_lhs, force_lhs, rhs, pulled_out, hidden_buf, pre_buf, sums,
    x1_send, x1_recv, state, group_rows, x2_send, x2_recv, x3_send, x3_recv, plane_send, plane_recv, plane_edge,
    y_send, y_recv, y_edge,
    p1, p2, p3,
    token, local_sem, x1_ss, x1_rs, x2_ss, x2_rs, x3_ss, x3_rs, plane_ss, plane_rs, edge_ss, edge_rs,
    y_ss, y_rs, ye_ss, ye_rs,
    p1_ss, p1_rs, p2_ss, p2_rs, p3_ss, p3_rs,
):
    gx = lax.axis_index("gx")
    gy = lax.axis_index("gy")
    ring = lax.div(gx, GROUP)
    member = lax.rem(gx, GROUP)

    def in_group(step):
        return lax.rem(member + step, GROUP)

    def in_ring(step):
        return lax.rem(ring + step, RING)

    def in_line(step):
        return lax.rem(gy + step, LINE)

    def group_device(other):
        return (ring * GROUP + other, gy)

    def ring_device(other):
        return (other * GROUP + member, gy)

    def line_device(other):
        return (gx, other)

    def plane_device(other, place):
        return (ring * GROUP + other, place)

    barrier = pltpu.get_barrier_semaphore()
    half = RING // 4
    partners = (
        [ring_device(in_ring(step)) for step in (4, 12, 3, 13, 2, 14, 1, 15)]
        + [line_device(in_line(step)) for step in range(1, LINE)]
        + [group_device(in_group(step)) for step in range(1, GROUP)]
    )
    for partner in partners:
        pl.semaphore_signal(barrier, inc=1, device_id=partner, device_id_type=MESH)

    loads = [
        pltpu.make_async_copy(x_table.at[gx], scalars, local_sem.at[0]),
        pltpu.make_async_copy(velocity, vel, local_sem.at[1]),
        pltpu.make_async_copy(y_table.at[gy], columns, local_sem.at[2]),
        pltpu.make_async_copy(weight_in, w_in, local_sem.at[3]),
        pltpu.make_async_copy(bias_in, w_bias, local_sem.at[4]),
        pltpu.make_async_copy(weight_out, w_out, local_sem.at[5]),
        pltpu.make_async_copy(cotangent, cot, local_sem.at[6]),
        pltpu.make_async_copy(z_table, ztab, local_sem.at[7]),
    ]
    for load in loads:
        load.start()

    def remote(src, dst, send_sem, recv_sem, device):
        return pltpu.make_async_remote_copy(
            src_ref=src, dst_ref=dst, send_sem=send_sem, recv_sem=recv_sem, device_id=device, device_id_type=MESH
        )

    sent = []

    def send(*args, drain=True):
        copy = remote(*args)
        copy.start()
        if drain:
            sent.append(copy)

    def drain(count):
        for copy in sent[:count]:
            copy.wait_send()
        del sent[:count]

    def scalar(index):
        return scalars[0, index]

    def build_weights():
        for load in loads[3:6]:
            load.wait()
        w_high, w_low = split(w_in[...])
        spread = ones_where(lax.shift_right_logical(iota((512, UNITS), 0), 3) == iota((512, UNITS), 1)).astype(BF16)
        spread_t = ones_where(iota((UNITS, 512), 0) == lax.shift_right_logical(iota((UNITS, 512), 1), 3)).astype(BF16)
        bias = w_bias[...]
        b_high, b_low = split(bias)
        b_rest = bias - b_high.astype(F32) - b_low.astype(F32)
        row = iota((8, 160), 0)
        col = iota((8, 160), 1)
        field = lax.shift_right_logical(col, 3)
        pick_high = ones_where(((field == row) | (field == row + 6)) & (row < 6)).astype(BF16)
        pick_low = ones_where((field == row + 12) & (row < 6)).astype(BF16)
        spread_high = matmul_nt(spread, w_high).astype(BF16)
        spread_low = matmul_nt(spread, w_low).astype(BF16)
        top = matmul(spread_high, pick_high[0:6]) + matmul(spread_low, pick_low[0:6])
        same = lax.bitwise_and(iota((512, 160), 0), 7) == lax.bitwise_and(iota((512, 160), 1), 7)
        top = jnp.where(same, top, 0.0)
        biases = jnp.concatenate([b_high.astype(F32), b_low.astype(F32), b_rest, jnp.zeros((5, UNITS), F32)], axis=0)
        spread_bias = matmul_nt(spread, biases.astype(BF16)).astype(BF16)
        top = top + matmul(spread_bias, ones_where(col == row + 144).astype(BF16))
        left_lhs[...] = top.astype(BF16)
        o_high, o_low = split(w_out[...])
        row, field, same = row[:, 0:96], field[:, 0:96], same[:, 0:96]
        pick_high = ones_where(((field == row) | (field == row + 4)) & (row < 3)).astype(BF16)
        pick_low = ones_where((field == row + 8) & (row < 3)).astype(BF16)
        spread_oh = matmul_nt(spread, o_high).astype(BF16)
        spread_ol = matmul_nt(spread, o_low).astype(BF16)
        bottom = matmul(spread_oh, pick_high[0:3]) + matmul(spread_ol, pick_low[0:3])
        out_lhs[...] = jnp.where(same, bottom, 0.0).astype(BF16)

        same_t = lax.bitwise_and(iota((96, 512), 0), 7) == lax.bitwise_and(iota((96, 512), 1), 7)
        row = lax.shift_right_logical(iota((96, 8), 0), 3)
        col = iota((96, 8), 1)
        get_high = ones_where((row == col) & (col < 6)).astype(BF16)
        get_low = ones_where((row == col + 6) & (col < 6)).astype(BF16)
        tall_w = matmul(get_high[:, 0:6], w_high) + matmul(get_low[:, 0:6], w_low)
        back_lhs[...] = jnp.where(same_t, matmul(tall_w.astype(BF16), spread_t), 0.0).astype(BF16)
        get_high = ones_where((row[0:64] == col[0:64]) & (col[0:64] < 3)).astype(BF16)
        get_low = ones_where((row[0:64] == col[0:64] + 4) & (col[0:64] < 3)).astype(BF16)
        tall_o = matmul(get_high[:, 0:3], o_high) + matmul(get_low[:, 0:3], o_low)
        force_lhs[...] = jnp.where(same_t[0:64], matmul(tall_o.astype(BF16), spread_t), 0.0).astype(BF16)

    def build_columns():
        loads[2].wait()
        line_columns = columns[...]
        for index in range(50):
            tall[index] = jnp.broadcast_to(line_columns[:, index:index + 1], (8, 128))

    def tall_column(index):
        half = tall[index]
        return jnp.concatenate([half, half], axis=1)

    lower = iota((8, 128), 1) < 64

    def turn(tile):
        return pltpu.roll(tile, 64, 1)

    def pack(left, right, piece):
        lanes = slice(128 * (piece // 2), 128 * (piece // 2) + 128)
        if piece % 2 == 0:
            return jnp.where(lower, left[:, lanes], turn(right[:, lanes]))
        return jnp.where(lower, turn(left[:, lanes]), right[:, lanes])

    def unpack(pieces):
        left = [jnp.where(lower, pieces[2 * t], turn(pieces[2 * t + 1])) for t in range(2)]
        right = [jnp.where(lower, turn(pieces[2 * t]), pieces[2 * t + 1]) for t in range(2)]
        return jnp.concatenate(left, axis=1), jnp.concatenate(right, axis=1)

    def two_scalars(left_index, right_index):
        return jnp.where(lower, scalar(left_index), scalar(right_index))

    def states(rows):
        return [sum(scalar(base + row) * rows[row] for row in range(ROWS)) for base in (UP_W, DOWN_W)]

    def local_rows(rows):
        return [
            sum(scalar(LOCAL + ROWS * row + col) * rows[col] for col in range(ROWS)) for row in range(ROWS)
        ]

    def pieces_send(source, target, send_sems, recv_sems, order):
        for step in (2, 1, 3):
            other = in_group(step)
            send(
                source.at[order, other], target.at[order, member],
                send_sems.at[order, other], recv_sems.at[order, member], group_device(other),
            )

    def pieces_wait(source, target, send_sems, recv_sems, order):
        for step in range(1, GROUP):
            other = in_group(step)
            remote(
                source.at[order, other], target.at[order, other],
                send_sems.at[order, other], recv_sems.at[order, other], group_device(other),
            ).wait_recv()

    def ring_send(order, load):
        gathered = []
        for comp in range(3):
            gathered.append(sum(
                two_scalars(UP_C + other, DOWN_C + other) * load(other, comp) for other in range(GROUP)
            ))
        first, second, third = gathered
        turned = turn(third)
        front = jnp.where(lower, first, turn(second))
        x2_send[order, 0, 0] = front[0:4]
        x2_send[order, 0, 1] = front[4:8]
        x2_send[order, 0, 2] = jnp.where(lower[0:4], third[0:4], turned[4:8])
        front = jnp.where(lower, turn(first), second)
        x2_send[order, 1, 0] = front[0:4]
        x2_send[order, 1, 1] = front[4:8]
        x2_send[order, 1, 2] = jnp.where(lower[0:4], turned[0:4], third[4:8])
        for step in (8, 7, 9, 6, 10, 5, 11, 4, 12, 3, 13, 2, 14, 1, 15):
            other = in_ring(step)
            kind = jnp.where(other > ring, 0, 1)
            send(
                x2_send.at[order, kind], x2_recv.at[order, ring],
                x2_ss.at[order, other], x2_rs.at[order, ring], ring_device(other),
            )

    def ring_receive(order):
        left = jnp.zeros((3, 4, 128), F32)
        right = jnp.zeros((3, 4, 128), F32)
        for step in (1, 15, 2, 14, 3, 13, 4, 12, 5, 11, 6, 10, 7, 9, 8):
            other = in_ring(step)
            remote(
                x2_send.at[order, 0], x2_recv.at[order, other],
                x2_ss.at[order, other], x2_rs.at[order, other], ring_device(other),
            ).wait_recv()
            part = x2_recv[order, other]
            left = left + scalar(RING_L + other) * part
            right = right + scalar(RING_R + other) * part
        front_left = jnp.concatenate([left[0], left[1]], axis=0)
        front_right = jnp.concatenate([right[0], right[1]], axis=0)
        back_left = jnp.concatenate([left[2], pltpu.roll(left[2], 64, 1)], axis=0)
        back_right = jnp.concatenate([pltpu.roll(right[2], 64, 1), right[2]], axis=0)
        return [
            jnp.where(lower, front_left, turn(front_right)),
            jnp.where(lower, turn(front_left), front_right),
            jnp.where(lower, back_left, back_right),
        ]

    def group_part(load, other, comp):
        total = jnp.zeros((8, 128), F32)
        for source in range(GROUP):
            index = 5 * other + 1 + source
            total = total + two_scalars(BACK_L + index, BACK_R + index) * load(source, comp)
        return total

    def ring_factor(other):
        return two_scalars(BACK_L + 5 * other, BACK_R + 5 * other)

    def projected(order, tile):
        return sum(tall[24 * order + 8 + col] * tile[col:col + 1] for col in range(8))

    def keep_rows(order, other, comp, out):
        for kind in range(4):
            plane_send[order, other, kind // 2, kind % 2, comp:comp + 1, :] = out[kind:kind + 1]

    def plane_rows_send(order, steps):
        for step in steps:
            other = in_group(step)
            for along in (4, 5, 3, 6, 2, 7, 1):
                place = in_line(along)
                side = jnp.where(place > gy, 0, 1)
                if along in (1, LINE - 1):
                    send(
                        plane_send.at[order, other, side], plane_edge.at[order, member, 0 if along == 1 else 1],
                        edge_ss.at[order], edge_rs.at[order], plane_device(other, place), drain=False,
                    )
                else:
                    send(
                        plane_send.at[order, other, side, 1], plane_recv.at[order, member, along - 2],
                        plane_ss.at[order], plane_rs.at[order], plane_device(other, place), drain=False,
                    )

    def plane_rows_all(order):
        device = plane_device(in_group(1), in_line(1))
        return (
            remote(plane_recv.at[order], plane_recv.at[order], plane_ss.at[order], plane_rs.at[order], device),
            remote(plane_edge.at[order], plane_edge.at[order], edge_ss.at[order], edge_rs.at[order], device),
        )

    def plane_rows_wait(order):
        for copy in plane_rows_all(order):
            copy.wait_recv()

    def plane_rows_drain(order):
        for copy in plane_rows_all(order):
            copy.wait_send()

    def from_plane(order, source, comp):
        def row(ref, *index):
            return ref[(order, source) + index + (slice(comp, comp + 1),)]

        factor = 24 * order + 16
        total = tall[48] * row(plane_edge, 0, 0) + tall[factor + 1] * row(plane_edge, 0, 1)
        total = total + tall[49] * row(plane_edge, 1, 0) + tall[factor + LINE - 1] * row(plane_edge, 1, 1)
        for along in range(2, LINE - 1):
            total = total + tall[factor + along] * row(plane_recv, along - 2)
        return total

    def own_block(order, tile):
        return sum(tall[24 * order + col] * tile[col:col + 1] for col in range(8))

    def line_send(load, order):
        base = 24 * order
        sent_columns = [tall_column(base + 8 + col) for col in range(8)]
        for comp in range(3):
            for row in range(ROWS):
                tile = load(comp, row)
                out = sum(sent_columns[col] * tile[col:col + 1] for col in range(8))
                for kind in range(4):
                    y_send[order, kind, comp, row:row + 1, :] = out[kind:kind + 1]
        for kind, step in ((0, 1), (1, LINE - 1)):
            send(
                y_send.at[order, 2 * kind], y_edge.at[order, kind],
                ye_ss.at[order, kind], ye_rs.at[order, kind], line_device(in_line(step)),
            )
        for step in (4, 5, 3, 2, 6, 1, 7):
            other = in_line(step)
            kind = jnp.where(other > gy, 1, 3)
            send(
                y_send.at[order, kind], y_recv.at[order, step - 1],
                y_ss.at[order, step - 1], y_rs.at[order, step - 1], line_device(other),
            )

    def line_local(load, order, store):
        base = 24 * order
        local_columns = [tall_column(base + col) for col in range(8)]
        for comp in range(3):
            for row in range(ROWS):
                tile = load(comp, row)
                store(comp, row, sum(local_columns[col] * tile[col:col + 1] for col in range(8)))

    def line_receive(order, load, store):
        base = 24 * order
        for kind, step in ((0, LINE - 1), (1, 1)):
            remote(
                y_send.at[order, 0], y_edge.at[order, kind],
                ye_ss.at[order, kind], ye_rs.at[order, kind], line_device(in_line(step)),
            ).wait_recv()
        for step in range(1, LINE):
            remote(
                y_send.at[order, 1], y_recv.at[order, step - 1],
                y_ss.at[order, step - 1], y_rs.at[order, step - 1], line_device(in_line(step)),
            ).wait_recv()
        factors = [tall_column(base + 16 + step) for step in range(1, LINE)]
        first = tall_column(48)
        last = tall_column(49)
        for comp in range(3):
            for row in range(ROWS):
                total = load(comp, row)
                total = total + first * y_edge[order, 0, comp, row:row + 1, :]
                total = total + last * y_edge[order, 1, comp, row:row + 1, :]
                for step in range(1, LINE):
                    total = total + factors[step - 1] * y_recv[order, step - 1, comp, row:row + 1, :]
                store(comp, row, total)

    def depth_apply(values, order):
        high, low = split(values)
        both = matmul(jnp.concatenate([high, low], axis=0), ztab[2 * order])
        count = values.shape[0]
        return both[0:count] + both[count:2 * count] + matmul(high, ztab[2 * order + 1])

    def pass_tokens():
        pl.semaphore_wait(barrier, len(partners))
        for kind, step in ((0, half), (1, RING - half)):
            pl.semaphore_signal(
                token.at[kind], inc=1, device_id=ring_device(in_ring(step)), device_id_type=MESH
            )

        for step in range(1, GROUP):
            pl.semaphore_signal(
                token.at[1 + step], inc=1, device_id=group_device(in_group(step)), device_id_type=MESH
            )

    def wait_tokens(first, last):
        for kind in range(first, last):
            pl.semaphore_wait(token.at[kind], 1)

    loads[0].wait()
    loads[1].wait()
    for comp in range(3):
        left, right = states([vel[comp, row] for row in range(ROWS)])
        for piece in range(GROUP):
            x1_send[0, piece, comp] = pack(left, right, piece)
    build_columns()
    pass_tokens()
    pieces_send(x1_send, x1_recv, x1_ss, x1_rs, 0)
    line_send(lambda comp, row: vel[comp, row], 0)
    x1_recv[0, member] = x1_send[0, member]
    build_weights()
    for load in loads[6:]:
        load.wait()

    def keep_along(comp, row, value):
        along_y[comp, row] = value

    line_local(lambda comp, row: vel[comp, row], 0, keep_along)
    pieces_wait(x1_send, x1_recv, x1_ss, x1_rs, 0)
    wait_tokens(0, 2)

    def first_piece(source, comp):
        return x1_recv[0, source, comp]

    ring_send(0, first_piece)
    line_receive(0, lambda comp, row: along_y[comp, row], keep_along)
    for comp in range(3):
        for row, value in enumerate(local_rows([vel[comp, row] for row in range(ROWS)])):
            smoothed[comp, row] = value
        for row, value in enumerate(local_rows([along_y[comp, row] for row in range(ROWS)])):
            feats[row, 8 * comp:8 * comp + 8, :] = value
    def outward(row):
        parts = [STEP_SIZE * cot[comp, row] for comp in range(3)]
        return jnp.concatenate(parts + [jnp.zeros((8, 256), F32)], axis=0)

    def grad_of_hidden(row, carry):
        out_high, out_low = split(outward(row))
        pulled_out[row] = matmul(out_lhs[...], jnp.concatenate([out_high, out_low, out_high], axis=0))
        rhs[row, 144:160, :] = jnp.ones((16, 256), BF16)
        return carry

    lax.fori_loop(0, ROWS, grad_of_hidden, 0)
    wait_tokens(2, 1 + GROUP)
    for other in range(GROUP):
        for comp in range(3):
            tile = group_part(first_piece, other, comp)
            x3_send[0, other, comp] = tile
            group_rows[other, comp] = projected(0, tile)
    ring_state = ring_receive(0)
    ring_rows = [projected(0, ring_state[comp]) for comp in range(3)]
    for step in range(GROUP):
        other = in_group(step)
        factor = ring_factor(other)
        for comp in range(3):
            x3_send[0, other, comp] += factor * ring_state[comp]
            keep_rows(0, other, comp, group_rows[other, comp] + factor * ring_rows[comp])
    plane_rows_send(0, (2,))
    pieces_send(x3_send, x3_recv, x3_ss, x3_rs, 0)
    plane_rows_send(0, (1, 3, 0))
    x3_recv[0, member] = x3_send[0, member]
    pieces_wait(x3_send, x3_recv, x3_ss, x3_rs, 0)
    for comp in range(3):
        left, right = unpack([x3_recv[0, piece, comp] for piece in range(GROUP)])
        for row in range(ROWS):
            smoothed[comp, row] += scalar(LEFT + row) * left + scalar(RIGHT + row) * right
    along_z = depth_apply(smoothed[...].reshape(96, 256), 0)
    for comp in range(3):
        for row in range(ROWS):
            start = (comp * ROWS + row) * 8
            feats[row, 24 + 8 * comp:32 + 8 * comp, :] = along_z[start:start + 8]
    for piece in range(GROUP):
        for comp in range(3):
            state[piece, comp] = own_block(0, x3_recv[0, piece, comp])
    plane_rows_wait(0)
    for comp in range(3):
        left, right = unpack([state[piece, comp] + from_plane(0, piece, comp) for piece in range(GROUP)])
        for row in range(ROWS):
            feats[row, 8 * comp:8 * comp + 8, :] += scalar(LEFT + row) * left + scalar(RIGHT + row) * right

    def closure(row):
        feature_high, feature_low = split(feats[row])
        rhs[row, 0:48, :] = feature_high
        rhs[row, 48:96, :] = feature_low
        rhs[row, 96:144, :] = feature_high
        hidden = jnp.tanh(matmul(left_lhs[...], rhs[row]))
        grad_pre = pulled_out[row] * (1.0 - hidden * hidden)
        pre_high, pre_low = split(grad_pre)
        hidden_buf[row] = hidden
        pre_buf[row, 0] = pre_high
        pre_buf[row, 1] = pre_low
        both = matmul(back_lhs[...], pre_high)
        gfeats[row] = both[0:48] + both[48:96] + matmul(back_lhs[0:48, :], pre_low)

    for row in range(ROWS):
        closure(row)

    def grad_along_y(comp, row):
        return gfeats[row, 8 * comp:8 * comp + 8, :]

    packed = {}
    for comp in range(3):
        left, right = states([grad_along_y(comp, row) for row in range(ROWS)])
        for piece in range(GROUP):
            packed[piece, comp] = pack(left, right, piece)
            keep_rows(1, piece, comp, projected(1, packed[piece, comp]))
    plane_rows_send(1, (2, 1, 3, 0))
    back_in = jnp.concatenate(
        [gfeats[row, 24 + 8 * comp:32 + 8 * comp, :] for comp in range(3) for row in range(ROWS)], axis=0
    )
    along_z = depth_apply(back_in, 1)
    for comp in range(3):
        starts = [(comp * ROWS + row) * 8 for row in range(ROWS)]
        left, right = states([along_z[start:start + 8] for start in starts])
        for piece in range(GROUP):
            x1_send[1, piece, comp] = own_block(1, packed[piece, comp]) + pack(left, right, piece)
        for row in range(ROWS):
            pulled[comp, row] = along_z[starts[row]:starts[row] + 8]
    pieces_send(x1_send, x1_recv, x1_ss, x1_rs, 1)
    x1_recv[1, member] = x1_send[1, member]

    def keep_pulled(comp, row, value):
        pulled[comp, row] = value

    def line_part():
        line_send(grad_along_y, 1)
        line_local(grad_along_y, 1, lambda comp, row, value: keep_pulled(comp, row, pulled[comp, row] + value))

    def forces(row, carry):
        hidden_high, hidden_low = split(hidden_buf[row])
        both = matmul(force_lhs[...], hidden_high)
        forcing = both[0:32] + both[32:64] + matmul(force_lhs[0:32, :], hidden_low)
        for comp in range(3):
            new_velocity[comp, row] = vel[comp, row] + STEP_SIZE * forcing[8 * comp:8 * comp + 8]
        return carry

    def row_sums(row, carry):
        hidden_high, hidden_low = split(hidden_buf[row])
        feature_high, feature_low = split(feats[row])
        ones = jnp.ones((16, 256), BF16)
        both = matmul_nt(jnp.concatenate([feature_high, ones, feature_low], axis=0), pre_buf[row, 0])
        rest = matmul_nt(jnp.concatenate([feature_high, ones], axis=0), pre_buf[row, 1])
        sums[0:48, :] += both[0:48] + both[64:112] + rest[0:48]
        sums[48:56, :] += both[48:56] + rest[48:56]
        out_high, out_low = split(outward(row))
        both = matmul_nt(jnp.concatenate([out_high, out_low], axis=0), hidden_high)
        rest = matmul_nt(out_high, hidden_low)
        sums[56:88, :] += both[0:32] + both[32:64] + rest
        return carry

    def partial_sums():
        sums[...] = jnp.zeros((88, 512), F32)
        lax.fori_loop(0, ROWS, row_sums, 0)
        same = lax.bitwise_and(iota((88, 512), 0), 7) == lax.bitwise_and(iota((88, 512), 1), 7)
        gather = ones_where(lax.shift_right_logical(iota((512, UNITS), 0), 3) == iota((512, UNITS), 1)).astype(BF16)
        high, low = split(jnp.where(same, sums[...], 0.0))
        narrow = matmul(high, gather) + matmul(low, gather)
        folded = [jnp.sum(narrow[8 * part:8 * part + 8], axis=0, keepdims=True) for part in range(11)]
        front = jnp.concatenate(folded[0:8], axis=0)
        back = jnp.concatenate(folded[8:11] + [jnp.zeros((5, UNITS), F32)], axis=0)
        p1[gy] = jnp.concatenate([front, back], axis=1)
        for step in range(1, LINE):
            other = in_line(step)
            send(p1.at[gy], p1.at[gy], p1_ss.at[other], p1_rs.at[gy], line_device(other))

    def sum_line():
        for step in range(1, LINE):
            other = in_line(step)
            remote(p1.at[other], p1.at[other], p1_ss.at[other], p1_rs.at[other], line_device(other)).wait_recv()
        total = p1[0]
        for other in range(1, LINE):
            total = total + p1[other]
        p2[member] = total
        for step in range(1, GROUP):
            other = in_group(step)
            send(p2.at[member], p2.at[member], p2_ss.at[other], p2_rs.at[member], group_device(other))

    def sum_group():
        for step in range(1, GROUP):
            other = in_group(step)
            remote(p2.at[other], p2.at[other], p2_ss.at[other], p2_rs.at[other], group_device(other)).wait_recv()
        total = p2[0]
        for other in range(1, GROUP):
            total = total + p2[other]
        p3[ring] = total
        for step in (8, 7, 9, 6, 10, 5, 11, 4, 12, 3, 13, 2, 14, 1, 15):
            other = in_ring(step)
            send(p3.at[ring], p3.at[ring], p3_ss.at[other], p3_rs.at[ring], ring_device(other))

    def sum_ring():
        for step in range(1, RING):
            other = in_ring(step)
            remote(p3.at[other], p3.at[other], p3_ss.at[other], p3_rs.at[other], ring_device(other)).wait_recv()
        total = p3[0]
        for other in range(1, RING):
            total = total + p3[other]
        grad_weights[...] = total * (1.0 / float(256 * 64 * 256))

    partial_sums()
    line_part()
    pieces_wait(x1_send, x1_recv, x1_ss, x1_rs, 1)
    plane_rows_wait(1)
    for source in range(GROUP):
        for comp in range(3):
            state[source, comp] = x1_recv[1, source, comp] + from_plane(1, source, comp)

    def second_piece(source, comp):
        return state[source, comp]

    early = len(sent)
    ring_send(1, second_piece)
    sum_line()
    lax.fori_loop(0, ROWS, forces, 0)
    line_receive(1, lambda comp, row: pulled[comp, row], keep_pulled)
    for comp in range(3):
        for row, value in enumerate(local_rows([pulled[comp, row] for row in range(ROWS)])):
            grad_velocity[comp, row] = cot[comp, row] + value
    sum_group()
    for other in range(GROUP):
        for comp in range(3):
            x3_send[1, other, comp] = group_part(second_piece, other, comp)
    drain(early)
    plane_rows_drain(0)
    plane_rows_drain(1)
    ring_state = ring_receive(1)
    for step in range(GROUP):
        other = in_group(step)
        factor = ring_factor(other)
        for comp in range(3):
            x3_send[1, other, comp] += factor * ring_state[comp]
    pieces_send(x3_send, x3_recv, x3_ss, x3_rs, 1)
    x3_recv[1, member] = x3_send[1, member]
    pieces_wait(x3_send, x3_recv, x3_ss, x3_rs, 1)
    for comp in range(3):
        left, right = unpack([x3_recv[1, piece, comp] for piece in range(GROUP)])
        for row in range(ROWS):
            grad_velocity[comp, row] += scalar(LEFT + row) * left + scalar(RIGHT + row) * right
    sum_ring()
    drain(len(sent))


def finish(new_velocity_in, grad_velocity_in, grads, new_velocity, grad_velocity, grad_in, grad_bias, grad_out_t, sems):
    copies = [
        pltpu.make_async_copy(new_velocity_in, new_velocity, sems.at[0]),
        pltpu.make_async_copy(grad_velocity_in, grad_velocity, sems.at[1]),
    ]
    for copy in copies:
        copy.start()
    front = grads[:, 0:UNITS]
    grad_in[...] = front[0:6]
    grad_bias[...] = front[6:7]
    grad_out_t[0:1] = front[7:8]
    grad_out_t[1:3] = grads[0:2, UNITS:2 * UNITS]
    for copy in copies:
        copy.wait()


def local(velocity, cotangent, weight_in, bias_in, weight_out):
    field = velocity.shape
    dma = pltpu.SemaphoreType.DMA
    anywhere = pl.BlockSpec(memory_space=pl.ANY)
    whole = pl.BlockSpec(memory_space=pltpu.VMEM)
    mid = pl.pallas_call(
        kernel,
        out_shape=(
            pltpu.VMEM(field, F32),
            pltpu.VMEM(field, F32),
            pltpu.VMEM((8, 128), F32),
        ),
        in_specs=[anywhere] * 8,
        out_specs=(whole, whole, whole),
        scratch_shapes=[
            pltpu.VMEM((6, UNITS), F32),
            pltpu.VMEM((1, UNITS), F32),
            pltpu.VMEM((3, UNITS), F32),
            pltpu.VMEM(field, F32),
            pltpu.VMEM(field, F32),
            pltpu.VMEM(field, F32),
            pltpu.VMEM(field, F32),
            pltpu.VMEM((ROWS, 48, 256), F32),
            pltpu.VMEM((ROWS, 48, 256), F32),
            pltpu.VMEM(field, F32),
            pltpu.SMEM((1, 128), F32),
            pltpu.VMEM((8, 128), F32),
            pltpu.VMEM((50, 8, 128), F32),
            pltpu.VMEM((4, 256, 256), BF16),
            pltpu.VMEM((512, 160), BF16),
            pltpu.VMEM((512, 96), BF16),
            pltpu.VMEM((96, 512), BF16),
            pltpu.VMEM((64, 512), BF16),
            pltpu.VMEM((ROWS, 160, 256), BF16),
            pltpu.VMEM((ROWS, 512, 256), F32),
            pltpu.VMEM((ROWS, 512, 256), F32),
            pltpu.VMEM((ROWS, 2, 512, 256), BF16),
            pltpu.VMEM((88, 512), F32),
            pltpu.VMEM((2, GROUP, 3, 8, 128), F32),
            pltpu.VMEM((2, GROUP, 3, 8, 128), F32),
            pltpu.VMEM((GROUP, 3, 8, 128), F32),
            pltpu.VMEM((GROUP, 3, 8, 128), F32),
            pltpu.VMEM((2, 2, 3, 4, 128), F32),
            pltpu.VMEM((2, RING, 3, 4, 128), F32),
            pltpu.VMEM((2, GROUP, 3, 8, 128), F32),
            pltpu.VMEM((2, GROUP, 3, 8, 128), F32),
            pltpu.VMEM((2, GROUP, 2, 2, 3, 128), F32),
            pltpu.VMEM((2, GROUP, LINE - 3, 3, 128), F32),
            pltpu.VMEM((2, GROUP, 2, 2, 3, 128), F32),
            pltpu.VMEM((2, 4, 3, ROWS, 256), F32),
            pltpu.VMEM((2, LINE - 1, 3, ROWS, 256), F32),
            pltpu.VMEM((2, 2, 3, ROWS, 256), F32),
            pltpu.VMEM((LINE, 8, 128), F32),
            pltpu.VMEM((GROUP, 8, 128), F32),
            pltpu.VMEM((RING, 8, 128), F32),
            pltpu.SemaphoreType.REGULAR((1 + GROUP,)),
            dma((8,)),
            dma((2, GROUP)), dma((2, GROUP)),
            dma((2, RING)), dma((2, RING)),
            dma((2, GROUP)), dma((2, GROUP)),
            dma((2,)), dma((2,)), dma((2,)), dma((2,)),
            dma((2, LINE - 1)), dma((2, LINE - 1)),
            dma((2, 2)), dma((2, 2)),
            dma((LINE,)), dma((LINE,)),
            dma((GROUP,)), dma((GROUP,)),
            dma((RING,)), dma((RING,)),
        ],
        compiler_params=pltpu.CompilerParams(collective_id=0, has_side_effects=True, vmem_limit_bytes=RESERVED),
        name="closure_step",
    )(
        velocity, cotangent, weight_in, bias_in.reshape(1, UNITS), weight_out.T,
        jnp.asarray(smoothing_table()).reshape(GROUP * RING, 1, 128), jnp.asarray(line_table()),
        jnp.asarray(depth_table(field[3])),
    )
    outs = pl.pallas_call(
        finish,
        out_shape=(
            jax.ShapeDtypeStruct(field, F32),
            jax.ShapeDtypeStruct(field, F32),
            jax.ShapeDtypeStruct((6, UNITS), F32),
            jax.ShapeDtypeStruct((1, UNITS), F32),
            jax.ShapeDtypeStruct((3, UNITS), F32),
        ),
        in_specs=[whole] * 3,
        out_specs=(anywhere, anywhere, whole, whole, whole),
        scratch_shapes=[dma((2,))],
        compiler_params=pltpu.CompilerParams(vmem_limit_bytes=1 << 20),
        name="finish",
    )(*mid)
    return outs[0], outs[1], outs[2], outs[3].reshape(UNITS), outs[4].T


def solution(mesh):
    in_specs = (P(None, "gx", "gy", None), P(None, "gx", "gy", None), P(), P(), P())
    out_specs = (P(None, "gx", "gy", None), P(None, "gx", "gy", None), P(), P(), P())
    return jax.shard_map(local, mesh=mesh, in_specs=in_specs, out_specs=out_specs, check_vma=False)
```

```python
import functools

import jax
import jax.numpy as jnp
import ml_dtypes
import numpy as np
from jax import lax
from jax.experimental import pallas as pl
from jax.experimental.pallas import tpu as pltpu
from jax.sharding import PartitionSpec as P

FILTER_ALPHA = 0.499
FILTER_GAIN = 0.5 + FILTER_ALPHA
COMPACT_ALPHA = 1.0 / 3.0
STEP_SIZE = 0.5
MESH = pl.DeviceIdType.MESH
F32 = jnp.float32
BF16 = jnp.bfloat16

GROUP = 4
RING = 16
LINE = 8
ROWS = 4
UNITS = 64
RESERVED = 66300000

UP_W, DOWN_W, UP_C, DOWN_C, RING_L, RING_R, BACK_L, BACK_R, LOCAL, LEFT, RIGHT = (
    0, 4, 8, 12, 16, 32, 48, 68, 88, 104, 108
)


def tridiagonal(length, coupling):
    return np.eye(length) + coupling * (np.eye(length, k=1) + np.eye(length, k=-1))


def smoothing_table():
    devices = GROUP * RING
    length = devices * ROWS
    matrix = tridiagonal(length, FILTER_ALPHA)
    inverse = np.linalg.inv(matrix)
    smoothing = np.linalg.solve(matrix, FILTER_GAIN * tridiagonal(length, 0.5))

    def move(row, pivot):
        return inverse[row, pivot] / inverse[pivot, pivot]

    table = np.zeros((devices, 128))
    block = GROUP * ROWS
    for device in range(devices):
        ring, member = divmod(device, GROUP)
        first = device * ROWS
        last = first + ROWS - 1
        entry = table[device]
        if device < devices - 1:
            entry[UP_W:UP_W + ROWS] = smoothing[last + 1, first:first + ROWS]
        if device > 0:
            entry[DOWN_W:DOWN_W + ROWS] = smoothing[first - 1, first:first + ROWS]
        group_first = ring * block
        group_last = group_first + block - 1
        for other in range(GROUP):
            start = group_first + other * ROWS
            if ring < RING - 1:
                entry[UP_C + other] = move(group_last + 1, start + ROWS)
            if ring > 0:
                entry[DOWN_C + other] = move(group_first - 1, start - 1)
        for other in range(RING):
            if other < ring:
                entry[RING_L + other] = move(group_first, (other + 1) * block)
            if other > ring:
                entry[RING_R + other] = move(group_last, other * block - 1)
        for target in range(GROUP):
            own_first = group_first + target * ROWS
            own_last = own_first + ROWS - 1
            entry[BACK_L + 5 * target] = move(own_first, group_first)
            entry[BACK_R + 5 * target] = move(own_last, group_last)
            for other in range(GROUP):
                start = group_first + other * ROWS
                if other < target:
                    entry[BACK_L + 5 * target + 1 + other] = move(own_first, start + ROWS)
                if other > target:
                    entry[BACK_R + 5 * target + 1 + other] = move(own_last, start - 1)
        entry[LOCAL:LOCAL + ROWS * ROWS] = smoothing[first:last + 1, first:last + 1].reshape(-1)
        for row in range(ROWS):
            entry[LEFT + row] = move(first + row, first)
            entry[RIGHT + row] = move(first + row, last)
    return table.astype(np.float32)


def derivative_matrix(length):
    right = 7.0 / 9.0 * (np.eye(length, k=1) - np.eye(length, k=-1)) + 1.0 / 36.0 * (
        np.eye(length, k=2) - np.eye(length, k=-2)
    )
    return np.linalg.solve(tridiagonal(length, COMPACT_ALPHA), right)


def line_table():
    size = 8
    length = LINE * size
    forward = derivative_matrix(length)
    table = np.zeros((LINE, size, 128))
    for place, matrix in enumerate((forward, forward.T)):
        base = 24 * place
        for device in range(LINE):
            rows = slice(device * size, device * size + size)
            table[device, :, base:base + 8] = matrix[rows, rows]
            if device < LINE - 1:
                table[device, 0, base + 8:base + 16] = matrix[device * size + 8, rows]
                table[device, 1, base + 8:base + 16] = matrix[device * size + 9, rows]
            if device > 0:
                table[device, 2, base + 8:base + 16] = matrix[device * size - 1, rows]
                table[device, 3, base + 8:base + 16] = matrix[device * size - 2, rows]
            for step in range(1, LINE):
                source = (device - step) % LINE
                columns = slice(source * size, source * size + size)
                pivot = source * size + 9 if source < device else source * size - 2
                sent = matrix[pivot, columns]
                factors = matrix[rows, columns] @ sent / (sent @ sent)
                if source == device - 1:
                    factors[0] = 0.0
                if source == device + 1:
                    factors[size - 1] = 0.0
                table[device, :, base + 16 + step] = factors
    table[1:, 0, 48] = 1.0
    table[:-1, size - 1, 49] = 1.0
    return table.astype(np.float32)


def split_table(matrix):
    high = matrix.astype(np.float32).astype(ml_dtypes.bfloat16)
    low = (matrix - high.astype(np.float64)).astype(np.float32).astype(ml_dtypes.bfloat16)
    return [high, low]


def depth_table(length):
    matrix = derivative_matrix(length)
    return np.stack(split_table(matrix.T.copy()) + split_table(matrix))


def split(values):
    high = values.astype(BF16)
    return high, (values - high.astype(F32)).astype(BF16)


def iota(shape, dim):
    return lax.broadcasted_iota(jnp.int32, shape, dim)


def ones_where(condition):
    return jnp.where(condition, 1.0, 0.0).astype(F32)


def matmul(a, b):
    return jnp.dot(a, b, preferred_element_type=F32)


def matmul_nt(a, b, precision=None):
    return lax.dot_general(a, b, (((1,), (1,)), ((), ())), precision=precision, preferred_element_type=F32)


def kernel(
    velocity, cotangent, weight_in, bias_in, weight_out, x_table, y_table, z_table,
    new_velocity, grad_velocity, grad_weights,
    w_in, w_bias, w_out, vel, cot, along_y, smoothed, feats, gfeats, pulled,
    scalars, columns, tall, ztab,
    left_lhs, out_lhs, back_lhs, force_lhs, rhs, pulled_out, hidden_buf, pre_buf, sums,
    x1_send, x1_recv, state, group_rows, x2_send, x2_recv, x3_send, x3_recv, plane_send, plane_recv, plane_edge,
    y_send, y_recv, y_edge,
    p1, p2, p3,
    token, local_sem, x1_ss, x1_rs, x2_ss, x2_rs, x3_ss, x3_rs, plane_ss, plane_rs, edge_ss, edge_rs,
    y_ss, y_rs, ye_ss, ye_rs,
    p1_ss, p1_rs, p2_ss, p2_rs, p3_ss, p3_rs,
):
    gx = lax.axis_index("gx")
    gy = lax.axis_index("gy")
    ring = lax.div(gx, GROUP)
    member = lax.rem(gx, GROUP)

    def in_group(step):
        return lax.rem(member + step, GROUP)

    def in_ring(step):
        return lax.rem(ring + step, RING)

    def in_line(step):
        return lax.rem(gy + step, LINE)

    def group_device(other):
        return (ring * GROUP + other, gy)

    def ring_device(other):
        return (other * GROUP + member, gy)

    def line_device(other):
        return (gx, other)

    def plane_device(other, place):
        return (ring * GROUP + other, place)

    barrier = pltpu.get_barrier_semaphore()
    half = RING // 4
    partners = (
        [ring_device(in_ring(step)) for step in (4, 12, 3, 13, 2, 14, 1, 15)]
        + [line_device(in_line(step)) for step in range(1, LINE)]
        + [group_device(in_group(step)) for step in range(1, GROUP)]
    )
    for partner in partners:
        pl.semaphore_signal(barrier, inc=1, device_id=partner, device_id_type=MESH)

    loads = [
        pltpu.make_async_copy(x_table.at[gx], scalars, local_sem.at[0]),
        pltpu.make_async_copy(velocity, vel, local_sem.at[1]),
        pltpu.make_async_copy(y_table.at[gy], columns, local_sem.at[2]),
        pltpu.make_async_copy(weight_in, w_in, local_sem.at[3]),
        pltpu.make_async_copy(bias_in, w_bias, local_sem.at[4]),
        pltpu.make_async_copy(weight_out, w_out, local_sem.at[5]),
        pltpu.make_async_copy(cotangent, cot, local_sem.at[6]),
        pltpu.make_async_copy(z_table, ztab, local_sem.at[7]),
    ]
    for load in loads:
        load.start()

    def remote(src, dst, send_sem, recv_sem, device):
        return pltpu.make_async_remote_copy(
            src_ref=src, dst_ref=dst, send_sem=send_sem, recv_sem=recv_sem, device_id=device, device_id_type=MESH
        )

    sent = []

    def send(*args, drain=True):
        copy = remote(*args)
        copy.start()
        if drain:
            sent.append(copy)

    def drain(count):
        for copy in sent[:count]:
            copy.wait_send()
        del sent[:count]

    def scalar(index):
        return scalars[0, index]

    def build_weights():
        for load in loads[3:6]:
            load.wait()
        w_high, w_low = split(w_in[...])
        spread = ones_where(lax.shift_right_logical(iota((512, UNITS), 0), 3) == iota((512, UNITS), 1)).astype(BF16)
        spread_t = ones_where(iota((UNITS, 512), 0) == lax.shift_right_logical(iota((UNITS, 512), 1), 3)).astype(BF16)
        bias = w_bias[...]
        b_high, b_low = split(bias)
        b_rest = bias - b_high.astype(F32) - b_low.astype(F32)
        row = iota((8, 160), 0)
        col = iota((8, 160), 1)
        field = lax.shift_right_logical(col, 3)
        pick_high = ones_where(((field == row) | (field == row + 6)) & (row < 6)).astype(BF16)
        pick_low = ones_where((field == row + 12) & (row < 6)).astype(BF16)
        spread_high = matmul_nt(spread, w_high).astype(BF16)
        spread_low = matmul_nt(spread, w_low).astype(BF16)
        top = matmul(spread_high, pick_high[0:6]) + matmul(spread_low, pick_low[0:6])
        same = lax.bitwise_and(iota((512, 160), 0), 7) == lax.bitwise_and(iota((512, 160), 1), 7)
        top = jnp.where(same, top, 0.0)
        biases = jnp.concatenate([b_high.astype(F32), b_low.astype(F32), b_rest, jnp.zeros((5, UNITS), F32)], axis=0)
        spread_bias = matmul_nt(spread, biases.astype(BF16)).astype(BF16)
        top = top + matmul(spread_bias, ones_where(col == row + 144).astype(BF16))
        left_lhs[...] = top.astype(BF16)
        o_high, o_low = split(w_out[...])
        row, field, same = row[:, 0:96], field[:, 0:96], same[:, 0:96]
        pick_high = ones_where(((field == row) | (field == row + 4)) & (row < 3)).astype(BF16)
        pick_low = ones_where((field == row + 8) & (row < 3)).astype(BF16)
        spread_oh = matmul_nt(spread, o_high).astype(BF16)
        spread_ol = matmul_nt(spread, o_low).astype(BF16)
        bottom = matmul(spread_oh, pick_high[0:3]) + matmul(spread_ol, pick_low[0:3])
        out_lhs[...] = jnp.where(same, bottom, 0.0).astype(BF16)

        same_t = lax.bitwise_and(iota((96, 512), 0), 7) == lax.bitwise_and(iota((96, 512), 1), 7)
        row = lax.shift_right_logical(iota((96, 8), 0), 3)
        col = iota((96, 8), 1)
        get_high = ones_where((row == col) & (col < 6)).astype(BF16)
        get_low = ones_where((row == col + 6) & (col < 6)).astype(BF16)
        tall_w = matmul(get_high[:, 0:6], w_high) + matmul(get_low[:, 0:6], w_low)
        back_lhs[...] = jnp.where(same_t, matmul(tall_w.astype(BF16), spread_t), 0.0).astype(BF16)
        get_high = ones_where((row[0:64] == col[0:64]) & (col[0:64] < 3)).astype(BF16)
        get_low = ones_where((row[0:64] == col[0:64] + 4) & (col[0:64] < 3)).astype(BF16)
        tall_o = matmul(get_high[:, 0:3], o_high) + matmul(get_low[:, 0:3], o_low)
        force_lhs[...] = jnp.where(same_t[0:64], matmul(tall_o.astype(BF16), spread_t), 0.0).astype(BF16)

    def build_columns():
        loads[2].wait()
        line_columns = columns[...]
        for index in range(50):
            tall[index] = jnp.broadcast_to(line_columns[:, index:index + 1], (8, 128))

    def tall_column(index):
        half = tall[index]
        return jnp.concatenate([half, half], axis=1)

    lower = iota((8, 128), 1) < 64

    def turn(tile):
        return pltpu.roll(tile, 64, 1)

    def pack(left, right, piece):
        lanes = slice(128 * (piece // 2), 128 * (piece // 2) + 128)
        if piece % 2 == 0:
            return jnp.where(lower, left[:, lanes], turn(right[:, lanes]))
        return jnp.where(lower, turn(left[:, lanes]), right[:, lanes])

    def unpack(pieces):
        left = [jnp.where(lower, pieces[2 * t], turn(pieces[2 * t + 1])) for t in range(2)]
        right = [jnp.where(lower, turn(pieces[2 * t]), pieces[2 * t + 1]) for t in range(2)]
        return jnp.concatenate(left, axis=1), jnp.concatenate(right, axis=1)

    def two_scalars(left_index, right_index):
        return jnp.where(lower, scalar(left_index), scalar(right_index))

    def states(rows):
        return [sum(scalar(base + row) * rows[row] for row in range(ROWS)) for base in (UP_W, DOWN_W)]

    def local_rows(rows):
        return [
            sum(scalar(LOCAL + ROWS * row + col) * rows[col] for col in range(ROWS)) for row in range(ROWS)
        ]

    def pieces_send(source, target, send_sems, recv_sems, order):
        for step in (2, 1, 3):
            other = in_group(step)
            send(
                source.at[order, other], target.at[order, member],
                send_sems.at[order, other], recv_sems.at[order, member], group_device(other),
            )

    def pieces_wait(source, target, send_sems, recv_sems, order):
        for step in range(1, GROUP):
            other = in_group(step)
            remote(
                source.at[order, other], target.at[order, other],
                send_sems.at[order, other], recv_sems.at[order, other], group_device(other),
            ).wait_recv()

    def ring_send(order, load):
        gathered = []
        for comp in range(3):
            gathered.append(sum(
                two_scalars(UP_C + other, DOWN_C + other) * load(other, comp) for other in range(GROUP)
            ))
        first, second, third = gathered
        turned = turn(third)
        front = jnp.where(lower, first, turn(second))
        x2_send[order, 0, 0] = front[0:4]
        x2_send[order, 0, 1] = front[4:8]
        x2_send[order, 0, 2] = jnp.where(lower[0:4], third[0:4], turned[4:8])
        front = jnp.where(lower, turn(first), second)
        x2_send[order, 1, 0] = front[0:4]
        x2_send[order, 1, 1] = front[4:8]
        x2_send[order, 1, 2] = jnp.where(lower[0:4], turned[0:4], third[4:8])
        for step in (8, 7, 9, 6, 10, 5, 11, 4, 12, 3, 13, 2, 14, 1, 15):
            other = in_ring(step)
            kind = jnp.where(other > ring, 0, 1)
            send(
                x2_send.at[order, kind], x2_recv.at[order, ring],
                x2_ss.at[order, other], x2_rs.at[order, ring], ring_device(other),
            )

    def ring_receive(order):
        left = jnp.zeros((3, 4, 128), F32)
        right = jnp.zeros((3, 4, 128), F32)
        for step in (1, 15, 2, 14, 3, 13, 4, 12, 5, 11, 6, 10, 7, 9, 8):
            other = in_ring(step)
            remote(
                x2_send.at[order, 0], x2_recv.at[order, other],
                x2_ss.at[order, other], x2_rs.at[order, other], ring_device(other),
            ).wait_recv()
            part = x2_recv[order, other]
            left = left + scalar(RING_L + other) * part
            right = right + scalar(RING_R + other) * part
        front_left = jnp.concatenate([left[0], left[1]], axis=0)
        front_right = jnp.concatenate([right[0], right[1]], axis=0)
        back_left = jnp.concatenate([left[2], pltpu.roll(left[2], 64, 1)], axis=0)
        back_right = jnp.concatenate([pltpu.roll(right[2], 64, 1), right[2]], axis=0)
        return [
            jnp.where(lower, front_left, turn(front_right)),
            jnp.where(lower, turn(front_left), front_right),
            jnp.where(lower, back_left, back_right),
        ]

    def group_part(load, other, comp):
        total = jnp.zeros((8, 128), F32)
        for source in range(GROUP):
            index = 5 * other + 1 + source
            total = total + two_scalars(BACK_L + index, BACK_R + index) * load(source, comp)
        return total

    def ring_factor(other):
        return two_scalars(BACK_L + 5 * other, BACK_R + 5 * other)

    def projected(order, tile):
        return sum(tall[24 * order + 8 + col] * tile[col:col + 1] for col in range(8))

    def keep_rows(order, other, comp, out):
        for kind in range(4):
            plane_send[order, other, kind // 2, kind % 2, comp:comp + 1, :] = out[kind:kind + 1]

    def plane_rows_send(order, steps):
        for step in steps:
            other = in_group(step)
            for along in (4, 5, 3, 6, 2, 7, 1):
                place = in_line(along)
                side = jnp.where(place > gy, 0, 1)
                if along in (1, LINE - 1):
                    send(
                        plane_send.at[order, other, side], plane_edge.at[order, member, 0 if along == 1 else 1],
                        edge_ss.at[order], edge_rs.at[order], plane_device(other, place), drain=False,
                    )
                else:
                    send(
                        plane_send.at[order, other, side, 1], plane_recv.at[order, member, along - 2],
                        plane_ss.at[order], plane_rs.at[order], plane_device(other, place), drain=False,
                    )

    def plane_rows_all(order):
        device = plane_device(in_group(1), in_line(1))
        return (
            remote(plane_recv.at[order], plane_recv.at[order], plane_ss.at[order], plane_rs.at[order], device),
            remote(plane_edge.at[order], plane_edge.at[order], edge_ss.at[order], edge_rs.at[order], device),
        )

    def plane_rows_wait(order):
        for copy in plane_rows_all(order):
            copy.wait_recv()

    def plane_rows_drain(order):
        for copy in plane_rows_all(order):
            copy.wait_send()

    def from_plane(order, source, comp):
        def row(ref, *index):
            return ref[(order, source) + index + (slice(comp, comp + 1),)]

        factor = 24 * order + 16
        total = tall[48] * row(plane_edge, 0, 0) + tall[factor + 1] * row(plane_edge, 0, 1)
        total = total + tall[49] * row(plane_edge, 1, 0) + tall[factor + LINE - 1] * row(plane_edge, 1, 1)
        for along in range(2, LINE - 1):
            total = total + tall[factor + along] * row(plane_recv, along - 2)
        return total

    def own_block(order, tile):
        return sum(tall[24 * order + col] * tile[col:col + 1] for col in range(8))

    def line_send(load, order):
        base = 24 * order
        sent_columns = [tall_column(base + 8 + col) for col in range(8)]
        for comp in range(3):
            for row in range(ROWS):
                tile = load(comp, row)
                out = sum(sent_columns[col] * tile[col:col + 1] for col in range(8))
                for kind in range(4):
                    y_send[order, kind, comp, row:row + 1, :] = out[kind:kind + 1]
        for kind, step in ((0, 1), (1, LINE - 1)):
            send(
                y_send.at[order, 2 * kind], y_edge.at[order, kind],
                ye_ss.at[order, kind], ye_rs.at[order, kind], line_device(in_line(step)),
            )
        for step in (4, 5, 3, 2, 6, 1, 7):
            other = in_line(step)
            kind = jnp.where(other > gy, 1, 3)
            send(
                y_send.at[order, kind], y_recv.at[order, step - 1],
                y_ss.at[order, step - 1], y_rs.at[order, step - 1], line_device(other),
            )

    def line_local(load, order, store):
        base = 24 * order
        local_columns = [tall_column(base + col) for col in range(8)]
        for comp in range(3):
            for row in range(ROWS):
                tile = load(comp, row)
                store(comp, row, sum(local_columns[col] * tile[col:col + 1] for col in range(8)))

    def line_receive(order, load, store):
        base = 24 * order
        for kind, step in ((0, LINE - 1), (1, 1)):
            remote(
                y_send.at[order, 0], y_edge.at[order, kind],
                ye_ss.at[order, kind], ye_rs.at[order, kind], line_device(in_line(step)),
            ).wait_recv()
        for step in range(1, LINE):
            remote(
                y_send.at[order, 1], y_recv.at[order, step - 1],
                y_ss.at[order, step - 1], y_rs.at[order, step - 1], line_device(in_line(step)),
            ).wait_recv()
        factors = [tall_column(base + 16 + step) for step in range(1, LINE)]
        first = tall_column(48)
        last = tall_column(49)
        for comp in range(3):
            for row in range(ROWS):
                total = load(comp, row)
                total = total + first * y_edge[order, 0, comp, row:row + 1, :]
                total = total + last * y_edge[order, 1, comp, row:row + 1, :]
                for step in range(1, LINE):
                    total = total + factors[step - 1] * y_recv[order, step - 1, comp, row:row + 1, :]
                store(comp, row, total)

    def depth_apply(values, order):
        high, low = split(values)
        both = matmul(jnp.concatenate([high, low], axis=0), ztab[2 * order])
        count = values.shape[0]
        return both[0:count] + both[count:2 * count] + matmul(high, ztab[2 * order + 1])

    def pass_tokens():
        pl.semaphore_wait(barrier, len(partners))
        for kind, step in ((0, half), (1, RING - half)):
            pl.semaphore_signal(
                token.at[kind], inc=1, device_id=ring_device(in_ring(step)), device_id_type=MESH
            )

        for step in range(1, GROUP):
            pl.semaphore_signal(
                token.at[1 + step], inc=1, device_id=group_device(in_group(step)), device_id_type=MESH
            )

    def wait_tokens(first, last):
        for kind in range(first, last):
            pl.semaphore_wait(token.at[kind], 1)

    loads[0].wait()
    loads[1].wait()
    for comp in range(3):
        left, right = states([vel[comp, row] for row in range(ROWS)])
        for piece in range(GROUP):
            x1_send[0, piece, comp] = pack(left, right, piece)
    build_columns()
    pass_tokens()
    pieces_send(x1_send, x1_recv, x1_ss, x1_rs, 0)
    line_send(lambda comp, row: vel[comp, row], 0)
    x1_recv[0, member] = x1_send[0, member]
    build_weights()
    for load in loads[6:]:
        load.wait()

    def keep_along(comp, row, value):
        along_y[comp, row] = value

    line_local(lambda comp, row: vel[comp, row], 0, keep_along)
    pieces_wait(x1_send, x1_recv, x1_ss, x1_rs, 0)
    wait_tokens(0, 2)

    def first_piece(source, comp):
        return x1_recv[0, source, comp]

    ring_send(0, first_piece)
    line_receive(0, lambda comp, row: along_y[comp, row], keep_along)
    for comp in range(3):
        for row, value in enumerate(local_rows([vel[comp, row] for row in range(ROWS)])):
            smoothed[comp, row] = value
        for row, value in enumerate(local_rows([along_y[comp, row] for row in range(ROWS)])):
            feats[row, 8 * comp:8 * comp + 8, :] = value
    def outward(row):
        parts = [STEP_SIZE * cot[comp, row] for comp in range(3)]
        return jnp.concatenate(parts + [jnp.zeros((8, 256), F32)], axis=0)

    def grad_of_hidden(row, carry):
        out_high, out_low = split(outward(row))
        pulled_out[row] = matmul(out_lhs[...], jnp.concatenate([out_high, out_low, out_high], axis=0))
        rhs[row, 144:160, :] = jnp.ones((16, 256), BF16)
        return carry

    lax.fori_loop(0, ROWS, grad_of_hidden, 0)
    wait_tokens(2, 1 + GROUP)
    for other in range(GROUP):
        for comp in range(3):
            tile = group_part(first_piece, other, comp)
            x3_send[0, other, comp] = tile
            group_rows[other, comp] = projected(0, tile)
    ring_state = ring_receive(0)
    ring_rows = [projected(0, ring_state[comp]) for comp in range(3)]
    for step in range(GROUP):
        other = in_group(step)
        factor = ring_factor(other)
        for comp in range(3):
            x3_send[0, other, comp] += factor * ring_state[comp]
            keep_rows(0, other, comp, group_rows[other, comp] + factor * ring_rows[comp])
    plane_rows_send(0, (2,))
    pieces_send(x3_send, x3_recv, x3_ss, x3_rs, 0)
    plane_rows_send(0, (1, 3, 0))
    x3_recv[0, member] = x3_send[0, member]
    pieces_wait(x3_send, x3_recv, x3_ss, x3_rs, 0)
    for comp in range(3):
        left, right = unpack([x3_recv[0, piece, comp] for piece in range(GROUP)])
        for row in range(ROWS):
            smoothed[comp, row] += scalar(LEFT + row) * left + scalar(RIGHT + row) * right
    along_z = depth_apply(smoothed[...].reshape(96, 256), 0)
    for comp in range(3):
        for row in range(ROWS):
            start = (comp * ROWS + row) * 8
            feats[row, 24 + 8 * comp:32 + 8 * comp, :] = along_z[start:start + 8]
    for piece in range(GROUP):
        for comp in range(3):
            state[piece, comp] = own_block(0, x3_recv[0, piece, comp])
    plane_rows_wait(0)
    for comp in range(3):
        left, right = unpack([state[piece, comp] + from_plane(0, piece, comp) for piece in range(GROUP)])
        for row in range(ROWS):
            feats[row, 8 * comp:8 * comp + 8, :] += scalar(LEFT + row) * left + scalar(RIGHT + row) * right

    def closure(row):
        feature_high, feature_low = split(feats[row])
        rhs[row, 0:48, :] = feature_high
        rhs[row, 48:96, :] = feature_low
        rhs[row, 96:144, :] = feature_high
        hidden = jnp.tanh(matmul(left_lhs[...], rhs[row]))
        grad_pre = pulled_out[row] * (1.0 - hidden * hidden)
        pre_high, pre_low = split(grad_pre)
        hidden_buf[row] = hidden
        pre_buf[row, 0] = pre_high
        pre_buf[row, 1] = pre_low
        both = matmul(back_lhs[...], pre_high)
        gfeats[row] = both[0:48] + both[48:96] + matmul(back_lhs[0:48, :], pre_low)

    for row in range(ROWS):
        closure(row)

    def grad_along_y(comp, row):
        return gfeats[row, 8 * comp:8 * comp + 8, :]

    packed = {}
    for comp in range(3):
        left, right = states([grad_along_y(comp, row) for row in range(ROWS)])
        for piece in range(GROUP):
            packed[piece, comp] = pack(left, right, piece)
            keep_rows(1, piece, comp, projected(1, packed[piece, comp]))
    plane_rows_send(1, (2, 1, 3, 0))
    back_in = jnp.concatenate(
        [gfeats[row, 24 + 8 * comp:32 + 8 * comp, :] for comp in range(3) for row in range(ROWS)], axis=0
    )
    along_z = depth_apply(back_in, 1)
    for comp in range(3):
        starts = [(comp * ROWS + row) * 8 for row in range(ROWS)]
        left, right = states([along_z[start:start + 8] for start in starts])
        for piece in range(GROUP):
            x1_send[1, piece, comp] = own_block(1, packed[piece, comp]) + pack(left, right, piece)
        for row in range(ROWS):
            pulled[comp, row] = along_z[starts[row]:starts[row] + 8]
    pieces_send(x1_send, x1_recv, x1_ss, x1_rs, 1)
    x1_recv[1, member] = x1_send[1, member]

    def keep_pulled(comp, row, value):
        pulled[comp, row] = value

    def line_part():
        line_send(grad_along_y, 1)
        line_local(grad_along_y, 1, lambda comp, row, value: keep_pulled(comp, row, pulled[comp, row] + value))

    def forces(row, carry):
        hidden_high, hidden_low = split(hidden_buf[row])
        both = matmul(force_lhs[...], hidden_high)
        forcing = both[0:32] + both[32:64] + matmul(force_lhs[0:32, :], hidden_low)
        for comp in range(3):
            new_velocity[comp, row] = vel[comp, row] + STEP_SIZE * forcing[8 * comp:8 * comp + 8]
        return carry

    def row_sums(row, carry):
        hidden_high, hidden_low = split(hidden_buf[row])
        feature_high, feature_low = split(feats[row])
        ones = jnp.ones((16, 256), BF16)
        both = matmul_nt(jnp.concatenate([feature_high, ones, feature_low], axis=0), pre_buf[row, 0])
        rest = matmul_nt(jnp.concatenate([feature_high, ones], axis=0), pre_buf[row, 1])
        sums[0:48, :] += both[0:48] + both[64:112] + rest[0:48]
        sums[48:56, :] += both[48:56] + rest[48:56]
        out_high, out_low = split(outward(row))
        both = matmul_nt(jnp.concatenate([out_high, out_low], axis=0), hidden_high)
        rest = matmul_nt(out_high, hidden_low)
        sums[56:88, :] += both[0:32] + both[32:64] + rest
        return carry

    def partial_sums():
        sums[...] = jnp.zeros((88, 512), F32)
        lax.fori_loop(0, ROWS, row_sums, 0)
        same = lax.bitwise_and(iota((88, 512), 0), 7) == lax.bitwise_and(iota((88, 512), 1), 7)
        gather = ones_where(lax.shift_right_logical(iota((512, UNITS), 0), 3) == iota((512, UNITS), 1)).astype(BF16)
        high, low = split(jnp.where(same, sums[...], 0.0))
        narrow = matmul(high, gather) + matmul(low, gather)
        folded = [jnp.sum(narrow[8 * part:8 * part + 8], axis=0, keepdims=True) for part in range(11)]
        front = jnp.concatenate(folded[0:8], axis=0)
        back = jnp.concatenate(folded[8:11] + [jnp.zeros((5, UNITS), F32)], axis=0)
        p1[gy] = jnp.concatenate([front, back], axis=1)
        for step in range(1, LINE):
            other = in_line(step)
            send(p1.at[gy], p1.at[gy], p1_ss.at[other], p1_rs.at[gy], line_device(other))

    def sum_line():
        for step in range(1, LINE):
            other = in_line(step)
            remote(p1.at[other], p1.at[other], p1_ss.at[other], p1_rs.at[other], line_device(other)).wait_recv()
        total = p1[0]
        for other in range(1, LINE):
            total = total + p1[other]
        p2[member] = total
        for step in range(1, GROUP):
            other = in_group(step)
            send(p2.at[member], p2.at[member], p2_ss.at[other], p2_rs.at[member], group_device(other))

    def sum_group():
        for step in range(1, GROUP):
            other = in_group(step)
            remote(p2.at[other], p2.at[other], p2_ss.at[other], p2_rs.at[other], group_device(other)).wait_recv()
        total = p2[0]
        for other in range(1, GROUP):
            total = total + p2[other]
        p3[ring] = total
        for step in (8, 7, 9, 6, 10, 5, 11, 4, 12, 3, 13, 2, 14, 1, 15):
            other = in_ring(step)
            send(p3.at[ring], p3.at[ring], p3_ss.at[other], p3_rs.at[ring], ring_device(other))

    def sum_ring():
        for step in range(1, RING):
            other = in_ring(step)
            remote(p3.at[other], p3.at[other], p3_ss.at[other], p3_rs.at[other], ring_device(other)).wait_recv()
        total = p3[0]
        for other in range(1, RING):
            total = total + p3[other]
        grad_weights[...] = total * (1.0 / float(256 * 64 * 256))

    partial_sums()
    line_part()
    pieces_wait(x1_send, x1_recv, x1_ss, x1_rs, 1)
    plane_rows_wait(1)
    for source in range(GROUP):
        for comp in range(3):
            state[source, comp] = x1_recv[1, source, comp] + from_plane(1, source, comp)

    def second_piece(source, comp):
        return state[source, comp]

    early = len(sent)
    ring_send(1, second_piece)
    sum_line()
    lax.fori_loop(0, ROWS, forces, 0)
    line_receive(1, lambda comp, row: pulled[comp, row], keep_pulled)
    for comp in range(3):
        for row, value in enumerate(local_rows([pulled[comp, row] for row in range(ROWS)])):
            grad_velocity[comp, row] = cot[comp, row] + value
    sum_group()
    for other in range(GROUP):
        for comp in range(3):
            x3_send[1, other, comp] = group_part(second_piece, other, comp)
    drain(early)
    plane_rows_drain(0)
    plane_rows_drain(1)
    ring_state = ring_receive(1)
    for step in range(GROUP):
        other = in_group(step)
        factor = ring_factor(other)
        for comp in range(3):
            x3_send[1, other, comp] += factor * ring_state[comp]
    pieces_send(x3_send, x3_recv, x3_ss, x3_rs, 1)
    x3_recv[1, member] = x3_send[1, member]
    pieces_wait(x3_send, x3_recv, x3_ss, x3_rs, 1)
    for comp in range(3):
        left, right = unpack([x3_recv[1, piece, comp] for piece in range(GROUP)])
        for row in range(ROWS):
            grad_velocity[comp, row] += scalar(LEFT + row) * left + scalar(RIGHT + row) * right
    sum_ring()
    drain(len(sent))


def finish(
    new_velocity_in, grad_velocity_in, grads, new_velocity, grad_velocity, grad_in, grad_bias, grad_out_t,
    small_in, small_bias, small_out, sems,
):
    copies = [
        pltpu.make_async_copy(source.at[comp], target.at[comp], sems.at[2 * comp + place])
        for comp in range(3)
        for place, (source, target) in enumerate(((new_velocity_in, new_velocity), (grad_velocity_in, grad_velocity)))
    ]
    for copy in copies:
        copy.start()
    front = grads[:, 0:UNITS]
    small_in[...] = front[0:6]
    small_bias[...] = front[6:7]
    small_out[0:1] = front[7:8]
    small_out[1:3] = grads[0:2, UNITS:2 * UNITS]
    small = ((small_in, grad_in), (small_bias, grad_bias), (small_out, grad_out_t))
    for place, (source, target) in enumerate(small):
        copies.append(pltpu.make_async_copy(source, target, sems.at[6 + place]))
        copies[-1].start()
    for copy in copies:
        copy.wait()


def local(velocity, cotangent, weight_in, bias_in, weight_out):
    field = velocity.shape
    dma = pltpu.SemaphoreType.DMA
    anywhere = pl.BlockSpec(memory_space=pl.ANY)
    whole = pl.BlockSpec(memory_space=pltpu.VMEM)
    mid = pl.pallas_call(
        kernel,
        out_shape=(
            pltpu.VMEM(field, F32),
            pltpu.VMEM(field, F32),
            pltpu.VMEM((8, 128), F32),
        ),
        in_specs=[anywhere] * 8,
        out_specs=(whole, whole, whole),
        scratch_shapes=[
            pltpu.VMEM((6, UNITS), F32),
            pltpu.VMEM((1, UNITS), F32),
            pltpu.VMEM((3, UNITS), F32),
            pltpu.VMEM(field, F32),
            pltpu.VMEM(field, F32),
            pltpu.VMEM(field, F32),
            pltpu.VMEM(field, F32),
            pltpu.VMEM((ROWS, 48, 256), F32),
            pltpu.VMEM((ROWS, 48, 256), F32),
            pltpu.VMEM(field, F32),
            pltpu.SMEM((1, 128), F32),
            pltpu.VMEM((8, 128), F32),
            pltpu.VMEM((50, 8, 128), F32),
            pltpu.VMEM((4, 256, 256), BF16),
            pltpu.VMEM((512, 160), BF16),
            pltpu.VMEM((512, 96), BF16),
            pltpu.VMEM((96, 512), BF16),
            pltpu.VMEM((64, 512), BF16),
            pltpu.VMEM((ROWS, 160, 256), BF16),
            pltpu.VMEM((ROWS, 512, 256), F32),
            pltpu.VMEM((ROWS, 512, 256), F32),
            pltpu.VMEM((ROWS, 2, 512, 256), BF16),
            pltpu.VMEM((88, 512), F32),
            pltpu.VMEM((2, GROUP, 3, 8, 128), F32),
            pltpu.VMEM((2, GROUP, 3, 8, 128), F32),
            pltpu.VMEM((GROUP, 3, 8, 128), F32),
            pltpu.VMEM((GROUP, 3, 8, 128), F32),
            pltpu.VMEM((2, 2, 3, 4, 128), F32),
            pltpu.VMEM((2, RING, 3, 4, 128), F32),
            pltpu.VMEM((2, GROUP, 3, 8, 128), F32),
            pltpu.VMEM((2, GROUP, 3, 8, 128), F32),
            pltpu.VMEM((2, GROUP, 2, 2, 3, 128), F32),
            pltpu.VMEM((2, GROUP, LINE - 3, 3, 128), F32),
            pltpu.VMEM((2, GROUP, 2, 2, 3, 128), F32),
            pltpu.VMEM((2, 4, 3, ROWS, 256), F32),
            pltpu.VMEM((2, LINE - 1, 3, ROWS, 256), F32),
            pltpu.VMEM((2, 2, 3, ROWS, 256), F32),
            pltpu.VMEM((LINE, 8, 128), F32),
            pltpu.VMEM((GROUP, 8, 128), F32),
            pltpu.VMEM((RING, 8, 128), F32),
            pltpu.SemaphoreType.REGULAR((1 + GROUP,)),
            dma((8,)),
            dma((2, GROUP)), dma((2, GROUP)),
            dma((2, RING)), dma((2, RING)),
            dma((2, GROUP)), dma((2, GROUP)),
            dma((2,)), dma((2,)), dma((2,)), dma((2,)),
            dma((2, LINE - 1)), dma((2, LINE - 1)),
            dma((2, 2)), dma((2, 2)),
            dma((LINE,)), dma((LINE,)),
            dma((GROUP,)), dma((GROUP,)),
            dma((RING,)), dma((RING,)),
        ],
        compiler_params=pltpu.CompilerParams(collective_id=0, has_side_effects=True, vmem_limit_bytes=RESERVED),
        name="closure_step",
    )(
        velocity, cotangent, weight_in, bias_in.reshape(1, UNITS), weight_out.T,
        jnp.asarray(smoothing_table()).reshape(GROUP * RING, 1, 128), jnp.asarray(line_table()),
        jnp.asarray(depth_table(field[3])),
    )
    outs = pl.pallas_call(
        finish,
        out_shape=(
            jax.ShapeDtypeStruct(field, F32),
            jax.ShapeDtypeStruct(field, F32),
            jax.ShapeDtypeStruct((6, UNITS), F32),
            jax.ShapeDtypeStruct((1, UNITS), F32),
            jax.ShapeDtypeStruct((3, UNITS), F32),
        ),
        in_specs=[whole] * 3,
        out_specs=(anywhere,) * 5,
        scratch_shapes=[
            pltpu.VMEM((6, UNITS), F32),
            pltpu.VMEM((1, UNITS), F32),
            pltpu.VMEM((3, UNITS), F32),
            dma((9,)),
        ],
        compiler_params=pltpu.CompilerParams(vmem_limit_bytes=1 << 20),
        name="finish",
    )(*mid)
    return outs[0], outs[1], outs[2], outs[3].reshape(UNITS), outs[4].T


def solution(mesh):
    in_specs = (P(None, "gx", "gy", None), P(None, "gx", "gy", None), P(), P(), P())
    out_specs = (P(None, "gx", "gy", None), P(None, "gx", "gy", None), P(), P(), P())
    return jax.shard_map(local, mesh=mesh, in_specs=in_specs, out_specs=out_specs, check_vma=False)
```

```python
import functools

import jax
import jax.numpy as jnp
import ml_dtypes
import numpy as np
from jax import lax
from jax.experimental import pallas as pl
from jax.experimental.pallas import tpu as pltpu
from jax.sharding import PartitionSpec as P

FILTER_ALPHA = 0.499
FILTER_GAIN = 0.5 + FILTER_ALPHA
COMPACT_ALPHA = 1.0 / 3.0
STEP_SIZE = 0.5
MESH = pl.DeviceIdType.MESH
F32 = jnp.float32
BF16 = jnp.bfloat16

GROUP = 4
RING = 16
LINE = 8
ROWS = 4
UNITS = 64
RESERVED = 66300000

UP_W, DOWN_W, UP_C, DOWN_C, RING_L, RING_R, BACK_L, BACK_R, LOCAL, LEFT, RIGHT = (
    0, 4, 8, 12, 16, 32, 48, 68, 88, 104, 108
)


def tridiagonal(length, coupling):
    return np.eye(length) + coupling * (np.eye(length, k=1) + np.eye(length, k=-1))


def smoothing_table():
    devices = GROUP * RING
    length = devices * ROWS
    matrix = tridiagonal(length, FILTER_ALPHA)
    inverse = np.linalg.inv(matrix)
    smoothing = np.linalg.solve(matrix, FILTER_GAIN * tridiagonal(length, 0.5))

    def move(row, pivot):
        return inverse[row, pivot] / inverse[pivot, pivot]

    table = np.zeros((devices, 128))
    block = GROUP * ROWS
    for device in range(devices):
        ring, member = divmod(device, GROUP)
        first = device * ROWS
        last = first + ROWS - 1
        entry = table[device]
        if device < devices - 1:
            entry[UP_W:UP_W + ROWS] = smoothing[last + 1, first:first + ROWS]
        if device > 0:
            entry[DOWN_W:DOWN_W + ROWS] = smoothing[first - 1, first:first + ROWS]
        group_first = ring * block
        group_last = group_first + block - 1
        for other in range(GROUP):
            start = group_first + other * ROWS
            if ring < RING - 1:
                entry[UP_C + other] = move(group_last + 1, start + ROWS)
            if ring > 0:
                entry[DOWN_C + other] = move(group_first - 1, start - 1)
        for other in range(RING):
            if other < ring:
                entry[RING_L + other] = move(group_first, (other + 1) * block)
            if other > ring:
                entry[RING_R + other] = move(group_last, other * block - 1)
        for target in range(GROUP):
            own_first = group_first + target * ROWS
            own_last = own_first + ROWS - 1
            entry[BACK_L + 5 * target] = move(own_first, group_first)
            entry[BACK_R + 5 * target] = move(own_last, group_last)
            for other in range(GROUP):
                start = group_first + other * ROWS
                if other < target:
                    entry[BACK_L + 5 * target + 1 + other] = move(own_first, start + ROWS)
                if other > target:
                    entry[BACK_R + 5 * target + 1 + other] = move(own_last, start - 1)
        entry[LOCAL:LOCAL + ROWS * ROWS] = smoothing[first:last + 1, first:last + 1].reshape(-1)
        for row in range(ROWS):
            entry[LEFT + row] = move(first + row, first)
            entry[RIGHT + row] = move(first + row, last)
    return table.astype(np.float32)


def derivative_matrix(length):
    right = 7.0 / 9.0 * (np.eye(length, k=1) - np.eye(length, k=-1)) + 1.0 / 36.0 * (
        np.eye(length, k=2) - np.eye(length, k=-2)
    )
    return np.linalg.solve(tridiagonal(length, COMPACT_ALPHA), right)


def line_table():
    size = 8
    length = LINE * size
    forward = derivative_matrix(length)
    table = np.zeros((LINE, size, 128))
    for place, matrix in enumerate((forward, forward.T)):
        base = 24 * place
        for device in range(LINE):
            rows = slice(device * size, device * size + size)
            table[device, :, base:base + 8] = matrix[rows, rows]
            if device < LINE - 1:
                table[device, 0, base + 8:base + 16] = matrix[device * size + 8, rows]
                table[device, 1, base + 8:base + 16] = matrix[device * size + 9, rows]
            if device > 0:
                table[device, 2, base + 8:base + 16] = matrix[device * size - 1, rows]
                table[device, 3, base + 8:base + 16] = matrix[device * size - 2, rows]
            for step in range(1, LINE):
                source = (device - step) % LINE
                columns = slice(source * size, source * size + size)
                pivot = source * size + 9 if source < device else source * size - 2
                sent = matrix[pivot, columns]
                factors = matrix[rows, columns] @ sent / (sent @ sent)
                if source == device - 1:
                    factors[0] = 0.0
                if source == device + 1:
                    factors[size - 1] = 0.0
                table[device, :, base + 16 + step] = factors
    table[1:, 0, 48] = 1.0
    table[:-1, size - 1, 49] = 1.0
    return table.astype(np.float32)


def split_table(matrix):
    high = matrix.astype(np.float32).astype(ml_dtypes.bfloat16)
    low = (matrix - high.astype(np.float64)).astype(np.float32).astype(ml_dtypes.bfloat16)
    return [high, low]


def depth_table(length):
    matrix = derivative_matrix(length)
    return np.stack(split_table(matrix.T.copy()) + split_table(matrix))


def split(values):
    high = values.astype(BF16)
    return high, (values - high.astype(F32)).astype(BF16)


def iota(shape, dim):
    return lax.broadcasted_iota(jnp.int32, shape, dim)


def ones_where(condition):
    return jnp.where(condition, 1.0, 0.0).astype(F32)


def matmul(a, b):
    return jnp.dot(a, b, preferred_element_type=F32)


def matmul_nt(a, b, precision=None):
    return lax.dot_general(a, b, (((1,), (1,)), ((), ())), precision=precision, preferred_element_type=F32)


def kernel(
    velocity, cotangent, weight_in, bias_in, weight_out, x_table, y_table, z_table,
    new_velocity, grad_velocity, grad_weights,
    w_in, w_bias, w_out, vel, cot, along_y, smoothed, feats, gfeats, pulled,
    scalars, columns, tall, ztab,
    left_lhs, out_lhs, back_lhs, force_lhs, rhs, pulled_out, hidden_buf, pre_buf, sums,
    x1_send, x1_recv, state, group_rows, x2_send, x2_recv, x3_send, x3_recv, plane_send, plane_recv, plane_edge,
    y_send, y_recv, y_edge,
    p1, p2, p3,
    token, local_sem, x1_ss, x1_rs, x2_ss, x2_rs, x3_ss, x3_rs, plane_ss, plane_rs, edge_ss, edge_rs,
    y_ss, y_rs, ye_ss, ye_rs,
    p1_ss, p1_rs, p2_ss, p2_rs, p3_ss, p3_rs,
):
    gx = lax.axis_index("gx")
    gy = lax.axis_index("gy")
    ring = lax.div(gx, GROUP)
    member = lax.rem(gx, GROUP)

    def in_group(step):
        return lax.rem(member + step, GROUP)

    def in_ring(step):
        return lax.rem(ring + step, RING)

    def in_line(step):
        return lax.rem(gy + step, LINE)

    def group_device(other):
        return (ring * GROUP + other, gy)

    def ring_device(other):
        return (other * GROUP + member, gy)

    def line_device(other):
        return (gx, other)

    def plane_device(other, place):
        return (ring * GROUP + other, place)

    barrier = pltpu.get_barrier_semaphore()
    half = RING // 4
    partners = (
        [ring_device(in_ring(step)) for step in (4, 12, 3, 13, 2, 14, 1, 15)]
        + [line_device(in_line(step)) for step in range(1, LINE)]
        + [group_device(in_group(step)) for step in range(1, GROUP)]
    )
    for partner in partners:
        pl.semaphore_signal(barrier, inc=1, device_id=partner, device_id_type=MESH)

    loads = [
        pltpu.make_async_copy(x_table.at[gx], scalars, local_sem.at[0]),
        pltpu.make_async_copy(velocity, vel, local_sem.at[1]),
        pltpu.make_async_copy(y_table.at[gy], columns, local_sem.at[2]),
        pltpu.make_async_copy(weight_in, w_in, local_sem.at[3]),
        pltpu.make_async_copy(bias_in, w_bias, local_sem.at[4]),
        pltpu.make_async_copy(weight_out, w_out, local_sem.at[5]),
        pltpu.make_async_copy(cotangent, cot, local_sem.at[6]),
        pltpu.make_async_copy(z_table, ztab, local_sem.at[7]),
    ]
    for load in loads:
        load.start()

    def remote(src, dst, send_sem, recv_sem, device):
        return pltpu.make_async_remote_copy(
            src_ref=src, dst_ref=dst, send_sem=send_sem, recv_sem=recv_sem, device_id=device, device_id_type=MESH
        )

    sent = []

    def send(*args, drain=True):
        copy = remote(*args)
        copy.start()
        if drain:
            sent.append(copy)

    def drain(count):
        for copy in sent[:count]:
            copy.wait_send()
        del sent[:count]

    def scalar(index):
        return scalars[0, index]

    def build_weights():
        for load in loads[3:6]:
            load.wait()
        w_high, w_low = split(w_in[...])
        spread = ones_where(lax.shift_right_logical(iota((512, UNITS), 0), 3) == iota((512, UNITS), 1)).astype(BF16)
        spread_t = ones_where(iota((UNITS, 512), 0) == lax.shift_right_logical(iota((UNITS, 512), 1), 3)).astype(BF16)
        bias = w_bias[...]
        b_high, b_low = split(bias)
        b_rest = bias - b_high.astype(F32) - b_low.astype(F32)
        row = iota((8, 160), 0)
        col = iota((8, 160), 1)
        field = lax.shift_right_logical(col, 3)
        pick_high = ones_where(((field == row) | (field == row + 6)) & (row < 6)).astype(BF16)
        pick_low = ones_where((field == row + 12) & (row < 6)).astype(BF16)
        spread_high = matmul_nt(spread, w_high).astype(BF16)
        spread_low = matmul_nt(spread, w_low).astype(BF16)
        top = matmul(spread_high, pick_high[0:6]) + matmul(spread_low, pick_low[0:6])
        same = lax.bitwise_and(iota((512, 160), 0), 7) == lax.bitwise_and(iota((512, 160), 1), 7)
        top = jnp.where(same, top, 0.0)
        biases = jnp.concatenate([b_high.astype(F32), b_low.astype(F32), b_rest, jnp.zeros((5, UNITS), F32)], axis=0)
        spread_bias = matmul_nt(spread, biases.astype(BF16)).astype(BF16)
        top = top + matmul(spread_bias, ones_where(col == row + 144).astype(BF16))
        left_lhs[...] = top.astype(BF16)
        o_high, o_low = split(w_out[...])
        row, field, same = row[:, 0:96], field[:, 0:96], same[:, 0:96]
        pick_high = ones_where(((field == row) | (field == row + 4)) & (row < 3)).astype(BF16)
        pick_low = ones_where((field == row + 8) & (row < 3)).astype(BF16)
        spread_oh = matmul_nt(spread, o_high).astype(BF16)
        spread_ol = matmul_nt(spread, o_low).astype(BF16)
        bottom = matmul(spread_oh, pick_high[0:3]) + matmul(spread_ol, pick_low[0:3])
        out_lhs[...] = jnp.where(same, bottom, 0.0).astype(BF16)

        same_t = lax.bitwise_and(iota((96, 512), 0), 7) == lax.bitwise_and(iota((96, 512), 1), 7)
        row = lax.shift_right_logical(iota((96, 8), 0), 3)
        col = iota((96, 8), 1)
        get_high = ones_where((row == col) & (col < 6)).astype(BF16)
        get_low = ones_where((row == col + 6) & (col < 6)).astype(BF16)
        tall_w = matmul(get_high[:, 0:6], w_high) + matmul(get_low[:, 0:6], w_low)
        back_lhs[...] = jnp.where(same_t, matmul(tall_w.astype(BF16), spread_t), 0.0).astype(BF16)
        get_high = ones_where((row[0:64] == col[0:64]) & (col[0:64] < 3)).astype(BF16)
        get_low = ones_where((row[0:64] == col[0:64] + 4) & (col[0:64] < 3)).astype(BF16)
        tall_o = matmul(get_high[:, 0:3], o_high) + matmul(get_low[:, 0:3], o_low)
        force_lhs[...] = jnp.where(same_t[0:64], matmul(tall_o.astype(BF16), spread_t), 0.0).astype(BF16)

    def build_columns():
        loads[2].wait()
        line_columns = columns[...]
        for index in range(50):
            tall[index] = jnp.broadcast_to(line_columns[:, index:index + 1], (8, 128))

    def tall_column(index):
        half = tall[index]
        return jnp.concatenate([half, half], axis=1)

    lower = iota((8, 128), 1) < 64

    def turn(tile):
        return pltpu.roll(tile, 64, 1)

    def pack(left, right, piece):
        lanes = slice(128 * (piece // 2), 128 * (piece // 2) + 128)
        if piece % 2 == 0:
            return jnp.where(lower, left[:, lanes], turn(right[:, lanes]))
        return jnp.where(lower, turn(left[:, lanes]), right[:, lanes])

    def unpack(pieces):
        left = [jnp.where(lower, pieces[2 * t], turn(pieces[2 * t + 1])) for t in range(2)]
        right = [jnp.where(lower, turn(pieces[2 * t]), pieces[2 * t + 1]) for t in range(2)]
        return jnp.concatenate(left, axis=1), jnp.concatenate(right, axis=1)

    def two_scalars(left_index, right_index):
        return jnp.where(lower, scalar(left_index), scalar(right_index))

    def states(rows):
        return [sum(scalar(base + row) * rows[row] for row in range(ROWS)) for base in (UP_W, DOWN_W)]

    def local_rows(rows):
        return [
            sum(scalar(LOCAL + ROWS * row + col) * rows[col] for col in range(ROWS)) for row in range(ROWS)
        ]

    def pieces_send(source, target, send_sems, recv_sems, order):
        for step in (2, 1, 3):
            other = in_group(step)
            send(
                source.at[order, other], target.at[order, member],
                send_sems.at[order, other], recv_sems.at[order, member], group_device(other),
            )

    def pieces_wait(source, target, send_sems, recv_sems, order):
        for step in range(1, GROUP):
            other = in_group(step)
            remote(
                source.at[order, other], target.at[order, other],
                send_sems.at[order, other], recv_sems.at[order, other], group_device(other),
            ).wait_recv()

    def ring_send(order, load):
        gathered = []
        for comp in range(3):
            gathered.append(sum(
                two_scalars(UP_C + other, DOWN_C + other) * load(other, comp) for other in range(GROUP)
            ))
        first, second, third = gathered
        turned = turn(third)
        front = jnp.where(lower, first, turn(second))
        x2_send[order, 0, 0] = front[0:4]
        x2_send[order, 0, 1] = front[4:8]
        x2_send[order, 0, 2] = jnp.where(lower[0:4], third[0:4], turned[4:8])
        front = jnp.where(lower, turn(first), second)
        x2_send[order, 1, 0] = front[0:4]
        x2_send[order, 1, 1] = front[4:8]
        x2_send[order, 1, 2] = jnp.where(lower[0:4], turned[0:4], third[4:8])
        for step in (8, 7, 9, 6, 10, 5, 11, 4, 12, 3, 13, 2, 14, 1, 15):
            other = in_ring(step)
            kind = jnp.where(other > ring, 0, 1)
            send(
                x2_send.at[order, kind], x2_recv.at[order, ring],
                x2_ss.at[order, other], x2_rs.at[order, ring], ring_device(other),
            )

    def ring_receive(order):
        left = jnp.zeros((3, 4, 128), F32)
        right = jnp.zeros((3, 4, 128), F32)
        for step in (1, 15, 2, 14, 3, 13, 4, 12, 5, 11, 6, 10, 7, 9, 8):
            other = in_ring(step)
            remote(
                x2_send.at[order, 0], x2_recv.at[order, other],
                x2_ss.at[order, other], x2_rs.at[order, other], ring_device(other),
            ).wait_recv()
            part = x2_recv[order, other]
            left = left + scalar(RING_L + other) * part
            right = right + scalar(RING_R + other) * part
        front_left = jnp.concatenate([left[0], left[1]], axis=0)
        front_right = jnp.concatenate([right[0], right[1]], axis=0)
        back_left = jnp.concatenate([left[2], pltpu.roll(left[2], 64, 1)], axis=0)
        back_right = jnp.concatenate([pltpu.roll(right[2], 64, 1), right[2]], axis=0)
        return [
            jnp.where(lower, front_left, turn(front_right)),
            jnp.where(lower, turn(front_left), front_right),
            jnp.where(lower, back_left, back_right),
        ]

    def group_part(load, other, comp):
        total = jnp.zeros((8, 128), F32)
        for source in range(GROUP):
            index = 5 * other + 1 + source
            total = total + two_scalars(BACK_L + index, BACK_R + index) * load(source, comp)
        return total

    def ring_factor(other):
        return two_scalars(BACK_L + 5 * other, BACK_R + 5 * other)

    def projected(order, tile):
        return sum(tall[24 * order + 8 + col] * tile[col:col + 1] for col in range(8))

    def keep_rows(order, other, comp, out):
        for kind in range(4):
            plane_send[order, other, kind // 2, kind % 2, comp:comp + 1, :] = out[kind:kind + 1]

    def plane_rows_send(order, steps):
        for step in steps:
            other = in_group(step)
            for along in (4, 5, 3, 6, 2, 7, 1):
                place = in_line(along)
                side = jnp.where(place > gy, 0, 1)
                if along in (1, LINE - 1):
                    send(
                        plane_send.at[order, other, side], plane_edge.at[order, member, 0 if along == 1 else 1],
                        edge_ss.at[order], edge_rs.at[order], plane_device(other, place), drain=False,
                    )
                else:
                    send(
                        plane_send.at[order, other, side, 1], plane_recv.at[order, member, along - 2],
                        plane_ss.at[order], plane_rs.at[order], plane_device(other, place), drain=False,
                    )

    def plane_rows_all(order):
        device = plane_device(in_group(1), in_line(1))
        return (
            remote(plane_recv.at[order], plane_recv.at[order], plane_ss.at[order], plane_rs.at[order], device),
            remote(plane_edge.at[order], plane_edge.at[order], edge_ss.at[order], edge_rs.at[order], device),
        )

    def plane_rows_wait(order):
        for copy in plane_rows_all(order):
            copy.wait_recv()

    def plane_rows_drain(order):
        for copy in plane_rows_all(order):
            copy.wait_send()

    def from_plane(order, source, comp):
        def row(ref, *index):
            return ref[(order, source) + index + (slice(comp, comp + 1),)]

        factor = 24 * order + 16
        total = tall[48] * row(plane_edge, 0, 0) + tall[factor + 1] * row(plane_edge, 0, 1)
        total = total + tall[49] * row(plane_edge, 1, 0) + tall[factor + LINE - 1] * row(plane_edge, 1, 1)
        for along in range(2, LINE - 1):
            total = total + tall[factor + along] * row(plane_recv, along - 2)
        return total

    def own_block(order, tile):
        return sum(tall[24 * order + col] * tile[col:col + 1] for col in range(8))

    def line_send(load, order):
        base = 24 * order
        sent_columns = [tall_column(base + 8 + col) for col in range(8)]
        for comp in range(3):
            for row in range(ROWS):
                tile = load(comp, row)
                out = sum(sent_columns[col] * tile[col:col + 1] for col in range(8))
                for kind in range(4):
                    y_send[order, kind, comp, row:row + 1, :] = out[kind:kind + 1]
        for kind, step in ((0, 1), (1, LINE - 1)):
            send(
                y_send.at[order, 2 * kind], y_edge.at[order, kind],
                ye_ss.at[order, kind], ye_rs.at[order, kind], line_device(in_line(step)),
            )
        for step in (4, 5, 3, 2, 6, 1, 7):
            other = in_line(step)
            kind = jnp.where(other > gy, 1, 3)
            send(
                y_send.at[order, kind], y_recv.at[order, step - 1],
                y_ss.at[order, step - 1], y_rs.at[order, step - 1], line_device(other),
            )

    def line_local(load, order, store):
        base = 24 * order
        local_columns = [tall_column(base + col) for col in range(8)]
        for comp in range(3):
            for row in range(ROWS):
                tile = load(comp, row)
                store(comp, row, sum(local_columns[col] * tile[col:col + 1] for col in range(8)))

    def line_receive(order, load, store):
        base = 24 * order
        for kind, step in ((0, LINE - 1), (1, 1)):
            remote(
                y_send.at[order, 0], y_edge.at[order, kind],
                ye_ss.at[order, kind], ye_rs.at[order, kind], line_device(in_line(step)),
            ).wait_recv()
        for step in range(1, LINE):
            remote(
                y_send.at[order, 1], y_recv.at[order, step - 1],
                y_ss.at[order, step - 1], y_rs.at[order, step - 1], line_device(in_line(step)),
            ).wait_recv()
        factors = [tall_column(base + 16 + step) for step in range(1, LINE)]
        first = tall_column(48)
        last = tall_column(49)
        for comp in range(3):
            for row in range(ROWS):
                total = load(comp, row)
                total = total + first * y_edge[order, 0, comp, row:row + 1, :]
                total = total + last * y_edge[order, 1, comp, row:row + 1, :]
                for step in range(1, LINE):
                    total = total + factors[step - 1] * y_recv[order, step - 1, comp, row:row + 1, :]
                store(comp, row, total)

    def depth_apply(values, order):
        high, low = split(values)
        both = matmul(jnp.concatenate([high, low], axis=0), ztab[2 * order])
        count = values.shape[0]
        return both[0:count] + both[count:2 * count] + matmul(high, ztab[2 * order + 1])

    def pass_tokens():
        pl.semaphore_wait(barrier, len(partners))
        for kind, step in ((0, half), (1, RING - half)):
            pl.semaphore_signal(
                token.at[kind], inc=1, device_id=ring_device(in_ring(step)), device_id_type=MESH
            )

        for step in range(1, GROUP):
            pl.semaphore_signal(
                token.at[1 + step], inc=1, device_id=group_device(in_group(step)), device_id_type=MESH
            )

    def wait_tokens(first, last):
        for kind in range(first, last):
            pl.semaphore_wait(token.at[kind], 1)

    loads[0].wait()
    loads[1].wait()
    for comp in range(3):
        left, right = states([vel[comp, row] for row in range(ROWS)])
        for piece in range(GROUP):
            x1_send[0, piece, comp] = pack(left, right, piece)
    pass_tokens()
    pieces_send(x1_send, x1_recv, x1_ss, x1_rs, 0)
    build_columns()
    line_send(lambda comp, row: vel[comp, row], 0)
    x1_recv[0, member] = x1_send[0, member]
    build_weights()
    for load in loads[6:]:
        load.wait()

    def keep_along(comp, row, value):
        along_y[comp, row] = value

    line_local(lambda comp, row: vel[comp, row], 0, keep_along)
    pieces_wait(x1_send, x1_recv, x1_ss, x1_rs, 0)
    wait_tokens(0, 2)

    def first_piece(source, comp):
        return x1_recv[0, source, comp]

    ring_send(0, first_piece)
    line_receive(0, lambda comp, row: along_y[comp, row], keep_along)
    for comp in range(3):
        for row, value in enumerate(local_rows([vel[comp, row] for row in range(ROWS)])):
            smoothed[comp, row] = value
        for row, value in enumerate(local_rows([along_y[comp, row] for row in range(ROWS)])):
            feats[row, 8 * comp:8 * comp + 8, :] = value
    def outward(row):
        parts = [STEP_SIZE * cot[comp, row] for comp in range(3)]
        return jnp.concatenate(parts + [jnp.zeros((8, 256), F32)], axis=0)

    def grad_of_hidden(row, carry):
        out_high, out_low = split(outward(row))
        pulled_out[row] = matmul(out_lhs[...], jnp.concatenate([out_high, out_low, out_high], axis=0))
        rhs[row, 144:160, :] = jnp.ones((16, 256), BF16)
        return carry

    lax.fori_loop(0, ROWS, grad_of_hidden, 0)
    wait_tokens(2, 1 + GROUP)
    for other in range(GROUP):
        for comp in range(3):
            tile = group_part(first_piece, other, comp)
            x3_send[0, other, comp] = tile
            group_rows[other, comp] = projected(0, tile)
    ring_state = ring_receive(0)
    ring_rows = [projected(0, ring_state[comp]) for comp in range(3)]
    for step in range(GROUP):
        other = in_group(step)
        factor = ring_factor(other)
        for comp in range(3):
            x3_send[0, other, comp] += factor * ring_state[comp]
            keep_rows(0, other, comp, group_rows[other, comp] + factor * ring_rows[comp])
    plane_rows_send(0, (2,))
    pieces_send(x3_send, x3_recv, x3_ss, x3_rs, 0)
    plane_rows_send(0, (1, 3, 0))
    x3_recv[0, member] = x3_send[0, member]
    pieces_wait(x3_send, x3_recv, x3_ss, x3_rs, 0)
    for comp in range(3):
        left, right = unpack([x3_recv[0, piece, comp] for piece in range(GROUP)])
        for row in range(ROWS):
            smoothed[comp, row] += scalar(LEFT + row) * left + scalar(RIGHT + row) * right
    along_z = depth_apply(smoothed[...].reshape(96, 256), 0)
    for comp in range(3):
        for row in range(ROWS):
            start = (comp * ROWS + row) * 8
            feats[row, 24 + 8 * comp:32 + 8 * comp, :] = along_z[start:start + 8]
    for piece in range(GROUP):
        for comp in range(3):
            state[piece, comp] = own_block(0, x3_recv[0, piece, comp])
    plane_rows_wait(0)
    for comp in range(3):
        left, right = unpack([state[piece, comp] + from_plane(0, piece, comp) for piece in range(GROUP)])
        for row in range(ROWS):
            feats[row, 8 * comp:8 * comp + 8, :] += scalar(LEFT + row) * left + scalar(RIGHT + row) * right

    def closure(row):
        feature_high, feature_low = split(feats[row])
        rhs[row, 0:48, :] = feature_high
        rhs[row, 48:96, :] = feature_low
        rhs[row, 96:144, :] = feature_high
        hidden = jnp.tanh(matmul(left_lhs[...], rhs[row]))
        grad_pre = pulled_out[row] * (1.0 - hidden * hidden)
        pre_high, pre_low = split(grad_pre)
        hidden_buf[row] = hidden
        pre_buf[row, 0] = pre_high
        pre_buf[row, 1] = pre_low
        both = matmul(back_lhs[...], pre_high)
        gfeats[row] = both[0:48] + both[48:96] + matmul(back_lhs[0:48, :], pre_low)

    for row in range(ROWS):
        closure(row)

    def grad_along_y(comp, row):
        return gfeats[row, 8 * comp:8 * comp + 8, :]

    packed = {}
    for comp in range(3):
        left, right = states([grad_along_y(comp, row) for row in range(ROWS)])
        for piece in range(GROUP):
            packed[piece, comp] = pack(left, right, piece)
            keep_rows(1, piece, comp, projected(1, packed[piece, comp]))
    plane_rows_send(1, (2, 1, 3))
    back_in = jnp.concatenate(
        [gfeats[row, 24 + 8 * comp:32 + 8 * comp, :] for comp in range(3) for row in range(ROWS)], axis=0
    )
    along_z = depth_apply(back_in, 1)
    for comp in range(3):
        starts = [(comp * ROWS + row) * 8 for row in range(ROWS)]
        left, right = states([along_z[start:start + 8] for start in starts])
        for piece in range(GROUP):
            x1_send[1, piece, comp] = own_block(1, packed[piece, comp]) + pack(left, right, piece)
        for row in range(ROWS):
            pulled[comp, row] = along_z[starts[row]:starts[row] + 8]
    pieces_send(x1_send, x1_recv, x1_ss, x1_rs, 1)
    plane_rows_send(1, (0,))
    x1_recv[1, member] = x1_send[1, member]

    def keep_pulled(comp, row, value):
        pulled[comp, row] = value

    def line_part():
        line_send(grad_along_y, 1)
        line_local(grad_along_y, 1, lambda comp, row, value: keep_pulled(comp, row, pulled[comp, row] + value))

    def forces(row, carry):
        hidden_high, hidden_low = split(hidden_buf[row])
        both = matmul(force_lhs[...], hidden_high)
        forcing = both[0:32] + both[32:64] + matmul(force_lhs[0:32, :], hidden_low)
        for comp in range(3):
            new_velocity[comp, row] = vel[comp, row] + STEP_SIZE * forcing[8 * comp:8 * comp + 8]
        return carry

    def row_sums(row, carry):
        hidden_high, hidden_low = split(hidden_buf[row])
        feature_high, feature_low = split(feats[row])
        ones = jnp.ones((16, 256), BF16)
        both = matmul_nt(jnp.concatenate([feature_high, ones, feature_low], axis=0), pre_buf[row, 0])
        rest = matmul_nt(jnp.concatenate([feature_high, ones], axis=0), pre_buf[row, 1])
        sums[0:48, :] += both[0:48] + both[64:112] + rest[0:48]
        sums[48:56, :] += both[48:56] + rest[48:56]
        out_high, out_low = split(outward(row))
        both = matmul_nt(jnp.concatenate([out_high, out_low], axis=0), hidden_high)
        rest = matmul_nt(out_high, hidden_low)
        sums[56:88, :] += both[0:32] + both[32:64] + rest
        return carry

    def partial_sums():
        sums[...] = jnp.zeros((88, 512), F32)
        lax.fori_loop(0, ROWS, row_sums, 0)
        same = lax.bitwise_and(iota((88, 512), 0), 7) == lax.bitwise_and(iota((88, 512), 1), 7)
        gather = ones_where(lax.shift_right_logical(iota((512, UNITS), 0), 3) == iota((512, UNITS), 1)).astype(BF16)
        high, low = split(jnp.where(same, sums[...], 0.0))
        narrow = matmul(high, gather) + matmul(low, gather)
        folded = [jnp.sum(narrow[8 * part:8 * part + 8], axis=0, keepdims=True) for part in range(11)]
        front = jnp.concatenate(folded[0:8], axis=0)
        back = jnp.concatenate(folded[8:11] + [jnp.zeros((5, UNITS), F32)], axis=0)
        p1[gy] = jnp.concatenate([front, back], axis=1)
        for step in range(1, LINE):
            other = in_line(step)
            send(p1.at[gy], p1.at[gy], p1_ss.at[other], p1_rs.at[gy], line_device(other))

    def sum_line():
        for step in range(1, LINE):
            other = in_line(step)
            remote(p1.at[other], p1.at[other], p1_ss.at[other], p1_rs.at[other], line_device(other)).wait_recv()
        total = p1[0]
        for other in range(1, LINE):
            total = total + p1[other]
        p2[member] = total
        for step in range(1, GROUP):
            other = in_group(step)
            send(p2.at[member], p2.at[member], p2_ss.at[other], p2_rs.at[member], group_device(other))

    def sum_group():
        for step in range(1, GROUP):
            other = in_group(step)
            remote(p2.at[other], p2.at[other], p2_ss.at[other], p2_rs.at[other], group_device(other)).wait_recv()
        total = p2[0]
        for other in range(1, GROUP):
            total = total + p2[other]
        p3[ring] = total
        for step in (8, 7, 9, 6, 10, 5, 11, 4, 12, 3, 13, 2, 14, 1, 15):
            other = in_ring(step)
            send(p3.at[ring], p3.at[ring], p3_ss.at[other], p3_rs.at[ring], ring_device(other))

    def sum_ring():
        for step in range(1, RING):
            other = in_ring(step)
            remote(p3.at[other], p3.at[other], p3_ss.at[other], p3_rs.at[other], ring_device(other)).wait_recv()
        total = p3[0]
        for other in range(1, RING):
            total = total + p3[other]
        grad_weights[...] = total * (1.0 / float(256 * 64 * 256))

    partial_sums()
    line_part()
    pieces_wait(x1_send, x1_recv, x1_ss, x1_rs, 1)
    plane_rows_wait(1)
    for source in range(GROUP):
        for comp in range(3):
            state[source, comp] = x1_recv[1, source, comp] + from_plane(1, source, comp)

    def second_piece(source, comp):
        return state[source, comp]

    early = len(sent)
    ring_send(1, second_piece)
    sum_line()
    lax.fori_loop(0, ROWS, forces, 0)
    line_receive(1, lambda comp, row: pulled[comp, row], keep_pulled)
    for comp in range(3):
        for row, value in enumerate(local_rows([pulled[comp, row] for row in range(ROWS)])):
            grad_velocity[comp, row] = cot[comp, row] + value
    sum_group()
    for other in range(GROUP):
        for comp in range(3):
            x3_send[1, other, comp] = group_part(second_piece, other, comp)
    drain(early)
    plane_rows_drain(0)
    plane_rows_drain(1)
    ring_state = ring_receive(1)
    for step in range(GROUP):
        other = in_group(step)
        factor = ring_factor(other)
        for comp in range(3):
            x3_send[1, other, comp] += factor * ring_state[comp]
    pieces_send(x3_send, x3_recv, x3_ss, x3_rs, 1)
    x3_recv[1, member] = x3_send[1, member]
    drain(RING - 1 + GROUP - 1)
    pieces_wait(x3_send, x3_recv, x3_ss, x3_rs, 1)
    for comp in range(3):
        left, right = unpack([x3_recv[1, piece, comp] for piece in range(GROUP)])
        for row in range(ROWS):
            grad_velocity[comp, row] += scalar(LEFT + row) * left + scalar(RIGHT + row) * right
    sum_ring()
    drain(len(sent))


def finish(
    new_velocity_in, grad_velocity_in, grads, new_velocity, grad_velocity, grad_in, grad_bias, grad_out_t,
    small_in, small_bias, small_out, sems,
):
    copies = [
        pltpu.make_async_copy(source.at[comp], target.at[comp], sems.at[2 * comp + place])
        for comp in range(3)
        for place, (source, target) in enumerate(((new_velocity_in, new_velocity), (grad_velocity_in, grad_velocity)))
    ]
    for copy in copies:
        copy.start()
    front = grads[:, 0:UNITS]
    small_in[...] = front[0:6]
    small_bias[...] = front[6:7]
    small_out[0:1] = front[7:8]
    small_out[1:3] = grads[0:2, UNITS:2 * UNITS]
    small = ((small_in, grad_in), (small_bias, grad_bias), (small_out, grad_out_t))
    for place, (source, target) in enumerate(small):
        copies.append(pltpu.make_async_copy(source, target, sems.at[6 + place]))
        copies[-1].start()
    for copy in copies:
        copy.wait()


def local(velocity, cotangent, weight_in, bias_in, weight_out):
    field = velocity.shape
    dma = pltpu.SemaphoreType.DMA
    anywhere = pl.BlockSpec(memory_space=pl.ANY)
    whole = pl.BlockSpec(memory_space=pltpu.VMEM)
    mid = pl.pallas_call(
        kernel,
        out_shape=(
            pltpu.VMEM(field, F32),
            pltpu.VMEM(field, F32),
            pltpu.VMEM((8, 128), F32),
        ),
        in_specs=[anywhere] * 8,
        out_specs=(whole, whole, whole),
        scratch_shapes=[
            pltpu.VMEM((6, UNITS), F32),
            pltpu.VMEM((1, UNITS), F32),
            pltpu.VMEM((3, UNITS), F32),
            pltpu.VMEM(field, F32),
            pltpu.VMEM(field, F32),
            pltpu.VMEM(field, F32),
            pltpu.VMEM(field, F32),
            pltpu.VMEM((ROWS, 48, 256), F32),
            pltpu.VMEM((ROWS, 48, 256), F32),
            pltpu.VMEM(field, F32),
            pltpu.SMEM((1, 128), F32),
            pltpu.VMEM((8, 128), F32),
            pltpu.VMEM((50, 8, 128), F32),
            pltpu.VMEM((4, 256, 256), BF16),
            pltpu.VMEM((512, 160), BF16),
            pltpu.VMEM((512, 96), BF16),
            pltpu.VMEM((96, 512), BF16),
            pltpu.VMEM((64, 512), BF16),
            pltpu.VMEM((ROWS, 160, 256), BF16),
            pltpu.VMEM((ROWS, 512, 256), F32),
            pltpu.VMEM((ROWS, 512, 256), F32),
            pltpu.VMEM((ROWS, 2, 512, 256), BF16),
            pltpu.VMEM((88, 512), F32),
            pltpu.VMEM((2, GROUP, 3, 8, 128), F32),
            pltpu.VMEM((2, GROUP, 3, 8, 128), F32),
            pltpu.VMEM((GROUP, 3, 8, 128), F32),
            pltpu.VMEM((GROUP, 3, 8, 128), F32),
            pltpu.VMEM((2, 2, 3, 4, 128), F32),
            pltpu.VMEM((2, RING, 3, 4, 128), F32),
            pltpu.VMEM((2, GROUP, 3, 8, 128), F32),
            pltpu.VMEM((2, GROUP, 3, 8, 128), F32),
            pltpu.VMEM((2, GROUP, 2, 2, 3, 128), F32),
            pltpu.VMEM((2, GROUP, LINE - 3, 3, 128), F32),
            pltpu.VMEM((2, GROUP, 2, 2, 3, 128), F32),
            pltpu.VMEM((2, 4, 3, ROWS, 256), F32),
            pltpu.VMEM((2, LINE - 1, 3, ROWS, 256), F32),
            pltpu.VMEM((2, 2, 3, ROWS, 256), F32),
            pltpu.VMEM((LINE, 8, 128), F32),
            pltpu.VMEM((GROUP, 8, 128), F32),
            pltpu.VMEM((RING, 8, 128), F32),
            pltpu.SemaphoreType.REGULAR((1 + GROUP,)),
            dma((8,)),
            dma((2, GROUP)), dma((2, GROUP)),
            dma((2, RING)), dma((2, RING)),
            dma((2, GROUP)), dma((2, GROUP)),
            dma((2,)), dma((2,)), dma((2,)), dma((2,)),
            dma((2, LINE - 1)), dma((2, LINE - 1)),
            dma((2, 2)), dma((2, 2)),
            dma((LINE,)), dma((LINE,)),
            dma((GROUP,)), dma((GROUP,)),
            dma((RING,)), dma((RING,)),
        ],
        compiler_params=pltpu.CompilerParams(collective_id=0, has_side_effects=True, vmem_limit_bytes=RESERVED),
        name="closure_step",
    )(
        velocity, cotangent, weight_in, bias_in.reshape(1, UNITS), weight_out.T,
        jnp.asarray(smoothing_table()).reshape(GROUP * RING, 1, 128), jnp.asarray(line_table()),
        jnp.asarray(depth_table(field[3])),
    )
    outs = pl.pallas_call(
        finish,
        out_shape=(
            jax.ShapeDtypeStruct(field, F32),
            jax.ShapeDtypeStruct(field, F32),
            jax.ShapeDtypeStruct((6, UNITS), F32),
            jax.ShapeDtypeStruct((1, UNITS), F32),
            jax.ShapeDtypeStruct((3, UNITS), F32),
        ),
        in_specs=[whole] * 3,
        out_specs=(anywhere,) * 5,
        scratch_shapes=[
            pltpu.VMEM((6, UNITS), F32),
            pltpu.VMEM((1, UNITS), F32),
            pltpu.VMEM((3, UNITS), F32),
            dma((9,)),
        ],
        compiler_params=pltpu.CompilerParams(vmem_limit_bytes=1 << 20),
        name="finish",
    )(*mid)
    return outs[0], outs[1], outs[2], outs[3].reshape(UNITS), outs[4].T


def solution(mesh):
    in_specs = (P(None, "gx", "gy", None), P(None, "gx", "gy", None), P(), P(), P())
    out_specs = (P(None, "gx", "gy", None), P(None, "gx", "gy", None), P(), P(), P())
    return jax.shard_map(local, mesh=mesh, in_specs=in_specs, out_specs=out_specs, check_vma=False)
```
